32 devices in a mesh: dp: 4 (over y, core), row: 2 (over x), col: 4 (over z).
Axes of the slice: x: 2, y: 2, z: 4, core: 2. Of those that a mesh axis runs over, the one named last changes fastest.
Arguments:
- tokens: float32 [16384, 1024], P(('dp', 'row', 'col')), may hold values from -6 to 6
- segment_ids: int32 [16384], P(('dp', 'row', 'col')), may hold values from 0 to 127, never falling along the last dimension, each value on 1 to 512 neighbouring positions
- cotangent: float32 [16384, 1024], P(('dp', 'row', 'col')), may hold values from -6 to 6
- weight_query: float32 [1024, 1024], P('row', 'col'), as said below
- weight_key: float32 [1024, 1024], P('row', 'col'), may hold values from -0.1875 to 0.1875
- weight_value: float32 [1024, 1024], P('row', 'col'), may hold values from -0.1875 to 0.1875
- weight_output: float32 [1024, 1024], P('row', 'col'), may hold values from -0.75 to 0.75
- weight_inner: float32 [1024, 4096], P('row', 'col'), may hold values from -0.1875 to 0.1875
- weight_outer: float32 [4096, 1024], P('row', 'col'), may hold values from -0.09375 to 0.09375
- bias_query: float32 [1024], P(('row', 'col')), may hold values from -1.5 to 1.5
- bias_value: float32 [1024], P(('row', 'col')), may hold values from -1.5 to 1.5
- bias_output: float32 [1024], P(('row', 'col')), may hold values from -1.5 to 1.5
- bias_inner: float32 [4096], P(('row', 'col')), may hold values from -1.5 to 1.5
- bias_outer: float32 [1024], P(('row', 'col')), may hold values from -1.5 to 1.5
- gain_attn: float32 [1024], P(('row', 'col')), may hold values from 0.25 to 1.75
- shift_attn: float32 [1024], P(('row', 'col')), may hold values from -1.5 to 1.5
- gain_block: float32 [1024], P(('row', 'col')), may hold values from 0.25 to 1.75
- shift_block: float32 [1024], P(('row', 'col')), may hold values from -1.5 to 1.5
- tau_num: int32 [1], replicated, may hold values from 100 to 399
- tau_den: int32 [1], replicated, may hold values from 400 to 999
Outputs:
- output: float32 [16384, 1024], P(('dp', 'row', 'col'))
- grad_tokens: float32 [16384, 1024], P(('dp', 'row', 'col'))
- grad_weight_query: float32 [1024, 1024], P('row', 'col')
- grad_weight_key: float32 [1024, 1024], P('row', 'col')
- grad_weight_value: float32 [1024, 1024], P('row', 'col')
- grad_weight_output: float32 [1024, 1024], P('row', 'col')
- grad_weight_inner: float32 [1024, 4096], P('row', 'col')
- grad_weight_outer: float32 [4096, 1024], P('row', 'col')
- grad_bias_query: float32 [1024], P(('row', 'col'))
- grad_bias_value: float32 [1024], P(('row', 'col'))
- grad_bias_output: float32 [1024], P(('row', 'col'))
- grad_bias_inner: float32 [4096], P(('row', 'col'))
- grad_bias_outer: float32 [1024], P(('row', 'col'))
- grad_gain_attn: float32 [1024], P(('row', 'col'))
- grad_shift_attn: float32 [1024], P(('row', 'col'))
- grad_gain_block: float32 [1024], P(('row', 'col'))
- grad_shift_block: float32 [1024], P(('row', 'col'))
- head_peak: float32 [16], replicated
- clipped_query: float32 [1024, 1024], P('row', 'col')
- clipped_key: float32 [1024, 1024], P('row', 'col')
The draws below stay inside these ranges and needn't reach their ends.
Inputs may be any that keep to these rules, and one draw needn't show every extreme that they name: `segment_ids`: along the tokens the numbers never fall; each document covers 1 to 512 consecutive tokens, one exactly 512. `weight_query`: entries within 18 / sqrt(1024) in magnitude.
All inputs are finite; a program needn't handle non-finite values.
Results may differ from the reference program's by a relative error of at most 0.019.
The reference program's roundings to bfloat16 on the way count: a program that leaves them out, or rounds other values in their place, can miss the bound.
Values may be sent and summed in bfloat16 or wider, within the bound.
A program may use at most 256 MiB of HBM per device.

```python
import math
import jax
import jax.numpy as jnp
import numpy as np
from jax import lax

D = 1024
H = 16
DH = 64
FF = 4096
SEQ = 512
TOKENS = 16384
DOCS = 128


def draw_weight_query(key, part):
    base = jnp.clip(jax.random.normal(jax.random.fold_in(key, 17), (D, D), jnp.float32), -6.0, 6.0)
    head_scale = jnp.exp(jax.random.uniform(jax.random.fold_in(key, 29), (H,), jnp.float32, 0.0, math.log(3.0)))
    return base * jnp.repeat(head_scale, DH)[None, :] * D ** (-0.5)


def block_levels(rng, dims, split, least, high):
    def one(position, shards_of):
        heights = jax.random.uniform(jax.random.fold_in(jax.random.fold_in(rng, 6), position), (shards_of,), jnp.float32, least / len(split), high / len(split))
        return jnp.repeat(jnp.exp(heights), dims[position] // shards_of).reshape((-1,) + (1,) * (len(dims) - position - 1))

    gain = one(*split[0])
    for cut in split[1:]:
        gain = gain * one(*cut)
    return gain


def profile(count, total, reach, lean):
    loads = [(1 << 20) // math.isqrt(standing ** lean) + 1 for standing in range(2, count + 1)]
    surplus, given = total - reach - (count - 1), [1] * (count - 1)
    while surplus > 0:
        free = [i for i in range(count - 1) if given[i] < reach]
        whole, left = sum([loads[i] for i in free]), surplus
        for i in free:
            extra = min(reach - given[i], max(1, left * loads[i] // whole), surplus)
            given[i] = given[i] + extra
            surplus = surplus - extra
    return np.array([reach] + given)


def uneven_parts(stream_key, number_of, total, limit, slope):
    if number_of == 2:
        one = jax.random.randint(stream_key, (), max(1, total - limit), min(limit, total - 1) + 1)
        return jnp.stack([one, total - one])
    tallies = jnp.asarray(profile(number_of, total, limit, slope), jnp.int32)
    couples = (number_of - 1) // 2
    giver, sink = tallies[1:1 + 2 * couples:2], tallies[2:2 + 2 * couples:2]
    slack = jnp.minimum(giver - 1, limit - sink)
    shifted = jax.random.randint(jax.random.fold_in(stream_key, 1), (couples,), 0, 1 << 20) % (slack + 1)
    tallies = tallies.at[1:1 + 2 * couples:2].set(giver - shifted).at[2:2 + 2 * couples:2].set(sink + shifted)
    return tallies[jax.random.permutation(jax.random.fold_in(stream_key, 2), number_of)]


def normal_values(own_key, dims, scale, reach, pieces=(), held_as=jnp.bfloat16):
    entries = scale * jax.random.normal(own_key, dims, jnp.float32)
    if pieces:
        entries = entries * block_levels(own_key, dims, pieces, -0.22, 0.18)
    return jnp.clip(entries, -reach, reach).astype(held_as)


def setup_inputs(seed: int = 0) -> dict:
    key_list = jax.random.split(jax.random.key(seed), 21)
    return {
        "tokens": normal_values(key_list[0], (TOKENS, D), 1.0, 6.0, ((0, 32),), jnp.float32),
        "segment_ids": jnp.searchsorted(jnp.cumsum(uneven_parts(key_list[1], DOCS, TOKENS, SEQ, 2)), jnp.arange(TOKENS), side="right").astype(jnp.int32),
        "cotangent": normal_values(key_list[2], (TOKENS, D), 1.0, 6.0, ((0, 32),), jnp.float32),
        "weight_query": draw_weight_query(jax.random.fold_in(key_list[20], 71), 0),
        "weight_key": normal_values(key_list[4], (D, D), D ** -0.5, 0.1875, ((0, 2), (1, 4)), jnp.float32),
        "weight_value": normal_values(key_list[5], (D, D), D ** -0.5, 0.1875, ((0, 2), (1, 4)), jnp.float32),
        "weight_output": normal_values(key_list[6], (D, D), (D // 16) ** -0.5, 0.75, ((0, 2), (1, 4)), jnp.float32),
        "weight_inner": normal_values(key_list[7], (D, FF), D ** -0.5, 0.1875, ((0, 2), (1, 4)), jnp.float32),
        "weight_outer": normal_values(key_list[8], (FF, D), FF ** -0.5, 0.09375, ((0, 2), (1, 4)), jnp.float32),
        "bias_query": normal_values(key_list[9], (D,), 0.3, 1.5, ((0, 8),), jnp.float32),
        "bias_value": normal_values(key_list[10], (D,), 0.3, 1.5, ((0, 8),), jnp.float32),
        "bias_output": normal_values(key_list[11], (D,), 0.3, 1.5, ((0, 8),), jnp.float32),
        "bias_inner": normal_values(key_list[12], (FF,), 0.3, 1.5, ((0, 8),), jnp.float32),
        "bias_outer": normal_values(key_list[13], (D,), 0.3, 1.5, ((0, 8),), jnp.float32),
        "gain_attn": jnp.clip(1.0 + 0.15 * jax.random.normal(key_list[14], (D,), jnp.float32), 0.25, 1.75),
        "shift_attn": normal_values(key_list[15], (D,), 0.3, 1.5, ((0, 8),), jnp.float32),
        "gain_block": jnp.clip(1.0 + 0.15 * jax.random.normal(key_list[16], (D,), jnp.float32), 0.25, 1.75),
        "shift_block": normal_values(key_list[17], (D,), 0.3, 1.5, ((0, 8),), jnp.float32),
        "tau_num": jax.random.randint(key_list[18], (1,), 100, 400).astype(jnp.int32),
        "tau_den": jax.random.randint(key_list[19], (1,), 400, 1000).astype(jnp.int32),
    }


@jax.custom_vjp
def low(v):
    return lax.optimization_barrier(v.astype(jnp.bfloat16)).astype(jnp.float32)

@jax.custom_vjp
def low_back(v):
    return v

def low_keep(v):
    return (low(v), None)

def low_pass(kept, grad):
    return (grad,)

def back_keep(v):
    return (v, None)

def back_low(kept, grad):
    return (low(grad),)
low.defvjp(low_keep, low_pass)
low_back.defvjp(back_keep, back_low)
norm_eps = 1e-12
neg_fill = -1e+30
highest = lax.Precision.HIGHEST

def norm_rows(values, gain_vec, shift_vec):
    center = values - lax.optimization_barrier(jnp.mean(values, axis=-1, keepdims=True))
    spread = lax.optimization_barrier(jnp.mean(center * center, axis=-1, keepdims=True))
    return center * lax.rsqrt(spread + norm_eps) * gain_vec + shift_vec

def both_round(values):
    return low(low_back(values))

def project(operand, weight):
    return jnp.dot(operand, weight, precision=highest)

def layer_blocks(tokens, segment_ids, params):
    weight_query, weight_key, weight_value, weight_output, weight_inner, weight_outer, bias_query, bias_value, bias_output, bias_inner, bias_outer, gain_attn, shift_attn, gain_block, shift_block = tuple((low(parameter) for parameter in params))
    seq_group = 8
    block_rows = seq_group * SEQ
    blocks = TOKENS // block_rows
    token_blocks = tokens.reshape(blocks, block_rows, D)
    segment_blocks = segment_ids.reshape(blocks, seq_group, SEQ)
    head_shape = (seq_group, SEQ, H, DH)

    def one_block(best_peak, inputs):
        token_rows, segment_rows = inputs
        token_low = low(token_rows)
        query_rows = both_round(project(token_low, weight_query) + bias_query)
        key_rows = both_round(project(token_low, weight_key))
        value_rows = both_round(project(token_low, weight_value) + bias_value)
        scores = jnp.einsum('sqhd,skhd->shqk', query_rows.reshape(head_shape), key_rows.reshape(head_shape), precision=highest) * DH ** (-0.5)
        scores = low_back(scores)
        allowed = (segment_rows[:, :, None] == segment_rows[:, None, :])[:, None, :, :]
        masked = jnp.where(allowed, scores, neg_fill)
        head_top = lax.optimization_barrier(jnp.max(masked, axis=(0, 2, 3)))
        row_top = lax.optimization_barrier(jnp.max(masked, axis=-1, keepdims=True))
        raised = jnp.exp(masked - row_top)
        attend = low(raised / lax.optimization_barrier(jnp.sum(raised, axis=-1, keepdims=True)))
        context = jnp.einsum('shqk,skhd->sqhd', attend, value_rows.reshape(head_shape), precision=highest)
        context = both_round(context.reshape(block_rows, D))
        branch = low_back(project(context, weight_output) + bias_output)
        normed = norm_rows(token_rows + branch, gain_attn, shift_attn)
        normed_low = low(normed)
        hidden_pre = low_back(project(normed_low, weight_inner) + bias_inner)
        activated = low(jax.nn.gelu(hidden_pre, approximate=False))
        mlp_out = low_back(project(activated, weight_outer) + bias_outer)
        result = norm_rows(normed + mlp_out, gain_block, shift_block)
        return (jnp.maximum(best_peak, head_top), result)
    start_peak = jnp.full((H,), neg_fill, dtype=jnp.float32)
    best_peak, results = lax.scan(jax.checkpoint(one_block), start_peak, (token_blocks, segment_blocks))
    return (results.reshape(TOKENS, D), best_peak)

def reference(tokens, segment_ids, cotangent, weight_query, weight_key, weight_value, weight_output, weight_inner, weight_outer, bias_query, bias_value, bias_output, bias_inner, bias_outer, gain_attn, shift_attn, gain_block, shift_block, tau_num, tau_den):

    def forward(token_rows, *params):
        return layer_blocks(token_rows, segment_ids, params)
    output, pullback, head_peak = jax.vjp(forward, tokens, weight_query, weight_key, weight_value, weight_output, weight_inner, weight_outer, bias_query, bias_value, bias_output, bias_inner, bias_outer, gain_attn, shift_attn, gain_block, shift_block, has_aux=True)
    grads = pullback(cotangent)
    tau_value = tau_num[0].astype(jnp.float32) / tau_den[0].astype(jnp.float32)
    factor = jnp.sqrt(tau_value / jnp.maximum(head_peak, tau_value))
    column_factor = jnp.repeat(factor, DH)
    clipped_query = weight_query * column_factor[None, :]
    clipped_key = weight_key * column_factor[None, :]
    return (output, grads[0], grads[1], grads[2], grads[3], grads[4], grads[5], grads[6], grads[7], grads[8], grads[9], grads[10], grads[11], grads[12], grads[13], grads[14], grads[15], head_peak, clipped_query, clipped_key)
```

```python
import functools
import jax
import jax.numpy as jnp
from jax import lax
from jax.experimental import pallas as pl
from jax.experimental.pallas import tpu as pltpu
from jax.sharding import PartitionSpec as P

MESH = pl.DeviceIdType.MESH

LAGS = (0, 2, 5, 60)
SEQ, H, DH = 512, 16, 64

def place():
    dp = lax.axis_index("dp")
    return lax.axis_index("row"), lax.axis_index("col"), dp, dp % 2, (dp // 2) % 2


def core_peer(dp):
    return {"dp": dp + 1 - 2 * (dp % 2)}


def y_peer(dp):
    side = (dp // 2) % 2
    return {"dp": dp + 2 - 4 * side}


class Sends:
    def __init__(self):
        self.items = []

    def start(self, when, src, dst, send_sem, recv_sem, device):
        copy = pltpu.make_async_remote_copy(
            src_ref=src, dst_ref=dst, send_sem=send_sem, recv_sem=recv_sem,
            device_id=device, device_id_type=MESH,
        )
        self.items.append((when, copy))
        if when is None:
            copy.start()
        else:
            pl.when(when)(copy.start)

    def finish(self):
        for when, copy in self.items:
            if when is None:
                copy.wait_send()
            else:
                pl.when(when)(copy.wait_send)


def wait_arrival(dst, recv_sem, device):
    pltpu.make_async_remote_copy(
        src_ref=dst, dst_ref=dst, send_sem=recv_sem, recv_sem=recv_sem,
        device_id=device, device_id_type=MESH,
    ).wait_recv()


def group_barrier(rows, cols):
    row, col, dp, _, _ = place()
    barrier = pltpu.get_barrier_semaphore()
    peers = [core_peer(dp), y_peer(dp)]
    mine = row * cols + col
    for step in range(1, rows * cols):
        other = (mine + step) % (rows * cols)
        peers.append({"row": other // cols, "col": other % cols})
    for peer in peers:
        pl.semaphore_signal(barrier, inc=1, device_id=peer, device_id_type=MESH)
    pl.semaphore_wait(barrier, len(peers))


def entries_of(heights):
    found = []
    for m, height in enumerate(heights):
        found.append((m, True, 0, height * 3 // 16))
        found.append((m, False, height * 3 // 4, height // 8))
    return found


def gather_kernel(rows, cols, entries, ahead, *refs):
    count = 1 + max(entry[0] for entry in entries)
    number = len(entries)
    blocks, vec = refs[:count], refs[count]
    wholes, vecs = refs[count + 1 : 2 * count + 1], refs[2 * count + 1]
    (z_in, x_in, y_in, c_in, v_in, z_out, x_out, y_out, c_out, v_out, own_sem, own_vec) = refs[2 * count + 2 :]
    row, col, dp, core, side = place()
    group_barrier(rows, cols)
    sends = Sends()
    other = 1 - row
    x_dev, y_dev, c_dev = {"row": other}, y_peer(dp), core_peer(dp)
    mine = row * cols + col

    for step in range(1, rows * cols):
        peer = (mine + step) % (rows * cols)
        sends.start(None, vec, vecs.at[mine], v_out.at[step], v_in.at[mine],
                    {"row": peer // cols, "col": peer % cols})

    def offset(e, of_core, of_side):
        _, paired, base, part = entries[e]
        return base + ((of_core * 2 + of_side) * part if paired else of_core * part)

    def region(e, of_row, of_col, of_core, of_side):
        m, _, _, part = entries[e]
        height, width = blocks[m].shape
        start = of_row * height + offset(e, of_core, of_side)
        return wholes[m].at[pl.ds(pl.multiple_of(start, 16), part),
                            pl.ds(pl.multiple_of(of_col * width, width), width)]

    def own_part(e):
        m, _, _, part = entries[e]
        return blocks[m].at[pl.ds(pl.multiple_of(offset(e, core, side), 16), part), :]

    def send_own(e):
        dst = region(e, row, col, core, side)
        src = own_part(e)
        for step in range(1, cols):
            sends.start(col + step < cols, src, dst, z_out.at[e, step, 0], z_in.at[e, col], {"col": jnp.minimum(col + step, cols - 1)})
            sends.start(col >= step, src, dst, z_out.at[e, step, 1], z_in.at[e, col], {"col": jnp.maximum(col - step, 0)})
            if step == 1:
                sends.start(None, src, dst, x_out.at[e, col], x_in.at[e, col], x_dev)

    def keep_own(m):
        height, width = blocks[m].shape
        return pltpu.make_async_copy(
            blocks[m],
            wholes[m].at[pl.ds(pl.multiple_of(row * height, height), height),
                         pl.ds(pl.multiple_of(col * width, width), width)],
            own_sem.at[m])

    def share(m, of_row, of_col, when):
        piece = region(m, of_row, of_col, core, side)
        if entries[m][1]:
            sends.start(when, piece, piece, y_out.at[m, of_row, of_col], y_in.at[m, of_row, of_col], y_dev)
        sends.start(when, piece, piece, c_out.at[m, of_row, of_col, 0], c_in.at[m, of_row, of_col, 0], c_dev)

    def columns(step):
        if step == 0:
            return [(0, None, col)]
        return [(-1, col >= step, jnp.maximum(col - step, 0)),
                (1, col + step < cols, jnp.minimum(col + step, cols - 1))]

    def guarded(when, body):
        if when is None:
            body()
        else:
            pl.when(when)(body)

    def both(a, b):
        return b if a is None else jnp.logical_and(a, b)

    def z_stage(m, step):
        if step == 0:
            if m + ahead < number:
                send_own(m + ahead)
            return
        for sign, when, at in columns(step):
            piece = region(m, row, at, core, side)
            guarded(when, lambda: wait_arrival(piece, z_in.at[m, at], {"col": col}))
            sends.start(when, piece, piece, x_out.at[m, at], x_in.at[m, at], x_dev)
            share(m, row, at, when)

    def x_stage(m, step):
        for _, when, at in columns(step):
            piece = region(m, other, at, core, side)
            guarded(when, lambda: wait_arrival(piece, x_in.at[m, at], x_dev))
            share(m, other, at, when)

    def y_stage(m, step):
        if not entries[m][1]:
            return
        for _, when, at in columns(step):
            for of_row in (row, other):
                if step == 0 and of_row is row:
                    continue
                piece = region(m, of_row, at, core, 1 - side)
                guarded(when, lambda: wait_arrival(piece, y_in.at[m, of_row, at], y_dev))
                sends.start(when, piece, piece, c_out.at[m, of_row, at, 1], c_in.at[m, of_row, at, 1], c_dev)

    def c_stage(m, step):
        for _, when, at in columns(step):
            for of_row in (row, other):
                if step == 0 and of_row is row:
                    continue
                piece = region(m, of_row, at, 1 - core, side)
                guarded(when, lambda: wait_arrival(piece, c_in.at[m, of_row, at, 0], c_dev))
                if entries[m][1]:
                    far = region(m, of_row, at, 1 - core, 1 - side)
                    guarded(when, lambda: wait_arrival(far, c_in.at[m, of_row, at, 1], c_dev))

    for e in range(ahead):
        send_own(e)
    for m in range(count):
        keep_own(m).start()
    keep_vec = pltpu.make_async_copy(vec, vecs.at[mine], own_vec)
    keep_vec.start()
    items = [(e, step) for e in range(number) for step in range(cols)]
    for tick in range(len(items) + LAGS[-1]):
        for lag, stage in zip(LAGS, (z_stage, x_stage, y_stage, c_stage)):
            if 0 <= tick - lag < len(items):
                stage(*items[tick - lag])
    for step in range(1, rows * cols):
        peer = (mine + step) % (rows * cols)
        wait_arrival(vecs.at[peer], v_in.at[peer], {"row": peer // cols, "col": peer % cols})
    for m in range(count):
        keep_own(m).wait()
    keep_vec.wait()
    sends.finish()


def gather_all(blocks, vec, ahead=3):
    rows, cols = lax.axis_size("row"), lax.axis_size("col")
    count = len(blocks)
    wholes = [jax.ShapeDtypeStruct((b.shape[0] * rows, b.shape[1] * cols), b.dtype) for b in blocks]
    out_shape = (*wholes, jax.ShapeDtypeStruct((rows * cols, *vec.shape), vec.dtype))
    entries = entries_of([b.shape[0] for b in blocks])
    number = len(entries)
    dma = pltpu.SemaphoreType.DMA
    return pl.pallas_call(
        functools.partial(gather_kernel, rows, cols, entries, ahead),
        out_shape=out_shape,
        in_specs=[pl.BlockSpec(memory_space=pltpu.VMEM)] * (count + 1),
        out_specs=[pl.BlockSpec(memory_space=pl.ANY)] * (count + 1),
        scratch_shapes=[
            dma((number, cols)), dma((number, cols)), dma((number, rows, cols)), dma((number, rows, cols, 2)), dma((rows * cols,)),
            dma((number, cols, 2)), dma((number, cols)), dma((number, rows, cols)), dma((number, rows, cols, 2)), dma((rows * cols,)),
            dma((count,)), dma,
        ],
        compiler_params=pltpu.CompilerParams(collective_id=0, has_side_effects=True),
        name="gather_all",
    )(*blocks, vec)


RL = (0, 1, 2, 3, 4, 5, 6)

def reduce_entries(heights):
    found = []
    for m, height in enumerate(heights):
        found.append((m, True, 0, height // 8))
        found.append((m, False, height // 2, height // 4))
    return found


def add_into(into, other):
    height, width = into.shape
    rows = max(16, min(height, 65536 // width // 16 * 16))
    while height % rows:
        rows -= 16

    @pl.loop(0, height // rows)
    def _(i):
        at = pl.ds(pl.multiple_of(i * rows, rows), rows)
        into[at, :] = into[at, :] + other[at, :]


def reduce_kernel(rows, cols, entries, *refs):
    count = 1 + max(entry[0] for entry in entries)
    number = len(entries)
    terms, vec = refs[:count], refs[count]
    outs, vec_out = refs[count + 1 : 2 * count + 1], refs[2 * count + 1]
    rest = list(refs[2 * count + 2 :])
    take = lambda n: [rest.pop(0) for _ in range(n)]
    acc, c_land, y_land, x_land, z_land, f_land = (take(number) for _ in range(6))
    full = take(count)
    v_acc, v_pair, v_cols = take(3)
    (load_sem, c_in, y_in, x_in, z_in, f_in, g_in, vp_in, vc_in,
     c_out, y_out, x_out, z_out, f_out, g_out, vp_out, vc_out) = rest
    row, col, dp, core, side = place()
    group_barrier(rows, cols)
    sends = Sends()
    other = 1 - row
    x_dev, y_dev, c_dev = {"row": other}, y_peer(dp), core_peer(dp)

    def band(e, of_row, of_core):
        m, paired, base, part = entries[e]
        height = terms[m].shape[0] // rows
        size = 2 * part if paired else part
        start = of_row * height + base + of_core * size
        return terms[m].at[pl.ds(pl.multiple_of(start, 16), size), :]

    def load(e):
        return [pltpu.make_async_copy(band(e, r, core), acc[e].at[r], load_sem.at[e, r]) for r in range(rows)]

    for e in range(number):
        for r in range(rows):
            sends.start(None, band(e, r, 1 - core), c_land[e].at[r], c_out.at[e, r], c_in.at[e, r], c_dev)
        for copy in load(e):
            copy.start()

    def mine(e, r, of_side):
        _, paired, _, part = entries[e]
        if paired:
            return acc[e].at[r, pl.ds(pl.multiple_of(of_side * part, 16), part), :]
        return acc[e].at[r]

    def columns(ref, e, at):
        width = terms[entries[e][0]].shape[1] // cols
        return ref.at[:, pl.ds(pl.multiple_of(at * width, width), width)]

    def send_x(e):
        sends.start(None, mine(e, other, side), x_land[e], x_out.at[e], x_in.at[e], x_dev)

    def core_stage(e):
        for copy in load(e):
            copy.wait()
        for r in range(rows):
            wait_arrival(c_land[e].at[r], c_in.at[e, r], c_dev)
        if entries[e][1]:
            for r in range(rows):
                add_into(mine(e, r, 1 - side), y_view(e, r))
                sends.start(None, mine(e, r, 1 - side), y_land[e].at[r], y_out.at[e, r], y_in.at[e, r], y_dev)
            for r in range(rows):
                add_into(mine(e, r, side), y_view(e, r, side))
        else:
            add_into(acc[e].at[other], c_land[e].at[other])
            send_x(e)
            add_into(acc[e].at[row], c_land[e].at[row])

    def y_view(e, r, of_side=None):
        part = entries[e][3]
        at = 1 - side if of_side is None else of_side
        return c_land[e].at[r, pl.ds(pl.multiple_of(at * part, 16), part), :]

    def y_stage(e):
        if not entries[e][1]:
            return
        for r in (other, row):
            wait_arrival(y_land[e].at[r], y_in.at[e, r], y_dev)
            add_into(mine(e, r, side), y_land[e].at[r])
            if r is other:
                send_x(e)

    def x_stage(e):
        wait_arrival(x_land[e], x_in.at[e], x_dev)
        add_into(mine(e, row, side), x_land[e])
        for step in range(1, cols):
            for way, ok, to in ((0, col + step < cols, jnp.minimum(col + step, cols - 1)),
                                (1, col >= step, jnp.maximum(col - step, 0))):
                sends.start(ok, columns(mine(e, row, side), e, to), z_land[e].at[col],
                            z_out.at[e, step, way], z_in.at[e, col], {"col": to})

    def out_rows(e, of_core, of_side):
        m, paired, base, part = entries[e]
        start = base + ((of_core * 2 + of_side) * part if paired else of_core * part)
        return full[m].at[pl.ds(pl.multiple_of(start, 16), part), :]

    def z_stage(e):
        total = columns(mine(e, row, side), e, col)
        for step in range(1, cols):
            for ok, at in ((col + step < cols, jnp.minimum(col + step, cols - 1)),
                           (col >= step, jnp.maximum(col - step, 0))):
                @pl.when(ok)
                def _():
                    wait_arrival(z_land[e].at[at], z_in.at[e, at], {"col": at})
                    add_into(total, z_land[e].at[at])
        if entries[e][1]:
            sends.start(None, total, out_rows(e, core, side), f_out.at[e], f_in.at[e], y_dev)
            sends.start(None, total, out_rows(e, core, side), g_out.at[e, 0], g_in.at[e, 0], c_dev)
            out_rows(e, core, side)[...] = total[...]
        else:
            sends.start(None, total, f_land[e], f_out.at[e], f_in.at[e], y_dev)

    def final_stage(e):
        m = entries[e][0]
        if entries[e][1]:
            piece = out_rows(e, core, 1 - side)
            wait_arrival(piece, f_in.at[e], y_dev)
            sends.start(None, piece, piece, g_out.at[e, 1], g_in.at[e, 1], c_dev)
        else:
            total = columns(mine(e, row, side), e, col)
            wait_arrival(f_land[e], f_in.at[e], y_dev)
            piece = out_rows(e, core, side)
            piece[...] = total[...] + f_land[e][...]
            sends.start(None, piece, piece, g_out.at[e, 0], g_in.at[e, 0], c_dev)

    def out_stage(e):
        m = entries[e][0]
        wait_arrival(out_rows(e, 1 - core, side), g_in.at[e, 0], c_dev)
        if entries[e][1]:
            wait_arrival(out_rows(e, 1 - core, 1 - side), g_in.at[e, 1], c_dev)
        _, paired, base, part = entries[e]
        size = 4 * part if paired else 2 * part

        @pl.loop(0, size // 32)
        def _(i):
            at = pl.ds(pl.multiple_of(base + i * 32, 32), 32)
            outs[m][at, :] = full[m][at, :].astype(jnp.float32)

    v_rows = v_acc.shape[0]
    merge = lambda a, b: jnp.concatenate([a[: v_rows - 8] + b[: v_rows - 8], jnp.maximum(a[v_rows - 8 :], b[v_rows - 8 :])])
    v_devs = (c_dev, y_dev, x_dev)

    def vec_send(k):
        src = vec if k == 0 else v_acc.at[k - 1]
        sends.start(None, src, v_pair.at[k], vp_out.at[k], vp_in.at[k], v_devs[k])

    def vec_merge(k):
        wait_arrival(v_pair.at[k], vp_in.at[k], v_devs[k])
        before = vec[...] if k == 0 else v_acc_load(k - 1)
        v_acc.at[k][...] = merge(before, v_pair[k])

    def v_acc_load(k):
        return v_acc[k]

    def vec_cols():
        for step in range(1, cols):
            to = (col + step) % cols
            sends.start(None, v_acc.at[2], v_cols.at[col], vc_out.at[step], vc_in.at[col], {"col": to})
        v_cols[pl.ds(col, 1)] = v_acc[2][None]

    def vec_last():
        for step in range(1, cols):
            at = (col + step) % cols
            wait_arrival(v_cols.at[at], vc_in.at[at], {"col": at})
        total = v_cols[0]
        for k in range(1, cols):
            total = merge(total, v_cols[k])
        vec_out[...] = total

    v_rows = v_acc.shape[1]
    steps = [lambda: vec_send(0), lambda: (vec_merge(0), vec_send(1)), lambda: (vec_merge(1), vec_send(2)),
             lambda: (vec_merge(2), vec_cols()), vec_last]
    stages = (core_stage, y_stage, x_stage, z_stage, final_stage, out_stage)
    for tick in range(number + RL[5]):
        for lag, stage in zip(RL, stages):
            if 0 <= tick - lag < number:
                stage(tick - lag)
        if tick < len(steps):
            steps[tick]()
    sends.finish()


def reduce_all(terms, vec, order):
    rows, cols = lax.axis_size("row"), lax.axis_size("col")
    count = len(terms)
    heights = [t.shape[0] // rows for t in terms]
    widths = [t.shape[1] for t in terms]
    pairs = reduce_entries(heights)
    entries = [entry for m in order for entry in pairs if entry[0] == m]
    number = len(entries)
    low = jnp.bfloat16
    sizes = [(2 * part if paired else part, part, widths[m]) for m, paired, _, part in entries]
    vm = pltpu.VMEM
    dma = pltpu.SemaphoreType.DMA
    scratch = (
        [vm((rows, band, width), low) for band, _, width in sizes]
        + [vm((rows, band, width), low) for band, _, width in sizes]
        + [vm((rows, part, width) if entries[e][1] else (rows, 16, 128), low) for e, (_, part, width) in enumerate(sizes)]
        + [vm((part, width), low) for _, part, width in sizes]
        + [vm((cols, part, width // cols), low) for _, part, width in sizes]
        + [vm((part, width // cols), low) for _, part, width in sizes]
        + [vm((heights[m], widths[m] // cols), low) for m in range(count)]
        + [vm((3, *vec.shape), jnp.float32), vm((3, *vec.shape), jnp.float32), vm((cols, *vec.shape), jnp.float32)]
        + [dma((number, rows)), dma((number, rows)), dma((number, rows)), dma((number,)), dma((number, cols)),
           dma((number,)), dma((number, 2)), dma((3,)), dma((cols,)),
           dma((number, rows)), dma((number, rows)), dma((number,)), dma((number, cols, 2)),
           dma((number,)), dma((number, 2)), dma((3,)), dma((cols,))]
    )
    out_shape = tuple(jax.ShapeDtypeStruct((heights[m], widths[m] // cols), jnp.float32) for m in range(count))
    return pl.pallas_call(
        functools.partial(reduce_kernel, rows, cols, entries),
        out_shape=(*out_shape, jax.ShapeDtypeStruct(vec.shape, jnp.float32)),
        in_specs=[pl.BlockSpec(memory_space=pl.ANY)] * count + [pl.BlockSpec(memory_space=pltpu.VMEM)],
        out_specs=[pl.BlockSpec(memory_space=pltpu.VMEM)] * (count + 1),
        scratch_shapes=scratch,
        compiler_params=pltpu.CompilerParams(collective_id=1, has_side_effects=True, vmem_limit_bytes=64000 * 1024),
        name="reduce_all",
    )(*terms, vec)


norm_eps = 1e-12
neg_fill = -1e30
low_type = jnp.bfloat16


def norm_rows(values, gain_vec, shift_vec):
    center = values - jnp.mean(values, axis=-1, keepdims=True)
    spread = jnp.mean(center * center, axis=-1, keepdims=True)
    return center * lax.rsqrt(spread + norm_eps) * gain_vec + shift_vec


def gelu_exact(values):
    return jax.nn.gelu(values, approximate=False)


def forward_dot(operand, weight):
    return jnp.dot(operand, weight, preferred_element_type=jnp.float32)


def back_dot(gradient, weight):
    return lax.dot_general(gradient, weight, (((1,), (1,)), ((), ())), preferred_element_type=jnp.float32)


def weight_term(operand, gradient):
    return lax.dot_general(operand, gradient, (((0,), (0,)), ((), ())),
                           preferred_element_type=jnp.float32).astype(low_type)


def column_sum(gradient_low):
    return jnp.sum(gradient_low, axis=0, dtype=jnp.float32)


def masked_scores(query_heads, key_heads, allowed):
    scores = jnp.einsum(
        "sqhd,skhd->shqk", query_heads, key_heads, preferred_element_type=jnp.float32
    ) * DH ** (-0.5)
    return jnp.where(allowed, scores, neg_fill)


def vector_rows(vectors):
    return jnp.concatenate([v.reshape(-1, 128) for v in vectors])


def on_device(tokens, segment_ids, cotangent, weight_query, weight_key, weight_value, weight_output, weight_inner,
              weight_outer, bias_query, bias_value, bias_output, bias_inner, bias_outer, gain_attn, shift_attn,
              gain_block, shift_block, tau_num, tau_den):
    rows, cols = lax.axis_size("row"), lax.axis_size("col")
    groups = rows * cols
    matrices = (weight_query, weight_key, weight_value, weight_output, weight_inner, weight_outer)
    vectors = (bias_query, bias_value, bias_output, bias_inner, bias_outer, gain_attn, shift_attn, gain_block, shift_block)
    lengths = [v.shape[0] for v in vectors]
    spread = [n * groups for n in lengths]
    flat = jnp.concatenate(vectors).astype(low_type)
    vec_rows = -(-flat.shape[0] // 2048) * 16
    flat = jnp.pad(flat, (0, vec_rows * 128 - flat.shape[0])).reshape(vec_rows, 128)
    gathered = gather_all([m.astype(low_type) for m in matrices], flat)
    whole_query, whole_key, whole_value, whole_output, whole_inner, whole_outer = gathered[:6]
    all_vecs = gathered[6].reshape(groups, -1)
    full, start = [], 0
    for n in lengths:
        full.append(all_vecs[:, start : start + n].reshape(-1).astype(jnp.float32))
        start += n
    (add_query, add_value, add_output, add_inner, add_outer,
     scale_attn, offset_attn, scale_block, offset_block) = full

    token_count = tokens.shape[0]
    seq_count = token_count // SEQ
    head_shape = (seq_count, SEQ, H, DH)
    token_low = tokens.astype(low_type)
    query_low = (forward_dot(token_low, whole_query) + add_query).astype(low_type)
    key_low = forward_dot(token_low, whole_key).astype(low_type)
    value_low = (forward_dot(token_low, whole_value) + add_value).astype(low_type)
    query_heads = query_low.reshape(head_shape)
    key_heads = key_low.reshape(head_shape)
    value_heads = value_low.reshape(head_shape)
    segment_rows = segment_ids.reshape(seq_count, SEQ)
    allowed = (segment_rows[:, :, None] == segment_rows[:, None, :])[:, None, :, :]
    masked = masked_scores(query_heads, key_heads, allowed)
    local_top = jnp.max(masked, axis=(0, 2, 3))
    row_top = jnp.max(masked, axis=-1, keepdims=True)
    raised = jnp.exp(masked - row_top)
    row_total = jnp.sum(raised, axis=-1, keepdims=True)
    attend = raised / row_total
    log_total = row_top + jnp.log(row_total)
    context = jnp.einsum("shqk,skhd->sqhd", attend.astype(low_type), value_heads, preferred_element_type=jnp.float32)
    context_low = context.reshape(token_count, H * DH).astype(low_type)
    first_sum = tokens + forward_dot(context_low, whole_output) + add_output
    normed = norm_rows(first_sum, scale_attn, offset_attn)
    normed_low = normed.astype(low_type)
    hidden_pre = forward_dot(normed_low, whole_inner) + add_inner
    activated_low = gelu_exact(hidden_pre).astype(low_type)
    second_sum = normed + forward_dot(activated_low, whole_outer) + add_outer
    output = norm_rows(second_sum, scale_block, offset_block)
    grad_second, grad_scale_block, grad_offset_block = jax.vjp(norm_rows, second_sum, scale_block, offset_block)[1](cotangent)
    outer_grad_low = grad_second.astype(low_type)
    act_grad = back_dot(outer_grad_low, whole_outer)
    hidden_grad_low = jax.vjp(gelu_exact, hidden_pre)[1](act_grad)[0].astype(low_type)
    normed_grad = grad_second + back_dot(hidden_grad_low, whole_inner)
    grad_first, grad_scale_attn, grad_offset_attn = jax.vjp(norm_rows, first_sum, scale_attn, offset_attn)[1](normed_grad)
    branch_grad_low = grad_first.astype(low_type)
    context_grad_low = back_dot(branch_grad_low, whole_output).astype(low_type)
    masked_again = masked_scores(query_heads, key_heads, allowed)
    attend_again = jnp.exp(masked_again - log_total)
    attend_low = attend_again.astype(low_type)
    context_grad_heads = context_grad_low.reshape(head_shape)
    value_grad = jnp.einsum("shqk,sqhd->skhd", attend_low, context_grad_heads, preferred_element_type=jnp.float32)
    attend_grad = jnp.einsum("sqhd,skhd->shqk", context_grad_heads, value_heads, preferred_element_type=jnp.float32)
    score_grad = attend_again * (attend_grad - jnp.sum(attend_again * attend_grad, axis=-1, keepdims=True))
    score_grad_low = score_grad.astype(low_type)
    query_grad = jnp.einsum("shqk,skhd->sqhd", score_grad_low, key_heads, preferred_element_type=jnp.float32) * DH ** (-0.5)
    key_grad = jnp.einsum("shqk,sqhd->skhd", score_grad_low, query_heads, preferred_element_type=jnp.float32) * DH ** (-0.5)
    query_grad_low = query_grad.reshape(token_count, H * DH).astype(low_type)
    key_grad_low = key_grad.reshape(token_count, H * DH).astype(low_type)
    value_grad_low = value_grad.reshape(token_count, H * DH).astype(low_type)
    grad_tokens = (grad_first + back_dot(query_grad_low, whole_query) + back_dot(key_grad_low, whole_key)
                   + back_dot(value_grad_low, whole_value))
    terms = (
        weight_term(token_low, query_grad_low),
        weight_term(token_low, key_grad_low),
        weight_term(token_low, value_grad_low),
        weight_term(context_low, branch_grad_low),
        weight_term(normed_low, hidden_grad_low),
        weight_term(activated_low, outer_grad_low),
    )
    vector_grads = (column_sum(query_grad_low), column_sum(value_grad_low), column_sum(branch_grad_low),
                    column_sum(hidden_grad_low), column_sum(outer_grad_low),
                    grad_scale_attn, grad_offset_attn, grad_scale_block, grad_offset_block)
    peak_rows = jnp.pad(local_top, (0, 1024 - H), constant_values=neg_fill)
    vec = vector_rows((*vector_grads, peak_rows))
    reduced = reduce_all(terms, vec, (5, 4, 3, 0, 1, 2))
    block_grads, vec_total = sum_groups(reduced[:6], reduced[6])

    at = lax.axis_index("row") * cols + lax.axis_index("col")
    owned, start = [], 0
    for n, whole_n in zip(lengths, spread):
        vector = vec_total[start : start + whole_n // 128].reshape(-1)
        owned.append(lax.dynamic_slice(vector, (at * n,), (n,)))
        start += whole_n // 128
    head_peak = vec_total[start, :H]
    tau_value = tau_num[0].astype(jnp.float32) / tau_den[0].astype(jnp.float32)
    factor = jnp.sqrt(tau_value / jnp.maximum(head_peak, tau_value))
    col_width = weight_query.shape[1]
    col_heads = (lax.axis_index("col") * col_width + jnp.arange(col_width, dtype=jnp.int32)) // DH
    column_factor = jnp.sum(
        jnp.where(col_heads[:, None] == jnp.arange(H, dtype=jnp.int32)[None, :], factor[None, :], 0.0), axis=1)
    return (output, grad_tokens, *block_grads, *owned, head_peak,
            weight_query * column_factor[None, :], weight_key * column_factor[None, :])


def sum_groups(blocks, vec):
    count = lax.axis_size("dp")
    totals, vec_sum = list(blocks), vec
    split = vec.shape[0] - 8
    for step in range(4, count, 4):
        shift = [(i, (i + step) % count) for i in range(count)]
        totals = [t + lax.ppermute(b, "dp", shift) for t, b in zip(totals, blocks)]
        moved = lax.ppermute(vec, "dp", shift)
        vec_sum = jnp.concatenate([vec_sum[:split] + moved[:split], jnp.maximum(vec_sum[split:], moved[split:])])
    return totals, vec_sum


def solution(mesh):
    tokens_spec, block_spec, vector_spec = P(("dp", "row", "col"), None), P("row", "col"), P(("row", "col"))
    in_specs = (tokens_spec, P(("dp", "row", "col")), tokens_spec, *(block_spec,) * 6, *(vector_spec,) * 9, P(), P())
    out_specs = (tokens_spec, tokens_spec, *(block_spec,) * 6, *(vector_spec,) * 9, P(), block_spec, block_spec)
    return jax.shard_map(on_device, mesh=mesh, in_specs=in_specs, out_specs=out_specs, check_vma=False)
```

```python
import functools
import jax
import jax.numpy as jnp
from jax import lax
from jax.experimental import pallas as pl
from jax.experimental.pallas import tpu as pltpu
from jax.sharding import PartitionSpec as P

MESH = pl.DeviceIdType.MESH

LAGS = (0, 2, 5)
SEQ, H, DH = 512, 16, 64
norm_eps = 1e-12
neg_fill = -1e30
low_type = jnp.bfloat16

def place():
    dp = lax.axis_index("dp")
    return lax.axis_index("row"), lax.axis_index("col"), dp, dp % 2, (dp // 2) % 2


def core_peer(dp):
    return {"dp": dp + 1 - 2 * (dp % 2)}


def y_peer(dp):
    side = (dp // 2) % 2
    return {"dp": dp + 2 - 4 * side}


class Sends:
    def __init__(self):
        self.items = []

    def start(self, when, src, dst, send_sem, recv_sem, device):
        copy = pltpu.make_async_remote_copy(
            src_ref=src, dst_ref=dst, send_sem=send_sem, recv_sem=recv_sem,
            device_id=device, device_id_type=MESH,
        )
        self.items.append((when, copy))
        if when is None:
            copy.start()
        else:
            pl.when(when)(copy.start)

    def finish(self):
        for when, copy in self.items:
            if when is None:
                copy.wait_send()
            else:
                pl.when(when)(copy.wait_send)


def wait_arrival(dst, recv_sem, device):
    pltpu.make_async_remote_copy(
        src_ref=dst, dst_ref=dst, send_sem=recv_sem, recv_sem=recv_sem,
        device_id=device, device_id_type=MESH,
    ).wait_recv()


def group_barrier(rows, cols):
    row, col, dp, _, _ = place()
    barrier = pltpu.get_barrier_semaphore()
    peers = [core_peer(dp), y_peer(dp)]
    mine = row * cols + col
    for step in range(1, rows * cols):
        other = (mine + step) % (rows * cols)
        peers.append({"row": other // cols, "col": other % cols})
    for peer in peers:
        pl.semaphore_signal(barrier, inc=1, device_id=peer, device_id_type=MESH)
    pl.semaphore_wait(barrier, len(peers))


def entries_of(heights):
    found = []
    for m, height in enumerate(heights):
        found.append((m, True, 0, height * 3 // 16))
        found.append((m, False, height * 3 // 4, height // 8))
    return found


def assemble_vectors(vecs, full_vec, lengths):
    groups = vecs.shape[0]
    for d in range(groups):
        rows_of = vecs[d].astype(jnp.float32)
        at = 0
        for i, n in enumerate(lengths):
            for part in range(-(-n // 128)):
                width = min(128, n - part * 128)
                start = d * n + part * 128
                full_vec[i : i + 1, start : start + width] = rows_of[at : at + 1, :width]
                at += 1


def row_stats(values):
    center = values - jnp.mean(values, axis=-1, keepdims=True)
    spread = jnp.mean(center * center, axis=-1, keepdims=True)
    scale = lax.rsqrt(spread + norm_eps)
    return center * scale, scale


def forward_kernel(rows, cols, entries, lengths, ahead, *refs):
    refs = list(refs)
    take = lambda n: [refs.pop(0) for _ in range(n)]
    blocks = take(6)
    vec, tokens, cotangent, seg_col, seg_row = take(5)
    wholes_out = take(6)
    (full_vec, q, k, v, ctx, stat, peak, n1, h1r, g, gp, output, dz2, sums) = take(14)
    wholes = take(6)
    vecs, token_low = take(2)
    (z_in, x_in, y_in, c_in, v_in, z_out, x_out, y_out, c_out, v_out, out_sem, own_vec) = refs
    count, number = 6, len(entries)
    row, col, dp, core, side = place()
    other = 1 - row
    mine = row * cols + col
    x_dev, y_dev, c_dev = {"row": other}, y_peer(dp), core_peer(dp)
    sends = Sends()

    for m in range(count):
        height, width = blocks[m].shape
        step = 32768 // width
        to_col = pl.ds(pl.multiple_of(col * width, width), width)

        @pl.loop(0, height // step)
        def _(i):
            wholes[m][pl.ds(pl.multiple_of(row * height + i * step, step), step), to_col] = (
                blocks[m][pl.ds(pl.multiple_of(i * step, step), step), :].astype(low_type))

    group_barrier(rows, cols)
    for step in range(1, rows * cols):
        peer = (mine + step) % (rows * cols)
        sends.start(None, vec, vecs.at[mine], v_out.at[step], v_in.at[mine], {"row": peer // cols, "col": peer % cols})

    def region(e, of_row, of_col, of_core, of_side):
        m, paired, base, part = entries[e]
        height, width = blocks[m].shape
        start = of_row * height + base + ((of_core * 2 + of_side) * part if paired else of_core * part)
        return wholes[m].at[pl.ds(pl.multiple_of(start, 16), part), pl.ds(pl.multiple_of(of_col * width, width), width)]

    def send_own(e):
        piece = region(e, row, col, core, side)
        for step in range(1, cols):
            sends.start(col + step < cols, piece, piece, z_out.at[e, step, 0], z_in.at[e, col], {"col": jnp.minimum(col + step, cols - 1)})
            sends.start(col >= step, piece, piece, z_out.at[e, step, 1], z_in.at[e, col], {"col": jnp.maximum(col - step, 0)})
            if step == 1:
                sends.start(None, piece, piece, x_out.at[e, col], x_in.at[e, col], x_dev)

    def share(e, of_row, of_col, when):
        piece = region(e, of_row, of_col, core, side)
        if entries[e][1]:
            sends.start(when, piece, piece, y_out.at[e, of_row, of_col], y_in.at[e, of_row, of_col], y_dev)
        sends.start(when, piece, piece, c_out.at[e, of_row, of_col, 0], c_in.at[e, of_row, of_col, 0], c_dev)

    def columns(step):
        if step == 0:
            return [(None, col)]
        return [(col >= step, jnp.maximum(col - step, 0)), (col + step < cols, jnp.minimum(col + step, cols - 1))]

    def guarded(when, body):
        if when is None:
            body()
        else:
            pl.when(when)(body)

    def z_stage(e, step):
        if step == 0:
            if e + ahead < number:
                send_own(e + ahead)
            return
        for when, at in columns(step):
            piece = region(e, row, at, core, side)
            guarded(when, lambda: wait_arrival(piece, z_in.at[e, at], {"col": col}))
            sends.start(when, piece, piece, x_out.at[e, at], x_in.at[e, at], x_dev)
            share(e, row, at, when)

    def x_stage(e, step):
        for when, at in columns(step):
            piece = region(e, other, at, core, side)
            guarded(when, lambda: wait_arrival(piece, x_in.at[e, at], x_dev))
            share(e, other, at, when)

    def y_stage(e, step):
        if not entries[e][1]:
            return
        for when, at in columns(step):
            for of_row in (row, other):
                if step == 0 and of_row is row:
                    continue
                piece = region(e, of_row, at, core, 1 - side)
                guarded(when, lambda: wait_arrival(piece, y_in.at[e, of_row, at], y_dev))
                sends.start(when, piece, piece, c_out.at[e, of_row, at, 1], c_in.at[e, of_row, at, 1], c_dev)

    def c_stage(e, step):
        for when, at in columns(step):
            for of_row in (row, other):
                if step == 0 and of_row is row:
                    continue
                piece = region(e, of_row, at, 1 - core, side)
                guarded(when, lambda: wait_arrival(piece, c_in.at[e, of_row, at, 0], c_dev))
                if entries[e][1]:
                    far = region(e, of_row, at, 1 - core, 1 - side)
                    guarded(when, lambda: wait_arrival(far, c_in.at[e, of_row, at, 1], c_dev))

    def keep(m):
        return pltpu.make_async_copy(wholes[m], wholes_out[m], out_sem.at[m])

    def complete(m):
        for e in range(number):
            if entries[e][0] == m:
                for step in range(cols):
                    c_stage(e, step)
        keep(m).start()

    tokens_count = tokens.shape[0]

    def cast_tokens():
        @pl.loop(0, tokens_count // 64)
        def _(i):
            at = pl.ds(pl.multiple_of(i * 64, 64), 64)
            token_low[at, :] = tokens[at, :].astype(low_type)

    def finish_vectors():
        for step in range(1, rows * cols):
            peer = (mine + step) % (rows * cols)
            wait_arrival(vecs.at[peer], v_in.at[peer], {"row": peer // cols, "col": peer % cols})
        keep_vec.wait()
        assemble_vectors(vecs, full_vec, lengths)

    def project(m, into, bias):
        @pl.loop(0, into.shape[1] // 256)
        def _(j):
            at = pl.ds(pl.multiple_of(j * 256, 256), 256)
            total = jnp.dot(token_low[...], wholes[m][:, at], preferred_element_type=jnp.float32)
            if bias is not None:
                total = total + full_vec[bias : bias + 1, at]
            into[:, at] = total.astype(low_type)

    def start_attention():
        stat[...] = jnp.zeros_like(stat)
        peak[...] = jnp.full(peak.shape, neg_fill, jnp.float32)

    def attend(pair, half):
        lanes = slice(pair * 128, pair * 128 + 128)
        lane = lax.broadcasted_iota(jnp.int32, (1, 128), 1)
        place_of = lax.broadcasted_iota(jnp.int32, (128, 128), 1)
        peak_place = lax.broadcasted_iota(jnp.int32, peak.shape, 1)

        @pl.loop(half * 2, half * 2 + 2)
        def _(i):
            at = pl.ds(pl.multiple_of(i * 128, 128), 128)
            same = seg_col[at, :] == seg_row[...]
            parts = []
            for a in range(2):
                head = 2 * pair + a
                keep_lanes = jnp.where((lane < 64) == (a == 0), DH ** (-0.5), 0.0).astype(low_type)
                scores = lax.dot_general(q[at, lanes] * keep_lanes, k[:, lanes], (((1,), (1,)), ((), ())),
                                         preferred_element_type=jnp.float32)
                scores = jnp.where(same, scores, neg_fill)
                top = jnp.max(scores, axis=1, keepdims=True)
                raised = jnp.exp(scores - top)
                total = jnp.sum(raised, axis=1, keepdims=True)
                attend_low = (raised * (1.0 / total)).astype(low_type)
                parts.append(jnp.dot(attend_low, v[:, lanes], preferred_element_type=jnp.float32))
                stat[at, :] = jnp.where(place_of == head, top + jnp.log(total), stat[at, :])
                peak[...] = jnp.where(peak_place == head, jnp.maximum(peak[...], jnp.max(top, axis=0, keepdims=True)), peak[...])
            ctx[at, lanes] = jnp.where(lane < 64, parts[0], parts[1]).astype(low_type)

    def first_norm(i):
        at = slice(i * 256, i * 256 + 256)
        place_of = lax.broadcasted_iota(jnp.int32, (256, 128), 1)

        @pl.loop(0, 4)
        def _(j):
            to = pl.ds(pl.multiple_of(j * 256, 256), 256)
            n1[at, to] = (tokens[at, to] + jnp.dot(ctx[at, :], wholes[3][:, to], preferred_element_type=jnp.float32)
                          + full_vec[2:3, to])

        @pl.loop(0, 8)
        def _(j):
            some = pl.ds(pl.multiple_of(i * 256 + j * 32, 32), 32)
            normal, scale = row_stats(n1[some, :])
            n1[some, :] = normal
            h1r[some, :] = (normal * full_vec[5:6, :1024] + full_vec[6:7, :1024]).astype(low_type)
            stat[some, :] = jnp.where(place_of[:32] == H, scale, stat[some, :])

    def hidden(lo, hi):
        @pl.loop(lo, hi)
        def _(j):
            at = pl.ds(pl.multiple_of(j * 256, 256), 256)
            u = jnp.dot(h1r[...], wholes[4][:, at], preferred_element_type=jnp.float32) + full_vec[3:4, at]
            below = 0.5 + 0.5 * lax.erf(u * 0.7071067811865476)
            g[:, at] = (u * below).astype(low_type)
            gp[:, at] = (below + u * (0.3989422804014327 * jnp.exp(-0.5 * u * u))).astype(low_type)

    def outer_product(step):
        here = slice(step * 1024, step * 1024 + 1024)

        @pl.loop(0, 4)
        def _(j):
            to = pl.ds(pl.multiple_of(j * 256, 256), 256)
            term = jnp.dot(g[:, here], wholes[5][here, to], preferred_element_type=jnp.float32)
            if step == 0:
                output[:, to] = term + (n1[:, to] * full_vec[5:6, to] + full_vec[6:7, to]) + full_vec[4:5, to]
            else:
                output[:, to] += term

    def second_norm():
        sums[...] = jnp.zeros_like(sums)

        @pl.loop(0, tokens_count // 32)
        def _(i):
            at = pl.ds(pl.multiple_of(i * 32, 32), 32)
            normal, scale = row_stats(output[at, :])
            grad = cotangent[at, :]
            scaled = grad * full_vec[7:8, :1024]
            gradient = (scaled - jnp.mean(scaled, axis=-1, keepdims=True)
                        - normal * jnp.mean(scaled * normal, axis=-1, keepdims=True)) * scale
            output[at, :] = normal * full_vec[7:8, :1024] + full_vec[8:9, :1024]
            dz2[at, :] = gradient
            low = gradient.astype(low_type).astype(jnp.float32)
            for r, part in enumerate((grad * normal, grad, low)):
                sums[r * 8 : r * 8 + 8, :] += part.reshape(4, 8, 1024).sum(axis=0)

    for e in range(ahead):
        send_own(e)
    keep_vec = pltpu.make_async_copy(vec, vecs.at[mine], own_vec)
    keep_vec.start()
    items = [(e, step) for e in range(number) for step in range(cols)]
    last = len(items) + LAGS[2]

    def ready(m):
        return min((2 * m + 2) * cols + LAGS[2] + 2, last)

    work = [(2, cast_tokens), (4, finish_vectors)]
    for m, into, bias in ((0, q, 0), (1, k, None), (2, v, 1)):
        work.append((ready(m), lambda m=m, into=into, bias=bias: (complete(m), project(m, into, bias))))
    work.append((ready(2), start_attention))
    work += [(ready(2) + 1 + (2 * pair + half) * cols // 4, lambda pair=pair, half=half: attend(pair, half))
             for pair in range(H // 2) for half in range(2)]
    work += [(ready(3), lambda: complete(3)), (ready(3), lambda: first_norm(0)), (ready(3), lambda: first_norm(1))]
    work.append((ready(4), lambda: complete(4)))
    work += [(ready(4) + lo // 2, lambda lo=lo: hidden(lo, lo + 2)) for lo in range(0, 16, 2)]
    work += [(ready(5), lambda: complete(5))] + [(ready(5), lambda s=s: outer_product(s)) for s in range(4)]
    work.append((ready(5), second_norm))

    for tick in range(last + 1):
        for lag, stage in zip(LAGS[:3], (z_stage, x_stage, y_stage)):
            if 0 <= tick - lag < len(items):
                stage(*items[tick - lag])
        while work and (work[0][0] <= tick or tick == last):
            work.pop(0)[1]()
    for m in range(count):
        keep(m).wait()
    sends.finish()


def forward_all(blocks, vec, lengths, tokens, cotangent, seg, ahead=3):
    rows, cols = lax.axis_size("row"), lax.axis_size("col")
    wholes = [jax.ShapeDtypeStruct((b.shape[0] * rows, b.shape[1] * cols), low_type) for b in blocks]
    entries = entries_of([b.shape[0] for b in blocks])
    number = len(entries)
    dma, vm, count = pltpu.SemaphoreType.DMA, pltpu.VMEM, tokens.shape[0]
    width, hidden = wholes[4].shape
    shape = jax.ShapeDtypeStruct
    f32 = jnp.float32
    results = [shape((16, hidden), f32), *[shape((count, width), low_type)] * 4, shape((count, 128), f32), shape((8, 128), f32),
               shape((count, width), f32), shape((count, width), low_type), shape((count, hidden), low_type),
               shape((count, hidden), low_type), shape((count, width), f32), shape((count, width), f32), shape((24, width), f32)]
    in_vmem = pl.BlockSpec(memory_space=pltpu.VMEM)
    found = pl.pallas_call(
        functools.partial(forward_kernel, rows, cols, entries, lengths, ahead),
        out_shape=(*wholes, *results),
        in_specs=[in_vmem] * 11,
        out_specs=[pl.BlockSpec(memory_space=pl.ANY)] * 6 + [in_vmem] * len(results),
        scratch_shapes=[vm(w.shape, low_type) for w in wholes] + [
            vm((rows * cols, *vec.shape), vec.dtype), vm(tokens.shape, low_type),
            dma((number, cols)), dma((number, cols)), dma((number, rows, cols)), dma((number, rows, cols, 2)), dma((rows * cols,)),
            dma((number, cols, 2)), dma((number, cols)), dma((number, rows, cols)), dma((number, rows, cols, 2)), dma((rows * cols,)),
            dma((6,)), dma,
        ],
        compiler_params=pltpu.CompilerParams(collective_id=0, has_side_effects=True, vmem_limit_bytes=65400 * 1024),
        name="forward_all",
    )(*blocks, vec, tokens, cotangent, seg.reshape(-1, 1), seg.reshape(1, -1))
    return found[:6], found[6:]


RL = (0, 1, 2, 3, 4, 5, 6)

def reduce_entries(heights):
    found = []
    for m, height in enumerate(heights):
        found.append((m, True, 0, height // 8))
        found.append((m, False, height // 2, height // 4))
    return found


def add_into(into, other):
    height, width = into.shape
    rows = max(16, min(height, 65536 // width // 16 * 16))
    while height % rows:
        rows -= 16

    @pl.loop(0, height // rows)
    def _(i):
        at = pl.ds(pl.multiple_of(i * rows, rows), rows)
        into[at, :] = into[at, :] + other[at, :]


def reduce_kernel(rows, cols, entries, *refs):
    count = 1 + max(entry[0] for entry in entries)
    number = len(entries)
    terms, vec = refs[:count], refs[count]
    outs, vec_out = refs[count + 1 : 2 * count + 1], refs[2 * count + 1]
    rest = list(refs[2 * count + 2 :])
    take = lambda n: [rest.pop(0) for _ in range(n)]
    acc, c_land, y_land, x_land, z_land, f_land = (take(number) for _ in range(6))
    full = take(count)
    v_acc, v_pair, v_cols = take(3)
    (load_sem, c_in, y_in, x_in, z_in, f_in, g_in, vp_in, vc_in,
     c_out, y_out, x_out, z_out, f_out, g_out, vp_out, vc_out) = rest
    row, col, dp, core, side = place()
    group_barrier(rows, cols)
    sends = Sends()
    other = 1 - row
    x_dev, y_dev, c_dev = {"row": other}, y_peer(dp), core_peer(dp)

    def band(e, of_row, of_core):
        m, paired, base, part = entries[e]
        height = terms[m].shape[0] // rows
        size = 2 * part if paired else part
        start = of_row * height + base + of_core * size
        return terms[m].at[pl.ds(pl.multiple_of(start, 16), size), :]

    def load(e):
        return [pltpu.make_async_copy(band(e, r, core), acc[e].at[r], load_sem.at[e, r]) for r in range(rows)]

    for e in range(number):
        for r in range(rows):
            sends.start(None, band(e, r, 1 - core), c_land[e].at[r], c_out.at[e, r], c_in.at[e, r], c_dev)
        for copy in load(e):
            copy.start()

    def mine(e, r, of_side):
        _, paired, _, part = entries[e]
        if paired:
            return acc[e].at[r, pl.ds(pl.multiple_of(of_side * part, 16), part), :]
        return acc[e].at[r]

    def columns(ref, e, at):
        width = terms[entries[e][0]].shape[1] // cols
        return ref.at[:, pl.ds(pl.multiple_of(at * width, width), width)]

    def send_x(e):
        sends.start(None, mine(e, other, side), x_land[e], x_out.at[e], x_in.at[e], x_dev)

    def core_stage(e):
        for copy in load(e):
            copy.wait()
        for r in range(rows):
            wait_arrival(c_land[e].at[r], c_in.at[e, r], c_dev)
        if entries[e][1]:
            for r in range(rows):
                add_into(mine(e, r, 1 - side), y_view(e, r))
                sends.start(None, mine(e, r, 1 - side), y_land[e].at[r], y_out.at[e, r], y_in.at[e, r], y_dev)
            for r in range(rows):
                add_into(mine(e, r, side), y_view(e, r, side))
        else:
            add_into(acc[e].at[other], c_land[e].at[other])
            send_x(e)
            add_into(acc[e].at[row], c_land[e].at[row])

    def y_view(e, r, of_side=None):
        part = entries[e][3]
        at = 1 - side if of_side is None else of_side
        return c_land[e].at[r, pl.ds(pl.multiple_of(at * part, 16), part), :]

    def y_stage(e):
        if not entries[e][1]:
            return
        for r in (other, row):
            wait_arrival(y_land[e].at[r], y_in.at[e, r], y_dev)
            add_into(mine(e, r, side), y_land[e].at[r])
            if r is other:
                send_x(e)

    def x_stage(e):
        wait_arrival(x_land[e], x_in.at[e], x_dev)
        add_into(mine(e, row, side), x_land[e])
        for step in range(1, cols):
            for way, ok, to in ((0, col + step < cols, jnp.minimum(col + step, cols - 1)),
                                (1, col >= step, jnp.maximum(col - step, 0))):
                sends.start(ok, columns(mine(e, row, side), e, to), z_land[e].at[col],
                            z_out.at[e, step, way], z_in.at[e, col], {"col": to})

    def out_rows(e, of_core, of_side):
        m, paired, base, part = entries[e]
        start = base + ((of_core * 2 + of_side) * part if paired else of_core * part)
        return full[m].at[pl.ds(pl.multiple_of(start, 16), part), :]

    def z_stage(e):
        total = columns(mine(e, row, side), e, col)
        for step in range(1, cols):
            for ok, at in ((col + step < cols, jnp.minimum(col + step, cols - 1)),
                           (col >= step, jnp.maximum(col - step, 0))):
                @pl.when(ok)
                def _():
                    wait_arrival(z_land[e].at[at], z_in.at[e, at], {"col": at})
                    add_into(total, z_land[e].at[at])
        if entries[e][1]:
            sends.start(None, total, out_rows(e, core, side), f_out.at[e], f_in.at[e], y_dev)
            sends.start(None, total, out_rows(e, core, side), g_out.at[e, 0], g_in.at[e, 0], c_dev)
            out_rows(e, core, side)[...] = total[...]
        else:
            sends.start(None, total, f_land[e], f_out.at[e], f_in.at[e], y_dev)

    def final_stage(e):
        m = entries[e][0]
        if entries[e][1]:
            piece = out_rows(e, core, 1 - side)
            wait_arrival(piece, f_in.at[e], y_dev)
            sends.start(None, piece, piece, g_out.at[e, 1], g_in.at[e, 1], c_dev)
        else:
            total = columns(mine(e, row, side), e, col)
            wait_arrival(f_land[e], f_in.at[e], y_dev)
            piece = out_rows(e, core, side)
            piece[...] = total[...] + f_land[e][...]
            sends.start(None, piece, piece, g_out.at[e, 0], g_in.at[e, 0], c_dev)

    def out_stage(e):
        m = entries[e][0]
        wait_arrival(out_rows(e, 1 - core, side), g_in.at[e, 0], c_dev)
        if entries[e][1]:
            wait_arrival(out_rows(e, 1 - core, 1 - side), g_in.at[e, 1], c_dev)
        _, paired, base, part = entries[e]
        size = 4 * part if paired else 2 * part

        @pl.loop(0, size // 32)
        def _(i):
            at = pl.ds(pl.multiple_of(base + i * 32, 32), 32)
            outs[m][at, :] = full[m][at, :].astype(jnp.float32)

    v_rows = v_acc.shape[0]
    merge = lambda a, b: jnp.concatenate([a[: v_rows - 8] + b[: v_rows - 8], jnp.maximum(a[v_rows - 8 :], b[v_rows - 8 :])])
    v_devs = (c_dev, y_dev, x_dev)

    def vec_send(k):
        src = vec if k == 0 else v_acc.at[k - 1]
        sends.start(None, src, v_pair.at[k], vp_out.at[k], vp_in.at[k], v_devs[k])

    def vec_merge(k):
        wait_arrival(v_pair.at[k], vp_in.at[k], v_devs[k])
        before = vec[...] if k == 0 else v_acc_load(k - 1)
        v_acc.at[k][...] = merge(before, v_pair[k])

    def v_acc_load(k):
        return v_acc[k]

    def vec_cols():
        for step in range(1, cols):
            to = (col + step) % cols
            sends.start(None, v_acc.at[2], v_cols.at[col], vc_out.at[step], vc_in.at[col], {"col": to})
        v_cols[pl.ds(col, 1)] = v_acc[2][None]

    def vec_last():
        for step in range(1, cols):
            at = (col + step) % cols
            wait_arrival(v_cols.at[at], vc_in.at[at], {"col": at})
        total = v_cols[0]
        for k in range(1, cols):
            total = merge(total, v_cols[k])
        vec_out[...] = total

    v_rows = v_acc.shape[1]
    steps = [lambda: vec_send(0), lambda: (vec_merge(0), vec_send(1)), lambda: (vec_merge(1), vec_send(2)),
             lambda: (vec_merge(2), vec_cols()), vec_last]
    stages = (core_stage, y_stage, x_stage, z_stage, final_stage, out_stage)
    for tick in range(number + RL[5]):
        for lag, stage in zip(RL, stages):
            if 0 <= tick - lag < number:
                stage(tick - lag)
        if tick < len(steps):
            steps[tick]()
    sends.finish()


def reduce_all(terms, vec, order):
    rows, cols = lax.axis_size("row"), lax.axis_size("col")
    count = len(terms)
    heights = [t.shape[0] // rows for t in terms]
    widths = [t.shape[1] for t in terms]
    pairs = reduce_entries(heights)
    entries = [entry for m in order for entry in pairs if entry[0] == m]
    number = len(entries)
    low = jnp.bfloat16
    sizes = [(2 * part if paired else part, part, widths[m]) for m, paired, _, part in entries]
    vm = pltpu.VMEM
    dma = pltpu.SemaphoreType.DMA
    scratch = (
        [vm((rows, band, width), low) for band, _, width in sizes]
        + [vm((rows, band, width), low) for band, _, width in sizes]
        + [vm((rows, part, width) if entries[e][1] else (rows, 16, 128), low) for e, (_, part, width) in enumerate(sizes)]
        + [vm((part, width), low) for _, part, width in sizes]
        + [vm((cols, part, width // cols), low) for _, part, width in sizes]
        + [vm((part, width // cols), low) for _, part, width in sizes]
        + [vm((heights[m], widths[m] // cols), low) for m in range(count)]
        + [vm((3, *vec.shape), jnp.float32), vm((3, *vec.shape), jnp.float32), vm((cols, *vec.shape), jnp.float32)]
        + [dma((number, rows)), dma((number, rows)), dma((number, rows)), dma((number,)), dma((number, cols)),
           dma((number,)), dma((number, 2)), dma((3,)), dma((cols,)),
           dma((number, rows)), dma((number, rows)), dma((number,)), dma((number, cols, 2)),
           dma((number,)), dma((number, 2)), dma((3,)), dma((cols,))]
    )
    out_shape = tuple(jax.ShapeDtypeStruct((heights[m], widths[m] // cols), jnp.float32) for m in range(count))
    return pl.pallas_call(
        functools.partial(reduce_kernel, rows, cols, entries),
        out_shape=(*out_shape, jax.ShapeDtypeStruct(vec.shape, jnp.float32)),
        in_specs=[pl.BlockSpec(memory_space=pl.ANY)] * count + [pl.BlockSpec(memory_space=pltpu.VMEM)],
        out_specs=[pl.BlockSpec(memory_space=pltpu.VMEM)] * (count + 1),
        scratch_shapes=scratch,
        compiler_params=pltpu.CompilerParams(collective_id=1, has_side_effects=True, vmem_limit_bytes=64000 * 1024),
        name="reduce_all",
    )(*terms, vec)


def forward_dot(operand, weight):
    return jnp.dot(operand, weight, preferred_element_type=jnp.float32)


def back_dot(gradient, weight):
    return lax.dot_general(gradient, weight, (((1,), (1,)), ((), ())), preferred_element_type=jnp.float32)


def weight_term(operand, gradient):
    return lax.dot_general(operand, gradient, (((0,), (0,)), ((), ())),
                           preferred_element_type=jnp.float32).astype(low_type)


def column_sum(gradient_low):
    return jnp.sum(gradient_low, axis=0, dtype=jnp.float32)


def masked_scores(query_heads, key_heads, allowed):
    scores = jnp.einsum(
        "sqhd,skhd->shqk", query_heads, key_heads, preferred_element_type=jnp.float32
    ) * DH ** (-0.5)
    return jnp.where(allowed, scores, neg_fill)


def vector_rows(vectors):
    return jnp.concatenate([v.reshape(-1, 128) for v in vectors])


def pad_rows(vector):
    short = -vector.shape[0] % 128
    return jnp.pad(vector, (0, short)).reshape(-1, 128)


def on_device(tokens, segment_ids, cotangent, weight_query, weight_key, weight_value, weight_output, weight_inner,
              weight_outer, bias_query, bias_value, bias_output, bias_inner, bias_outer, gain_attn, shift_attn,
              gain_block, shift_block, tau_num, tau_den):
    rows, cols = lax.axis_size("row"), lax.axis_size("col")
    groups = rows * cols
    matrices = (weight_query, weight_key, weight_value, weight_output, weight_inner, weight_outer)
    vectors = (bias_query, bias_value, bias_output, bias_inner, bias_outer, gain_attn, shift_attn, gain_block, shift_block)
    lengths = [v.shape[0] for v in vectors]
    spread = [n * groups for n in lengths]
    flat = jnp.concatenate([pad_rows(v) for v in vectors]).astype(low_type)
    flat = jnp.pad(flat, ((0, -flat.shape[0] % 16), (0, 0)))
    wholes, found = forward_all(matrices, flat, lengths, tokens, cotangent, segment_ids)
    whole_query, whole_key, whole_value, whole_output, whole_inner, whole_outer = wholes
    (params, query_low, key_low, value_low, context_low, stat, peak, normal_first, normed_low, activated_low,
     slope, output, grad_second, sums) = found
    scale_attn = params[5, : tokens.shape[1]]
    sums = sums.reshape(3, 8, -1).sum(axis=1)

    token_count = tokens.shape[0]
    seq_count = token_count // SEQ
    head_shape = (seq_count, SEQ, H, DH)
    token_low = tokens.astype(low_type)
    query_heads = query_low.reshape(head_shape)
    key_heads = key_low.reshape(head_shape)
    value_heads = value_low.reshape(head_shape)
    segment_rows = segment_ids.reshape(seq_count, SEQ)
    allowed = (segment_rows[:, :, None] == segment_rows[:, None, :])[:, None, :, :]
    outer_grad_low = grad_second.astype(low_type)
    act_grad = back_dot(outer_grad_low, whole_outer)
    hidden_grad_low = (act_grad * slope.astype(jnp.float32)).astype(low_type)
    normed_grad = grad_second + back_dot(hidden_grad_low, whole_inner)
    scaled = normed_grad * scale_attn
    grad_first = (scaled - jnp.mean(scaled, axis=-1, keepdims=True)
                  - normal_first * jnp.mean(scaled * normal_first, axis=-1, keepdims=True)) * stat[:, H : H + 1]
    grad_scale_attn = jnp.sum(normed_grad * normal_first, axis=0)
    grad_offset_attn = jnp.sum(normed_grad, axis=0)
    branch_grad_low = grad_first.astype(low_type)
    context_grad_low = back_dot(branch_grad_low, whole_output).astype(low_type)
    masked_again = masked_scores(query_heads, key_heads, allowed)
    log_total = stat[:, :H].T[None, :, :, None]
    attend_again = jnp.exp(masked_again - log_total)
    attend_low = attend_again.astype(low_type)
    context_grad_heads = context_grad_low.reshape(head_shape)
    value_grad = jnp.einsum("shqk,sqhd->skhd", attend_low, context_grad_heads, preferred_element_type=jnp.float32)
    attend_grad = jnp.einsum("sqhd,skhd->shqk", context_grad_heads, value_heads, preferred_element_type=jnp.float32)
    score_grad = attend_again * (attend_grad - jnp.sum(attend_again * attend_grad, axis=-1, keepdims=True))
    score_grad_low = score_grad.astype(low_type)
    query_grad = jnp.einsum("shqk,skhd->sqhd", score_grad_low, key_heads, preferred_element_type=jnp.float32) * DH ** (-0.5)
    key_grad = jnp.einsum("shqk,sqhd->skhd", score_grad_low, query_heads, preferred_element_type=jnp.float32) * DH ** (-0.5)
    query_grad_low = query_grad.reshape(token_count, H * DH).astype(low_type)
    key_grad_low = key_grad.reshape(token_count, H * DH).astype(low_type)
    value_grad_low = value_grad.reshape(token_count, H * DH).astype(low_type)
    grad_tokens = (grad_first + back_dot(query_grad_low, whole_query) + back_dot(key_grad_low, whole_key)
                   + back_dot(value_grad_low, whole_value))
    terms = (
        weight_term(token_low, query_grad_low),
        weight_term(token_low, key_grad_low),
        weight_term(token_low, value_grad_low),
        weight_term(context_low, branch_grad_low),
        weight_term(normed_low, hidden_grad_low),
        weight_term(activated_low, outer_grad_low),
    )
    vector_grads = (column_sum(query_grad_low), column_sum(value_grad_low), column_sum(branch_grad_low),
                    column_sum(hidden_grad_low), sums[2], grad_scale_attn, grad_offset_attn, sums[0], sums[1])
    vec = vector_rows((*vector_grads, peak))
    reduced = reduce_all(terms, vec, (5, 4, 3, 0, 1, 2))
    block_grads, vec_total = sum_groups(reduced[:6], reduced[6])

    at = lax.axis_index("row") * cols + lax.axis_index("col")
    owned, start = [], 0
    for n, whole_n in zip(lengths, spread):
        vector = vec_total[start : start + whole_n // 128].reshape(-1)
        owned.append(lax.dynamic_slice(vector, (at * n,), (n,)))
        start += whole_n // 128
    head_peak = vec_total[start, :H]
    tau_value = tau_num[0].astype(jnp.float32) / tau_den[0].astype(jnp.float32)
    factor = jnp.sqrt(tau_value / jnp.maximum(head_peak, tau_value))
    col_width = weight_query.shape[1]
    col_heads = (lax.axis_index("col") * col_width + jnp.arange(col_width, dtype=jnp.int32)) // DH
    column_factor = jnp.sum(
        jnp.where(col_heads[:, None] == jnp.arange(H, dtype=jnp.int32)[None, :], factor[None, :], 0.0), axis=1)
    return (output, grad_tokens, *block_grads, *owned, head_peak,
            weight_query * column_factor[None, :], weight_key * column_factor[None, :])


def sum_groups(blocks, vec):
    count = lax.axis_size("dp")
    totals, vec_sum = list(blocks), vec
    split = vec.shape[0] - 8
    for step in range(4, count, 4):
        shift = [(i, (i + step) % count) for i in range(count)]
        totals = [t + lax.ppermute(b, "dp", shift) for t, b in zip(totals, blocks)]
        moved = lax.ppermute(vec, "dp", shift)
        vec_sum = jnp.concatenate([vec_sum[:split] + moved[:split], jnp.maximum(vec_sum[split:], moved[split:])])
    return totals, vec_sum


def solution(mesh):
    tokens_spec, block_spec, vector_spec = P(("dp", "row", "col"), None), P("row", "col"), P(("row", "col"))
    in_specs = (tokens_spec, P(("dp", "row", "col")), tokens_spec, *(block_spec,) * 6, *(vector_spec,) * 9, P(), P())
    out_specs = (tokens_spec, tokens_spec, *(block_spec,) * 6, *(vector_spec,) * 9, P(), block_spec, block_spec)
    return jax.shard_map(on_device, mesh=mesh, in_specs=in_specs, out_specs=out_specs, check_vma=False)
```

```python
import functools
import jax
import jax.numpy as jnp
from jax import lax
from jax.experimental import pallas as pl
from jax.experimental.pallas import tpu as pltpu
from jax.sharding import PartitionSpec as P

MESH = pl.DeviceIdType.MESH

LAGS = (0, 2, 5)
SEQ, H, DH = 512, 16, 64
norm_eps = 1e-12
neg_fill = -1e30
low_type = jnp.bfloat16

def place():
    dp = lax.axis_index("dp")
    return lax.axis_index("row"), lax.axis_index("col"), dp, dp % 2, (dp // 2) % 2


def core_peer(dp):
    return {"dp": dp + 1 - 2 * (dp % 2)}


def y_peer(dp):
    side = (dp // 2) % 2
    return {"dp": dp + 2 - 4 * side}


class Sends:
    def __init__(self):
        self.items = []

    def start(self, when, src, dst, send_sem, recv_sem, device):
        copy = pltpu.make_async_remote_copy(
            src_ref=src, dst_ref=dst, send_sem=send_sem, recv_sem=recv_sem,
            device_id=device, device_id_type=MESH,
        )
        self.items.append((when, copy))
        if when is None:
            copy.start()
        else:
            pl.when(when)(copy.start)

    def finish(self):
        for when, copy in self.items:
            if when is None:
                copy.wait_send()
            else:
                pl.when(when)(copy.wait_send)


def wait_arrival(dst, recv_sem, device):
    pltpu.make_async_remote_copy(
        src_ref=dst, dst_ref=dst, send_sem=recv_sem, recv_sem=recv_sem,
        device_id=device, device_id_type=MESH,
    ).wait_recv()


def group_barrier(rows, cols):
    row, col, dp, _, _ = place()
    barrier = pltpu.get_barrier_semaphore()
    peers = [core_peer(dp), y_peer(dp)]
    mine = row * cols + col
    for step in range(1, rows * cols):
        other = (mine + step) % (rows * cols)
        peers.append({"row": other // cols, "col": other % cols})
    for peer in peers:
        pl.semaphore_signal(barrier, inc=1, device_id=peer, device_id_type=MESH)
    pl.semaphore_wait(barrier, len(peers))


def entries_of(heights):
    found = []
    for m, height in enumerate(heights):
        found.append((m, True, 0, height * 3 // 16))
        found.append((m, False, height * 3 // 4, height // 8))
    return found


def assemble_vectors(vecs, full_vec, lengths):
    groups = vecs.shape[0]
    for d in range(groups):
        rows_of = vecs[d].astype(jnp.float32)
        at = 0
        for i, n in enumerate(lengths):
            for part in range(-(-n // 128)):
                width = min(128, n - part * 128)
                start = d * n + part * 128
                full_vec[i : i + 1, start : start + width] = rows_of[at : at + 1, :width]
                at += 1


def row_stats(values):
    center = values - jnp.mean(values, axis=-1, keepdims=True)
    spread = jnp.mean(center * center, axis=-1, keepdims=True)
    scale = lax.rsqrt(spread + norm_eps)
    return center * scale, scale


def forward_kernel(rows, cols, entries, lengths, ahead, *refs):
    refs = list(refs)
    take = lambda n: [refs.pop(0) for _ in range(n)]
    blocks = take(6)
    vec, tokens, cotangent, seg_col, seg_row = take(5)
    wholes_out, terms_out = take(3), take(3)
    (q, k, v, stat, token_low, dctx, output, dz, vec_terms) = take(9)
    wholes = take(6)
    (vecs, full_vec, ctx, peak, n1, h1r, g, gp, low_grad, sums, hidden_sums, staged) = take(12)
    (stage_sem, z_in, x_in, y_in, c_in, v_in, z_out, x_out, y_out, c_out, v_out, out_sem, own_vec) = refs
    count, number = 6, len(entries)
    row, col, dp, core, side = place()
    other = 1 - row
    mine = row * cols + col
    x_dev, y_dev, c_dev = {"row": other}, y_peer(dp), core_peer(dp)
    sends = Sends()

    for m in range(count):
        height, width = blocks[m].shape
        step = 32768 // width
        to_col = pl.ds(pl.multiple_of(col * width, width), width)

        @pl.loop(0, height // step)
        def _(i):
            wholes[m][pl.ds(pl.multiple_of(row * height + i * step, step), step), to_col] = (
                blocks[m][pl.ds(pl.multiple_of(i * step, step), step), :].astype(low_type))

    group_barrier(rows, cols)
    for step in range(1, rows * cols):
        peer = (mine + step) % (rows * cols)
        sends.start(None, vec, vecs.at[mine], v_out.at[step], v_in.at[mine], {"row": peer // cols, "col": peer % cols})

    def region(e, of_row, of_col, of_core, of_side):
        m, paired, base, part = entries[e]
        height, width = blocks[m].shape
        start = of_row * height + base + ((of_core * 2 + of_side) * part if paired else of_core * part)
        return wholes[m].at[pl.ds(pl.multiple_of(start, 16), part), pl.ds(pl.multiple_of(of_col * width, width), width)]

    def send_own(e):
        piece = region(e, row, col, core, side)
        for step in range(1, cols):
            sends.start(col + step < cols, piece, piece, z_out.at[e, step, 0], z_in.at[e, col], {"col": jnp.minimum(col + step, cols - 1)})
            sends.start(col >= step, piece, piece, z_out.at[e, step, 1], z_in.at[e, col], {"col": jnp.maximum(col - step, 0)})
            if step == 1:
                sends.start(None, piece, piece, x_out.at[e, col], x_in.at[e, col], x_dev)

    def share(e, of_row, of_col, when):
        piece = region(e, of_row, of_col, core, side)
        if entries[e][1]:
            sends.start(when, piece, piece, y_out.at[e, of_row, of_col], y_in.at[e, of_row, of_col], y_dev)
        sends.start(when, piece, piece, c_out.at[e, of_row, of_col, 0], c_in.at[e, of_row, of_col, 0], c_dev)

    def columns(step):
        if step == 0:
            return [(None, col)]
        return [(col >= step, jnp.maximum(col - step, 0)), (col + step < cols, jnp.minimum(col + step, cols - 1))]

    def guarded(when, body):
        if when is None:
            body()
        else:
            pl.when(when)(body)

    def z_stage(e, step):
        if step == 0:
            if e + ahead < number:
                send_own(e + ahead)
            return
        for when, at in columns(step):
            piece = region(e, row, at, core, side)
            guarded(when, lambda: wait_arrival(piece, z_in.at[e, at], {"col": col}))
            sends.start(when, piece, piece, x_out.at[e, at], x_in.at[e, at], x_dev)
            share(e, row, at, when)

    def x_stage(e, step):
        for when, at in columns(step):
            piece = region(e, other, at, core, side)
            guarded(when, lambda: wait_arrival(piece, x_in.at[e, at], x_dev))
            share(e, other, at, when)

    def y_stage(e, step):
        if not entries[e][1]:
            return
        for when, at in columns(step):
            for of_row in (row, other):
                if step == 0 and of_row is row:
                    continue
                piece = region(e, of_row, at, core, 1 - side)
                guarded(when, lambda: wait_arrival(piece, y_in.at[e, of_row, at], y_dev))
                sends.start(when, piece, piece, c_out.at[e, of_row, at, 1], c_in.at[e, of_row, at, 1], c_dev)

    def c_stage(e, step):
        for when, at in columns(step):
            for of_row in (row, other):
                if step == 0 and of_row is row:
                    continue
                piece = region(e, of_row, at, 1 - core, side)
                guarded(when, lambda: wait_arrival(piece, c_in.at[e, of_row, at, 0], c_dev))
                if entries[e][1]:
                    far = region(e, of_row, at, 1 - core, 1 - side)
                    guarded(when, lambda: wait_arrival(far, c_in.at[e, of_row, at, 1], c_dev))

    def keep(m):
        return pltpu.make_async_copy(wholes[m], wholes_out[m], out_sem.at[m])

    def complete(m):
        for e in range(number):
            if entries[e][0] == m:
                for step in range(cols):
                    c_stage(e, step)
        if m < 3:
            keep(m).start()

    tokens_count = tokens.shape[0]

    def cast_tokens():
        @pl.loop(0, tokens_count // 64)
        def _(i):
            at = pl.ds(pl.multiple_of(i * 64, 64), 64)
            token_low[at, :] = tokens[at, :].astype(low_type)

    def finish_vectors():
        for step in range(1, rows * cols):
            peer = (mine + step) % (rows * cols)
            wait_arrival(vecs.at[peer], v_in.at[peer], {"row": peer // cols, "col": peer % cols})
        keep_vec.wait()
        assemble_vectors(vecs, full_vec, lengths)

    def project(m, into, bias):
        @pl.loop(0, into.shape[1] // 256)
        def _(j):
            at = pl.ds(pl.multiple_of(j * 256, 256), 256)
            total = jnp.dot(token_low[...], wholes[m][:, at], preferred_element_type=jnp.float32)
            if bias is not None:
                total = total + full_vec[bias : bias + 1, at]
            into[:, at] = total.astype(low_type)

    def start_attention():
        stat[...] = jnp.zeros_like(stat)
        peak[...] = jnp.full(peak.shape, neg_fill, jnp.float32)

    def attend(pair, half):
        lanes = slice(pair * 128, pair * 128 + 128)
        lane = lax.broadcasted_iota(jnp.int32, (1, 128), 1)
        place_of = lax.broadcasted_iota(jnp.int32, (128, 128), 1)
        peak_place = lax.broadcasted_iota(jnp.int32, peak.shape, 1)

        @pl.loop(half * 2, half * 2 + 2)
        def _(i):
            at = pl.ds(pl.multiple_of(i * 128, 128), 128)
            same = seg_col[at, :] == seg_row[...]
            parts = []
            for a in range(2):
                head = 2 * pair + a
                keep_lanes = jnp.where((lane < 64) == (a == 0), DH ** (-0.5), 0.0).astype(low_type)
                scores = lax.dot_general(q[at, lanes] * keep_lanes, k[:, lanes], (((1,), (1,)), ((), ())),
                                         preferred_element_type=jnp.float32)
                scores = jnp.where(same, scores, neg_fill)
                top = jnp.max(scores, axis=1, keepdims=True)
                raised = jnp.exp(scores - top)
                total = jnp.sum(raised, axis=1, keepdims=True)
                attend_low = (raised * (1.0 / total)).astype(low_type)
                parts.append(jnp.dot(attend_low, v[:, lanes], preferred_element_type=jnp.float32))
                stat[at, :] = jnp.where(place_of == head, top + jnp.log(total), stat[at, :])
                peak[...] = jnp.where(peak_place == head, jnp.maximum(peak[...], jnp.max(top, axis=0, keepdims=True)), peak[...])
            ctx[at, lanes] = jnp.where(lane < 64, parts[0], parts[1]).astype(low_type)

    def first_norm(i):
        at = slice(i * 256, i * 256 + 256)
        place_of = lax.broadcasted_iota(jnp.int32, (256, 128), 1)

        @pl.loop(0, 4)
        def _(j):
            to = pl.ds(pl.multiple_of(j * 256, 256), 256)
            n1[at, to] = (tokens[at, to] + jnp.dot(ctx[at, :], wholes[3][:, to], preferred_element_type=jnp.float32)
                          + full_vec[2:3, to])

        @pl.loop(0, 8)
        def _(j):
            some = pl.ds(pl.multiple_of(i * 256 + j * 32, 32), 32)
            normal, scale = row_stats(n1[some, :])
            n1[some, :] = normal
            h1r[some, :] = (normal * full_vec[5:6, :1024] + full_vec[6:7, :1024]).astype(low_type)
            stat[some, :] = jnp.where(place_of[:32] == H, scale, stat[some, :])

    def hidden(lo, hi):
        @pl.loop(lo, hi)
        def _(j):
            at = pl.ds(pl.multiple_of(j * 256, 256), 256)
            u = jnp.dot(h1r[...], wholes[4][:, at], preferred_element_type=jnp.float32) + full_vec[3:4, at]
            below = 0.5 + 0.5 * lax.erf(u * 0.7071067811865476)
            g[:, at] = (u * below).astype(low_type)
            gp[:, at] = (below + u * (0.3989422804014327 * jnp.exp(-0.5 * u * u))).astype(low_type)

    def outer_product(step):
        here = slice(step * 1024, step * 1024 + 1024)

        @pl.loop(0, 4)
        def _(j):
            to = pl.ds(pl.multiple_of(j * 256, 256), 256)
            term = jnp.dot(g[:, here], wholes[5][here, to], preferred_element_type=jnp.float32)
            if step == 0:
                output[:, to] = term + (n1[:, to] * full_vec[5:6, to] + full_vec[6:7, to]) + full_vec[4:5, to]
            else:
                output[:, to] += term

    def second_norm():
        sums[...] = jnp.zeros_like(sums)

        @pl.loop(0, tokens_count // 32)
        def _(i):
            at = pl.ds(pl.multiple_of(i * 32, 32), 32)
            normal, scale = row_stats(output[at, :])
            grad = cotangent[at, :]
            scaled = grad * full_vec[7:8, :1024]
            gradient = (scaled - jnp.mean(scaled, axis=-1, keepdims=True)
                        - normal * jnp.mean(scaled * normal, axis=-1, keepdims=True)) * scale
            output[at, :] = normal * full_vec[7:8, :1024] + full_vec[8:9, :1024]
            dz[at, :] = gradient
            low = gradient.astype(low_type)
            low_grad[at, :] = low
            add_sums((low.astype(jnp.float32), grad * normal, grad), (0, 1, 2))

    def add_sums(parts, places):
        for part, r in zip(parts, places):
            sums[r * 8 : r * 8 + 8, :] += part.reshape(part.shape[0] // 8, 8, part.shape[1]).sum(axis=0)

    def weight_term(m, left, right, number_of):
        across = right.shape[1] // 1024

        def send(n):
            r, c = (n, 0) if across == 1 else (n // across, n % across)
            to = terms_out[m].at[pl.ds(pl.multiple_of(r * 256, 256), 256), pl.ds(pl.multiple_of(c * 1024, 1024), 1024)]
            return pltpu.make_async_copy(staged.at[n % 2], to, stage_sem.at[n % 2])

        @pl.loop(0, number_of)
        def _(n):
            r, c = (n, 0) if across == 1 else (n // across, n % across)

            @pl.when(n >= 2)
            def _():
                send(n - 2).wait()

            staged[n % 2] = lax.dot_general(
                left[:, pl.ds(pl.multiple_of(r * 256, 256), 256)], right[:, pl.ds(pl.multiple_of(c * 1024, 1024), 1024)],
                (((0,), (0,)), ((), ())), preferred_element_type=jnp.float32).astype(low_type)
            send(n).start()

        send(number_of - 2).wait()
        send(number_of - 1).wait()

    def hidden_gradient():
        @pl.loop(0, gp.shape[1] // 256)
        def _(j):
            at = pl.ds(pl.multiple_of(j * 256, 256), 256)
            act = lax.dot_general(low_grad[...], wholes[5][at, :], (((1,), (1,)), ((), ())), preferred_element_type=jnp.float32)
            low = (act * gp[:, at].astype(jnp.float32)).astype(low_type)
            gp[:, at] = low
            hidden_sums[:, at] = low.astype(jnp.float32).reshape(tokens_count // 8, 8, 256).sum(axis=0)

    def back_to_first():
        @pl.loop(0, 4)
        def _(j):
            to = pl.ds(pl.multiple_of(j * 256, 256), 256)
            dz[:, to] += lax.dot_general(gp[...], wholes[4][to, :], (((1,), (1,)), ((), ())), preferred_element_type=jnp.float32)

        @pl.loop(0, tokens_count // 32)
        def _(i):
            at = pl.ds(pl.multiple_of(i * 32, 32), 32)
            place_of = lax.broadcasted_iota(jnp.int32, (32, 128), 1)
            scale = jnp.sum(jnp.where(place_of == H, stat[at, :], 0.0), axis=1, keepdims=True)
            grad, normal = dz[at, :], n1[at, :]
            scaled = grad * full_vec[5:6, :1024]
            gradient = (scaled - jnp.mean(scaled, axis=-1, keepdims=True)
                        - normal * jnp.mean(scaled * normal, axis=-1, keepdims=True)) * scale
            dz[at, :] = gradient
            low = gradient.astype(low_type)
            low_grad[at, :] = low
            add_sums((low.astype(jnp.float32), grad * normal, grad), (3, 4, 5))

        @pl.loop(0, 4)
        def _(j):
            to = pl.ds(pl.multiple_of(j * 256, 256), 256)
            dctx[:, to] = lax.dot_general(low_grad[...], wholes[3][to, :], (((1,), (1,)), ((), ())),
                                          preferred_element_type=jnp.float32).astype(low_type)

    def collect_sums():
        vec_terms[0:16, :] = jnp.zeros((16, 128), jnp.float32)

        def put(start, total):
            for r in range(total.shape[1] // 128):
                vec_terms[start + r : start + r + 1, :] = total[:, r * 128 : r * 128 + 128]

        start = 16
        for r in (3, None, 0, 4, 5, 1, 2):
            source = hidden_sums[...] if r is None else sums[r * 8 : r * 8 + 8, :]
            put(start, jnp.sum(source, axis=0, keepdims=True))
            start += source.shape[1] // 128
        vec_terms[start : start + 8, :] = peak[...]

    for e in range(ahead):
        send_own(e)
    keep_vec = pltpu.make_async_copy(vec, vecs.at[mine], own_vec)
    keep_vec.start()
    items = [(e, step) for e in range(number) for step in range(cols)]
    last = len(items) + LAGS[2]

    def ready(m):
        return min((2 * m + 2) * cols + LAGS[2] + 2, last)

    work = [(2, cast_tokens), (4, finish_vectors)]
    for m, into, bias in ((0, q, 0), (1, k, None), (2, v, 1)):
        work.append((ready(m), lambda m=m, into=into, bias=bias: (complete(m), project(m, into, bias))))
    work.append((ready(2), start_attention))
    work += [(ready(2) + 1 + (2 * pair + half) * cols // 4, lambda pair=pair, half=half: attend(pair, half))
             for pair in range(H // 2) for half in range(2)]
    work += [(ready(3), lambda: complete(3)), (ready(3), lambda: first_norm(0)), (ready(3), lambda: first_norm(1))]
    work.append((ready(4), lambda: complete(4)))
    work += [(ready(4) + lo // 2, lambda lo=lo: hidden(lo, lo + 2)) for lo in range(0, 16, 2)]
    work += [(ready(5), lambda: complete(5))] + [(ready(5), lambda s=s: outer_product(s)) for s in range(4)]
    end = ready(5)
    work += [(end, second_norm), (end, lambda: weight_term(2, g, low_grad, g.shape[1] // 256)), (end, hidden_gradient),
             (end, lambda: weight_term(1, h1r, gp, 4 * (gp.shape[1] // 1024))), (end, back_to_first),
             (end, lambda: weight_term(0, ctx, low_grad, 4)), (end, collect_sums)]

    for tick in range(last + 1):
        for lag, stage in zip(LAGS[:3], (z_stage, x_stage, y_stage)):
            if 0 <= tick - lag < len(items):
                stage(*items[tick - lag])
        while work and (work[0][0] <= tick or tick == last):
            work.pop(0)[1]()
    for m in range(3):
        keep(m).wait()
    sends.finish()


def forward_all(blocks, vec, lengths, tokens, cotangent, seg, ahead=3):
    rows, cols = lax.axis_size("row"), lax.axis_size("col")
    wholes = [jax.ShapeDtypeStruct((b.shape[0] * rows, b.shape[1] * cols), low_type) for b in blocks]
    entries = entries_of([b.shape[0] for b in blocks])
    number = len(entries)
    dma, vm, count = pltpu.SemaphoreType.DMA, pltpu.VMEM, tokens.shape[0]
    width, hidden = wholes[4].shape
    shape = jax.ShapeDtypeStruct
    f32 = jnp.float32
    results = [*[shape((count, width), low_type)] * 3, shape((count, 128), f32), *[shape((count, width), low_type)] * 2,
               *[shape((count, width), f32)] * 2, shape(((width * 8 + hidden) // 128 + 8, 128), f32)]
    in_vmem = pl.BlockSpec(memory_space=pltpu.VMEM)
    found = pl.pallas_call(
        functools.partial(forward_kernel, rows, cols, entries, lengths, ahead),
        out_shape=(*wholes[:3], *wholes[3:], *results),
        in_specs=[in_vmem] * 11,
        out_specs=[pl.BlockSpec(memory_space=pl.ANY)] * 6 + [in_vmem] * len(results),
        scratch_shapes=[vm(w.shape, low_type) for w in wholes] + [
            vm((rows * cols, *vec.shape), vec.dtype), vm((16, hidden), f32), vm((count, width), low_type), vm((8, 128), f32),
            vm((count, width), f32), vm((count, width), low_type), vm((count, hidden), low_type), vm((count, hidden), low_type),
            vm((count, width), low_type), vm((48, width), f32), vm((8, hidden), f32), vm((2, 256, 1024), low_type), dma((2,)),
            dma((number, cols)), dma((number, cols)), dma((number, rows, cols)), dma((number, rows, cols, 2)), dma((rows * cols,)),
            dma((number, cols, 2)), dma((number, cols)), dma((number, rows, cols)), dma((number, rows, cols, 2)), dma((rows * cols,)),
            dma((3,)), dma,
        ],
        compiler_params=pltpu.CompilerParams(collective_id=0, has_side_effects=True, vmem_limit_bytes=65400 * 1024),
        name="forward_all",
    )(*blocks, vec, tokens, cotangent, seg.reshape(-1, 1), seg.reshape(1, -1))
    return found[:3], found[3:6], found[6:]


RL = (0, 1, 2, 3, 4, 5)
PARTS = (1, 1, 1, 1, 1, 1)

def reduce_entries(heights, order):
    found = []
    for m in order:
        height = heights[m]
        for i in range(PARTS[m]):
            base, size = i * height // PARTS[m], height // PARTS[m]
            found.append((m, True, base, size // 8))
            found.append((m, False, base + size // 2, size // 4))
    return found


def add_into(into, other):
    height, width = into.shape
    rows = max(16, min(height, 65536 // width // 16 * 16))
    while height % rows:
        rows -= 16

    @pl.loop(0, height // rows)
    def _(i):
        at = pl.ds(pl.multiple_of(i * rows, rows), rows)
        into[at, :] = into[at, :] + other[at, :]


def backward_kernel(rows, cols, entries, *refs):
    refs = list(refs)
    take = lambda n: [refs.pop(0) for _ in range(n)]
    number, count = len(entries), 6
    late_terms, whole_in = take(3), take(3)
    q, k, v, stat, token_low, dctx, dz_in, seg_col, seg_row, vec_in = take(10)
    full, (vec_out, grad_tokens) = take(count), take(2)
    acc, c_land, y_land, x_land, z_land, f_land = (take(number) for _ in range(6))
    early_terms, grads = take(3), take(3)
    terms = early_terms + late_terms
    whole, key_sum, value_sum, vec, v_acc, v_pair, v_cols = take(7)
    (load_sem, c_in, y_in, x_in, z_in, f_in, g_in, vp_in, vc_in,
     c_out, y_out, x_out, z_out, f_out, g_out, vp_out, vc_out, whole_sem, dz_sem) = refs
    row, col, dp, core, side = place()
    group_barrier(rows, cols)
    sends = Sends()
    other = 1 - row
    x_dev, y_dev, c_dev = {"row": other}, y_peer(dp), core_peer(dp)

    def band(e, of_row, of_core):
        m, paired, base, part = entries[e]
        height = terms[m].shape[0] // rows
        size = 2 * part if paired else part
        start = of_row * height + base + of_core * size
        return terms[m].at[pl.ds(pl.multiple_of(start, 16), size), :]

    def load(e):
        return [pltpu.make_async_copy(band(e, r, core), acc[e].at[r], load_sem.at[e, r]) for r in range(rows)]

    def begin(e):
        for r in range(rows):
            sends.start(None, band(e, r, 1 - core), c_land[e].at[r], c_out.at[e, r], c_in.at[e, r], c_dev)
        for copy in load(e):
            copy.start()

    early = [e for e in range(number) if entries[e][0] >= 3]
    for e in early:
        begin(e)
    dz_copy = pltpu.make_async_copy(dz_in, grad_tokens, dz_sem)
    dz_copy.start()

    def fetch(m):
        return pltpu.make_async_copy(whole_in[m], whole, whole_sem)

    fetch(0).start()
    token_count = token_low.shape[0]
    f32 = jnp.float32

    def attend_back(pair, half):
        lanes = slice(pair * 128, pair * 128 + 128)
        lane = lax.broadcasted_iota(jnp.int32, (1, 128), 1)
        place_of = lax.broadcasted_iota(jnp.int32, (128, 128), 1)
        if half == 0:
            key_sum[...] = jnp.zeros_like(key_sum)
            value_sum[...] = jnp.zeros_like(value_sum)

        @pl.loop(half * 2, half * 2 + 2)
        def _(i):
            at = pl.ds(pl.multiple_of(i * 128, 128), 128)
            same = seg_col[at, :] == seg_row[...]
            parts = []
            for a in range(2):
                mine_only = (lane < 64) == (a == 0)
                query = q[at, lanes] * jnp.where(mine_only, DH ** (-0.5), 0.0).astype(low_type)
                grad = dctx[at, lanes] * jnp.where(mine_only, 1.0, 0.0).astype(low_type)
                total = jnp.sum(jnp.where(place_of == 2 * pair + a, stat[at, :], 0.0), axis=1, keepdims=True)
                scores = lax.dot_general(query, k[:, lanes], (((1,), (1,)), ((), ())), preferred_element_type=f32)
                attend = jnp.exp(jnp.where(same, scores, neg_fill) - total)
                attend_grad = lax.dot_general(grad, v[:, lanes], (((1,), (1,)), ((), ())), preferred_element_type=f32)
                mean = jnp.sum(attend * attend_grad, axis=1, keepdims=True)
                score_low = (attend * (attend_grad - mean)).astype(low_type)
                value_sum[...] += lax.dot_general(attend.astype(low_type), grad, (((0,), (0,)), ((), ())), preferred_element_type=f32)
                key_sum[...] += lax.dot_general(score_low, query, (((0,), (0,)), ((), ())), preferred_element_type=f32)
                parts.append(jnp.dot(score_low, k[:, lanes], preferred_element_type=f32))
            grads[0][at, lanes] = (jnp.where(lane < 64, parts[0], parts[1]) * DH ** (-0.5)).astype(low_type)
        if half == 1:
            grads[1][:, lanes] = key_sum[...].astype(low_type)
            grads[2][:, lanes] = value_sum[...].astype(low_type)

    def finish_matrix(m):
        if m == 0:
            dz_copy.wait()
        fetch(m).wait()

        @pl.loop(0, terms[m].shape[0] // 256)
        def _(i):
            at = pl.ds(pl.multiple_of(i * 256, 256), 256)
            terms[m][at, :] = lax.dot_general(token_low[:, at], grads[m][...], (((0,), (0,)), ((), ())),
                                              preferred_element_type=f32).astype(low_type)

        for e in range(number):
            if entries[e][0] == m:
                begin(e)

        @pl.loop(0, 4)
        def _(j):
            to = pl.ds(pl.multiple_of(j * 256, 256), 256)
            grad_tokens[:, to] += lax.dot_general(grads[m][...], whole[to, :], (((1,), (1,)), ((), ())),
                                                  preferred_element_type=f32)

        if m < 2:
            fetch(m + 1).start()

    def fill_vectors():
        vec[...] = vec_in[...]
        for start, m in ((0, 0), (8, 2)):
            total = jnp.zeros((8, grads[m].shape[1]), f32)
            for i in range(token_count // 128):
                total += grads[m][i * 128 : i * 128 + 128, :].astype(f32).reshape(16, 8, -1).sum(axis=0)
            total = jnp.sum(total, axis=0, keepdims=True)
            for r in range(8):
                vec[start + r : start + r + 1, :] = total[:, r * 128 : r * 128 + 128]

    def mine(e, r, of_side):
        _, paired, _, part = entries[e]
        if paired:
            return acc[e].at[r, pl.ds(pl.multiple_of(of_side * part, 16), part), :]
        return acc[e].at[r]

    def columns(ref, e, at):
        width = terms[entries[e][0]].shape[1] // cols
        return ref.at[:, pl.ds(pl.multiple_of(at * width, width), width)]

    def send_x(e):
        sends.start(None, mine(e, other, side), x_land[e], x_out.at[e], x_in.at[e], x_dev)

    def core_stage(e):
        for copy in load(e):
            copy.wait()
        for r in range(rows):
            wait_arrival(c_land[e].at[r], c_in.at[e, r], c_dev)
        if entries[e][1]:
            for r in range(rows):
                add_into(mine(e, r, 1 - side), y_view(e, r))
                sends.start(None, mine(e, r, 1 - side), y_land[e].at[r], y_out.at[e, r], y_in.at[e, r], y_dev)
            for r in range(rows):
                add_into(mine(e, r, side), y_view(e, r, side))
        else:
            add_into(acc[e].at[other], c_land[e].at[other])
            send_x(e)
            add_into(acc[e].at[row], c_land[e].at[row])

    def y_view(e, r, of_side=None):
        part = entries[e][3]
        at = 1 - side if of_side is None else of_side
        return c_land[e].at[r, pl.ds(pl.multiple_of(at * part, 16), part), :]

    def y_stage(e):
        if not entries[e][1]:
            return
        for r in (other, row):
            wait_arrival(y_land[e].at[r], y_in.at[e, r], y_dev)
            add_into(mine(e, r, side), y_land[e].at[r])
            if r is other:
                send_x(e)

    def x_stage(e):
        wait_arrival(x_land[e], x_in.at[e], x_dev)
        add_into(mine(e, row, side), x_land[e])
        for step in range(1, cols):
            for way, ok, to in ((0, col + step < cols, jnp.minimum(col + step, cols - 1)),
                                (1, col >= step, jnp.maximum(col - step, 0))):
                sends.start(ok, columns(mine(e, row, side), e, to), z_land[e].at[col],
                            z_out.at[e, step, way], z_in.at[e, col], {"col": to})

    def out_rows(e, of_core, of_side):
        m, paired, base, part = entries[e]
        start = base + ((of_core * 2 + of_side) * part if paired else of_core * part)
        return full[m].at[pl.ds(pl.multiple_of(start, 16), part), :]

    def z_stage(e):
        total = columns(mine(e, row, side), e, col)
        for step in range(1, cols):
            for ok, at in ((col + step < cols, jnp.minimum(col + step, cols - 1)),
                           (col >= step, jnp.maximum(col - step, 0))):
                @pl.when(ok)
                def _():
                    wait_arrival(z_land[e].at[at], z_in.at[e, at], {"col": at})
                    add_into(total, z_land[e].at[at])
        if entries[e][1]:
            sends.start(None, total, out_rows(e, core, side), f_out.at[e], f_in.at[e], y_dev)
            sends.start(None, total, out_rows(e, core, side), g_out.at[e, 0], g_in.at[e, 0], c_dev)
            out_rows(e, core, side)[...] = total[...]
        else:
            sends.start(None, total, f_land[e], f_out.at[e], f_in.at[e], y_dev)

    def final_stage(e):
        m = entries[e][0]
        if entries[e][1]:
            piece = out_rows(e, core, 1 - side)
            wait_arrival(piece, f_in.at[e], y_dev)
            sends.start(None, piece, piece, g_out.at[e, 1], g_in.at[e, 1], c_dev)
        else:
            total = columns(mine(e, row, side), e, col)
            wait_arrival(f_land[e], f_in.at[e], y_dev)
            piece = out_rows(e, core, side)
            piece[...] = total[...] + f_land[e][...]
            sends.start(None, piece, piece, g_out.at[e, 0], g_in.at[e, 0], c_dev)

    def out_stage(e):
        m = entries[e][0]
        wait_arrival(out_rows(e, 1 - core, side), g_in.at[e, 0], c_dev)
        if entries[e][1]:
            wait_arrival(out_rows(e, 1 - core, 1 - side), g_in.at[e, 1], c_dev)

    v_rows = v_acc.shape[1]
    merge = lambda a, b: jnp.concatenate([a[: v_rows - 8] + b[: v_rows - 8], jnp.maximum(a[v_rows - 8 :], b[v_rows - 8 :])])
    v_devs = (c_dev, y_dev, x_dev)

    def vec_send(k):
        src = vec if k == 0 else v_acc.at[k - 1]
        sends.start(None, src, v_pair.at[k], vp_out.at[k], vp_in.at[k], v_devs[k])

    def vec_merge(k):
        wait_arrival(v_pair.at[k], vp_in.at[k], v_devs[k])
        before = vec[...] if k == 0 else v_acc_load(k - 1)
        v_acc.at[k][...] = merge(before, v_pair[k])

    def v_acc_load(k):
        return v_acc[k]

    def vec_cols():
        for step in range(1, cols):
            to = (col + step) % cols
            sends.start(None, v_acc.at[2], v_cols.at[col], vc_out.at[step], vc_in.at[col], {"col": to})
        v_cols[pl.ds(col, 1)] = v_acc[2][None]

    def vec_last():
        for step in range(1, cols):
            at = (col + step) % cols
            wait_arrival(v_cols.at[at], vc_in.at[at], {"col": at})
        total = v_cols[0]
        for k in range(1, cols):
            total = merge(total, v_cols[k])
        vec_out[...] = total

    steps = [lambda: vec_send(0), lambda: (vec_merge(0), vec_send(1)), lambda: (vec_merge(1), vec_send(2)),
             lambda: (vec_merge(2), vec_cols()), vec_last]
    stages = (core_stage, y_stage, x_stage, z_stage, final_stage, out_stage)
    work = [lambda pair=pair, half=half: attend_back(pair, half) for pair in range(H // 2) for half in range(2)]
    work += [lambda m=m: finish_matrix(m) for m in range(3)] + [fill_vectors]
    for tick in range(number + RL[5]):
        for lag, stage in zip(RL, stages):
            if 0 <= tick - lag < number:
                if stage is core_stage and tick >= len(early):
                    while work:
                        work.pop(0)()
                stage(tick - lag)
                if work:
                    work.pop(0)()
        if 0 <= tick - len(early) < len(steps):
            steps[tick - len(early)]()
    sends.finish()


def backward_all(late_terms, wholes, found, seg):
    rows, cols = lax.axis_size("row"), lax.axis_size("col")
    q, k, v, stat, token_low, dctx, dz, vec = found
    shapes = [w.shape for w in wholes] + [t.shape for t in late_terms]
    count = len(shapes)
    heights = [s[0] // rows for s in shapes]
    widths = [s[1] for s in shapes]
    entries = reduce_entries(heights, (5, 4, 3, 0, 1, 2))
    number = len(entries)
    sizes = [(2 * part if paired else part, part, widths[m]) for m, paired, _, part in entries]
    vm, dma, f32 = pltpu.VMEM, pltpu.SemaphoreType.DMA, jnp.float32
    scratch = (
        [vm((rows, band, width), low_type) for band, _, width in sizes]
        + [vm((rows, band, width), low_type) for band, _, width in sizes]
        + [vm((rows, part, width) if entries[e][1] else (rows, 16, 128), low_type) for e, (_, part, width) in enumerate(sizes)]
        + [vm((part, width), low_type) for _, part, width in sizes]
        + [vm((cols, part, width // cols), low_type) for _, part, width in sizes]
        + [vm((part, width // cols), low_type) for _, part, width in sizes]
        + [vm(w.shape, low_type) for w in wholes] + [vm(q.shape, low_type) for _ in range(3)]
        + [vm(wholes[0].shape, low_type), vm((q.shape[0], 128), f32), vm((q.shape[0], 128), f32), vm(vec.shape, f32)]
        + [vm((3, *vec.shape), f32), vm((3, *vec.shape), f32), vm((cols, *vec.shape), f32)]
        + [dma((number, rows)), dma((number, rows)), dma((number, rows)), dma((number,)), dma((number, cols)),
           dma((number,)), dma((number, 2)), dma((3,)), dma((cols,)),
           dma((number, rows)), dma((number, rows)), dma((number,)), dma((number, cols, 2)),
           dma((number,)), dma((number, 2)), dma((3,)), dma((cols,)), dma, dma]
    )
    blocks = [jax.ShapeDtypeStruct((heights[m], widths[m] // cols), low_type) for m in range(count)]
    anywhere, in_vmem = pl.BlockSpec(memory_space=pl.ANY), pl.BlockSpec(memory_space=pltpu.VMEM)
    found = pl.pallas_call(
        functools.partial(backward_kernel, rows, cols, entries),
        out_shape=(*blocks, jax.ShapeDtypeStruct(vec.shape, f32), jax.ShapeDtypeStruct(dz.shape, f32)),
        in_specs=[anywhere] * 6 + [in_vmem] * 6 + [anywhere] + [in_vmem] * 3,
        out_specs=[in_vmem] * 8,
        scratch_shapes=scratch,
        compiler_params=pltpu.CompilerParams(collective_id=1, has_side_effects=True, vmem_limit_bytes=65400 * 1024),
        name="backward_all",
    )(*late_terms, *wholes, q, k, v, stat, token_low, dctx, dz, seg.reshape(-1, 1), seg.reshape(1, -1), vec)
    return found[:6], found[6], found[7]


def pad_rows(vector):
    short = -vector.shape[0] % 128
    return jnp.pad(vector, (0, short)).reshape(-1, 128)


def on_device(tokens, segment_ids, cotangent, weight_query, weight_key, weight_value, weight_output, weight_inner,
              weight_outer, bias_query, bias_value, bias_output, bias_inner, bias_outer, gain_attn, shift_attn,
              gain_block, shift_block, tau_num, tau_den):
    rows, cols = lax.axis_size("row"), lax.axis_size("col")
    groups = rows * cols
    matrices = (weight_query, weight_key, weight_value, weight_output, weight_inner, weight_outer)
    vectors = (bias_query, bias_value, bias_output, bias_inner, bias_outer, gain_attn, shift_attn, gain_block, shift_block)
    lengths = [v.shape[0] for v in vectors]
    spread = [n * groups for n in lengths]
    flat = jnp.concatenate([pad_rows(v) for v in vectors]).astype(low_type)
    flat = jnp.pad(flat, ((0, -flat.shape[0] % 16), (0, 0)))
    wholes, late_terms, found = forward_all(matrices, flat, lengths, tokens, cotangent, segment_ids)
    q, k, v, stat, token_low, dctx, output, dz, vec_terms = found
    low_blocks, vec_total, grad_tokens = backward_all(
        late_terms, wholes, (q, k, v, stat, token_low, dctx, dz, vec_terms), segment_ids)
    block_grads, vec_total = sum_groups([b.astype(jnp.float32) for b in low_blocks], vec_total)

    at = lax.axis_index("row") * cols + lax.axis_index("col")
    owned, start = [], 0
    for n, whole_n in zip(lengths, spread):
        vector = vec_total[start : start + whole_n // 128].reshape(-1)
        owned.append(lax.dynamic_slice(vector, (at * n,), (n,)))
        start += whole_n // 128
    head_peak = vec_total[start, :H]
    tau_value = tau_num[0].astype(jnp.float32) / tau_den[0].astype(jnp.float32)
    factor = jnp.sqrt(tau_value / jnp.maximum(head_peak, tau_value))
    col_width = weight_query.shape[1]
    col_heads = (lax.axis_index("col") * col_width + jnp.arange(col_width, dtype=jnp.int32)) // DH
    column_factor = jnp.sum(
        jnp.where(col_heads[:, None] == jnp.arange(H, dtype=jnp.int32)[None, :], factor[None, :], 0.0), axis=1)
    return (output, grad_tokens, *block_grads, *owned, head_peak,
            weight_query * column_factor[None, :], weight_key * column_factor[None, :])


def sum_groups(blocks, vec):
    count = lax.axis_size("dp")
    totals, vec_sum = list(blocks), vec
    split = vec.shape[0] - 8
    for step in range(4, count, 4):
        shift = [(i, (i + step) % count) for i in range(count)]
        totals = [t + lax.ppermute(b, "dp", shift) for t, b in zip(totals, blocks)]
        moved = lax.ppermute(vec, "dp", shift)
        vec_sum = jnp.concatenate([vec_sum[:split] + moved[:split], jnp.maximum(vec_sum[split:], moved[split:])])
    return totals, vec_sum


def solution(mesh):
    tokens_spec, block_spec, vector_spec = P(("dp", "row", "col"), None), P("row", "col"), P(("row", "col"))
    in_specs = (tokens_spec, P(("dp", "row", "col")), tokens_spec, *(block_spec,) * 6, *(vector_spec,) * 9, P(), P())
    out_specs = (tokens_spec, tokens_spec, *(block_spec,) * 6, *(vector_spec,) * 9, P(), block_spec, block_spec)
    return jax.shard_map(on_device, mesh=mesh, in_specs=in_specs, out_specs=out_specs, check_vma=False)
```

```python
import functools
import jax
import jax.numpy as jnp
from jax import lax
from jax.experimental import pallas as pl
from jax.experimental.pallas import tpu as pltpu
from jax.sharding import PartitionSpec as P

MESH = pl.DeviceIdType.MESH

LAGS = (0, 2, 5)
SEQ, H, DH = 512, 16, 64
norm_eps = 1e-12
neg_fill = -1e30
low_type = jnp.bfloat16

def place():
    dp = lax.axis_index("dp")
    return lax.axis_index("row"), lax.axis_index("col"), dp, dp % 2, (dp // 2) % 2


def core_peer(dp):
    return {"dp": dp + 1 - 2 * (dp % 2)}


def y_peer(dp):
    side = (dp // 2) % 2
    return {"dp": dp + 2 - 4 * side}


class Sends:
    def __init__(self):
        self.items = []

    def start(self, when, src, dst, send_sem, recv_sem, device):
        copy = pltpu.make_async_remote_copy(
            src_ref=src, dst_ref=dst, send_sem=send_sem, recv_sem=recv_sem,
            device_id=device, device_id_type=MESH,
        )
        self.items.append((when, copy))
        if when is None:
            copy.start()
        else:
            pl.when(when)(copy.start)

    def finish(self):
        for when, copy in self.items:
            if when is None:
                copy.wait_send()
            else:
                pl.when(when)(copy.wait_send)


def wait_arrival(dst, recv_sem, device):
    pltpu.make_async_remote_copy(
        src_ref=dst, dst_ref=dst, send_sem=recv_sem, recv_sem=recv_sem,
        device_id=device, device_id_type=MESH,
    ).wait_recv()


def group_barrier(rows, cols):
    row, col, dp, _, _ = place()
    barrier = pltpu.get_barrier_semaphore()
    peers = [core_peer(dp), y_peer(dp)]
    mine = row * cols + col
    for step in range(1, rows * cols):
        other = (mine + step) % (rows * cols)
        peers.append({"row": other // cols, "col": other % cols})
    for peer in peers:
        pl.semaphore_signal(barrier, inc=1, device_id=peer, device_id_type=MESH)
    pl.semaphore_wait(barrier, len(peers))


def entries_of(heights):
    found = []
    for m, height in enumerate(heights):
        found.append((m, True, 0, height * 3 // 16))
        found.append((m, False, height * 3 // 4, height // 8))
    return found


def assemble_vectors(vecs, full_vec, lengths):
    groups = vecs.shape[0]
    for d in range(groups):
        rows_of = vecs[d].astype(jnp.float32)
        at = 0
        for i, n in enumerate(lengths):
            for part in range(-(-n // 128)):
                width = min(128, n - part * 128)
                start = d * n + part * 128
                full_vec[i : i + 1, start : start + width] = rows_of[at : at + 1, :width]
                at += 1


def row_stats(values):
    center = values - jnp.mean(values, axis=-1, keepdims=True)
    spread = jnp.mean(center * center, axis=-1, keepdims=True)
    scale = lax.rsqrt(spread + norm_eps)
    return center * scale, scale


def put_vector(ref, start, total):
    for r in range(total.shape[1] // 128):
        ref[start + r : start + r + 1, :] = total[:, r * 128 : r * 128 + 128]


def fold_rows(values):
    return values.reshape(values.shape[0] // 8, 8, values.shape[1]).sum(axis=0)


def product_term(into, left, rights, staged, stage_sem):
    tiles = left.shape[1] // 256

    def send(slot, r, c):
        rows = pl.ds(pl.multiple_of(r * 256, 256), 256)
        return pltpu.make_async_copy(staged[slot], into.at[rows, c * 1024 : c * 1024 + 1024], stage_sem.at[slot])

    for c, right in enumerate(rights):
        @pl.loop(0, tiles // 2)
        def _(i):
            for slot in range(2):
                r = i * 2 + slot
                if c == 0:
                    pl.when(i > 0)(lambda: send(slot, r, c).wait())
                else:
                    send(slot, r, c).wait()
                staged[slot][...] = lax.dot_general(left[:, pl.ds(pl.multiple_of(r * 256, 256), 256)], right[...],
                                               (((0,), (0,)), ((), ())), preferred_element_type=jnp.float32).astype(low_type)
                send(slot, r, c).start()
    for slot in range(2):
        send(slot, 0, 0).wait()


def forward_kernel(rows, cols, entries, lengths, ahead, *refs):
    refs = list(refs)
    take = lambda n: [refs.pop(0) for _ in range(n)]
    blocks = take(6)
    vec, tokens, cotangent, seg_col, seg_row = take(5)
    wholes_out, outer_term = take(6), take(1)[0]
    (q, k, v, stat, token_low, ctx, h1r, low_grad, gp, n1, gain, output, dz, vec_terms) = take(14)
    wholes = take(6)
    (vecs, full_vec, peak, g, sums, staged) = take(6)
    (stage_sem, z_in, x_in, y_in, c_in, v_in, z_out, x_out, y_out, c_out, v_out, out_sem, own_vec) = refs
    count, number = 6, len(entries)
    row, col, dp, core, side = place()
    other = 1 - row
    mine = row * cols + col
    x_dev, y_dev, c_dev = {"row": other}, y_peer(dp), core_peer(dp)
    sends = Sends()

    for m in range(count):
        height, width = blocks[m].shape
        step = 32768 // width
        to_col = pl.ds(pl.multiple_of(col * width, width), width)

        @pl.loop(0, height // step)
        def _(i):
            wholes[m][pl.ds(pl.multiple_of(row * height + i * step, step), step), to_col] = (
                blocks[m][pl.ds(pl.multiple_of(i * step, step), step), :].astype(low_type))

    group_barrier(rows, cols)
    for step in range(1, rows * cols):
        peer = (mine + step) % (rows * cols)
        sends.start(None, vec, vecs.at[mine], v_out.at[step], v_in.at[mine], {"row": peer // cols, "col": peer % cols})

    def region(e, of_row, of_col, of_core, of_side):
        m, paired, base, part = entries[e]
        height, width = blocks[m].shape
        start = of_row * height + base + ((of_core * 2 + of_side) * part if paired else of_core * part)
        return wholes[m].at[pl.ds(pl.multiple_of(start, 16), part), pl.ds(pl.multiple_of(of_col * width, width), width)]

    def send_own(e):
        piece = region(e, row, col, core, side)
        for step in range(1, cols):
            sends.start(col + step < cols, piece, piece, z_out.at[e, step, 0], z_in.at[e, col], {"col": jnp.minimum(col + step, cols - 1)})
            sends.start(col >= step, piece, piece, z_out.at[e, step, 1], z_in.at[e, col], {"col": jnp.maximum(col - step, 0)})
            if step == 1:
                sends.start(None, piece, piece, x_out.at[e, col], x_in.at[e, col], x_dev)

    def share(e, of_row, of_col, when):
        piece = region(e, of_row, of_col, core, side)
        if entries[e][1]:
            sends.start(when, piece, piece, y_out.at[e, of_row, of_col], y_in.at[e, of_row, of_col], y_dev)
        sends.start(when, piece, piece, c_out.at[e, of_row, of_col, 0], c_in.at[e, of_row, of_col, 0], c_dev)

    def columns(step):
        if step == 0:
            return [(None, col)]
        return [(col >= step, jnp.maximum(col - step, 0)), (col + step < cols, jnp.minimum(col + step, cols - 1))]

    def guarded(when, body):
        if when is None:
            body()
        else:
            pl.when(when)(body)

    def z_stage(e, step):
        if step == 0:
            if e + ahead < number:
                send_own(e + ahead)
            return
        for when, at in columns(step):
            piece = region(e, row, at, core, side)
            guarded(when, lambda: wait_arrival(piece, z_in.at[e, at], {"col": col}))
            sends.start(when, piece, piece, x_out.at[e, at], x_in.at[e, at], x_dev)
            share(e, row, at, when)

    def x_stage(e, step):
        for when, at in columns(step):
            piece = region(e, other, at, core, side)
            guarded(when, lambda: wait_arrival(piece, x_in.at[e, at], x_dev))
            share(e, other, at, when)

    def y_stage(e, step):
        if not entries[e][1]:
            return
        for when, at in columns(step):
            for of_row in (row, other):
                if step == 0 and of_row is row:
                    continue
                piece = region(e, of_row, at, core, 1 - side)
                guarded(when, lambda: wait_arrival(piece, y_in.at[e, of_row, at], y_dev))
                sends.start(when, piece, piece, c_out.at[e, of_row, at, 1], c_in.at[e, of_row, at, 1], c_dev)

    def c_stage(e, step):
        for when, at in columns(step):
            for of_row in (row, other):
                if step == 0 and of_row is row:
                    continue
                piece = region(e, of_row, at, 1 - core, side)
                guarded(when, lambda: wait_arrival(piece, c_in.at[e, of_row, at, 0], c_dev))
                if entries[e][1]:
                    far = region(e, of_row, at, 1 - core, 1 - side)
                    guarded(when, lambda: wait_arrival(far, c_in.at[e, of_row, at, 1], c_dev))

    def keep(m):
        return pltpu.make_async_copy(wholes[m], wholes_out[m], out_sem.at[m])

    def complete(m):
        for e in range(number):
            if entries[e][0] == m:
                for step in range(cols):
                    c_stage(e, step)
        keep(m).start()

    tokens_count = tokens.shape[0]

    def cast_tokens():
        @pl.loop(0, tokens_count // 64)
        def _(i):
            at = pl.ds(pl.multiple_of(i * 64, 64), 64)
            token_low[at, :] = tokens[at, :].astype(low_type)

    def finish_vectors():
        for step in range(1, rows * cols):
            peer = (mine + step) % (rows * cols)
            wait_arrival(vecs.at[peer], v_in.at[peer], {"row": peer // cols, "col": peer % cols})
        keep_vec.wait()
        assemble_vectors(vecs, full_vec, lengths)

    def project(m, into, bias):
        @pl.loop(0, into.shape[1] // 256)
        def _(j):
            at = pl.ds(pl.multiple_of(j * 256, 256), 256)
            total = jnp.dot(token_low[...], wholes[m][:, at], preferred_element_type=jnp.float32)
            if bias is not None:
                total = total + full_vec[bias : bias + 1, at]
            into[:, at] = total.astype(low_type)

    def start_attention():
        stat[...] = jnp.zeros_like(stat)
        peak[...] = jnp.full(peak.shape, neg_fill, jnp.float32)

    def attend(pair, half):
        lanes = slice(pair * 128, pair * 128 + 128)
        lane = lax.broadcasted_iota(jnp.int32, (1, 128), 1)
        place_of = lax.broadcasted_iota(jnp.int32, (128, 128), 1)
        peak_place = lax.broadcasted_iota(jnp.int32, peak.shape, 1)

        @pl.loop(half * 2, half * 2 + 2)
        def _(i):
            at = pl.ds(pl.multiple_of(i * 128, 128), 128)
            same = seg_col[at, :] == seg_row[...]
            parts = []
            for a in range(2):
                head = 2 * pair + a
                keep_lanes = jnp.where((lane < 64) == (a == 0), DH ** (-0.5), 0.0).astype(low_type)
                scores = lax.dot_general(q[at, lanes] * keep_lanes, k[:, lanes], (((1,), (1,)), ((), ())),
                                         preferred_element_type=jnp.float32)
                scores = jnp.where(same, scores, neg_fill)
                top = jnp.max(scores, axis=1, keepdims=True)
                raised = jnp.exp(scores - top)
                total = jnp.sum(raised, axis=1, keepdims=True)
                attend_low = (raised * (1.0 / total)).astype(low_type)
                parts.append(jnp.dot(attend_low, v[:, lanes], preferred_element_type=jnp.float32))
                stat[at, :] = jnp.where(place_of == head, top + jnp.log(total), stat[at, :])
                peak[...] = jnp.where(peak_place == head, jnp.maximum(peak[...], jnp.max(top, axis=0, keepdims=True)), peak[...])
            ctx[at, lanes] = jnp.where(lane < 64, parts[0], parts[1]).astype(low_type)

    def first_norm(i):
        at = slice(i * 256, i * 256 + 256)
        place_of = lax.broadcasted_iota(jnp.int32, (256, 128), 1)

        @pl.loop(0, 4)
        def _(j):
            to = pl.ds(pl.multiple_of(j * 256, 256), 256)
            n1[at, to] = (tokens[at, to] + jnp.dot(ctx[at, :], wholes[3][:, to], preferred_element_type=jnp.float32)
                          + full_vec[2:3, to])

        @pl.loop(0, 8)
        def _(j):
            some = pl.ds(pl.multiple_of(i * 256 + j * 32, 32), 32)
            normal, scale = row_stats(n1[some, :])
            n1[some, :] = normal
            h1r[some, :] = (normal * full_vec[5:6, :1024] + full_vec[6:7, :1024]).astype(low_type)
            stat[some, :] = jnp.where(place_of[:32] == H, scale, stat[some, :])

    def hidden(lo, hi):
        @pl.loop(lo, hi)
        def _(j):
            at = pl.ds(pl.multiple_of(j * 256, 256), 256)
            u = jnp.dot(h1r[...], wholes[4][:, at], preferred_element_type=jnp.float32) + full_vec[3:4, at]
            below = 0.5 + 0.5 * lax.erf(u * 0.7071067811865476)
            g[:, at] = (u * below).astype(low_type)
            gp[:, at] = (below + u * (0.3989422804014327 * jnp.exp(-0.5 * u * u))).astype(low_type)

    def outer_product(step):
        here = slice(step * 1024, step * 1024 + 1024)

        @pl.loop(0, 4)
        def _(j):
            to = pl.ds(pl.multiple_of(j * 256, 256), 256)
            term = jnp.dot(g[:, here], wholes[5][here, to], preferred_element_type=jnp.float32)
            if step == 0:
                output[:, to] = term + (n1[:, to] * full_vec[5:6, to] + full_vec[6:7, to]) + full_vec[4:5, to]
            else:
                output[:, to] += term

    def second_norm():
        sums[...] = jnp.zeros_like(sums)

        @pl.loop(0, tokens_count // 32)
        def _(i):
            at = pl.ds(pl.multiple_of(i * 32, 32), 32)
            normal, scale = row_stats(output[at, :])
            grad = cotangent[at, :]
            scaled = grad * full_vec[7:8, :1024]
            gradient = (scaled - jnp.mean(scaled, axis=-1, keepdims=True)
                        - normal * jnp.mean(scaled * normal, axis=-1, keepdims=True)) * scale
            output[at, :] = normal * full_vec[7:8, :1024] + full_vec[8:9, :1024]
            dz[at, :] = gradient
            low = gradient.astype(low_type)
            low_grad[at, :] = low
            add_sums((low.astype(jnp.float32), grad * normal, grad), (0, 1, 2))

    def add_sums(parts, places):
        for part, r in zip(parts, places):
            sums[r * 8 : r * 8 + 8, :] += part.reshape(part.shape[0] // 8, 8, part.shape[1]).sum(axis=0)

    def collect_sums():
        vec_terms[...] = jnp.zeros_like(vec_terms)
        last_rows = vec_terms.shape[0] - 8
        for r, start in ((0, last_rows - 40), (1, last_rows - 16), (2, last_rows - 8)):
            put_vector(vec_terms, start, jnp.sum(sums[r * 8 : r * 8 + 8, :], axis=0, keepdims=True))
        vec_terms[last_rows:, :] = peak[...]
        gain[...] = jnp.broadcast_to(full_vec[5:6, : gain.shape[1]], gain.shape)

    for e in range(ahead):
        send_own(e)
    keep_vec = pltpu.make_async_copy(vec, vecs.at[mine], own_vec)
    keep_vec.start()
    items = [(e, step) for e in range(number) for step in range(cols)]
    last = len(items) + LAGS[2]

    def ready(m):
        return min((2 * m + 2) * cols + LAGS[2] + 2, last)

    work = [(2, cast_tokens), (4, finish_vectors)]
    for m, into, bias in ((0, q, 0), (1, k, None), (2, v, 1)):
        work.append((ready(m), lambda m=m, into=into, bias=bias: (complete(m), project(m, into, bias))))
    work.append((ready(2), start_attention))
    work += [(ready(2) + 1 + (2 * pair + half) * cols // 4, lambda pair=pair, half=half: attend(pair, half))
             for pair in range(H // 2) for half in range(2)]
    work += [(ready(3), lambda: complete(3)), (ready(3), lambda: first_norm(0)), (ready(3), lambda: first_norm(1))]
    work.append((ready(4), lambda: complete(4)))
    work += [(ready(4) + lo // 2, lambda lo=lo: hidden(lo, lo + 2)) for lo in range(0, 16, 2)]
    work += [(ready(5), lambda: complete(5))] + [(ready(5), lambda s=s: outer_product(s)) for s in range(4)]
    end = ready(5)
    work += [(end, second_norm), (end, lambda: product_term(outer_term, g, [low_grad], [staged.at[0], staged.at[1]], stage_sem)), (end, collect_sums)]

    for tick in range(last + 1):
        for lag, stage in zip(LAGS[:3], (z_stage, x_stage, y_stage)):
            if 0 <= tick - lag < len(items):
                stage(*items[tick - lag])
        while work and (work[0][0] <= tick or tick == last):
            work.pop(0)[1]()
    for m in range(count):
        keep(m).wait()
    sends.finish()


def forward_all(blocks, vec, lengths, tokens, cotangent, seg, ahead=3):
    rows, cols = lax.axis_size("row"), lax.axis_size("col")
    wholes = [jax.ShapeDtypeStruct((b.shape[0] * rows, b.shape[1] * cols), low_type) for b in blocks]
    entries = entries_of([b.shape[0] for b in blocks])
    number = len(entries)
    dma, vm, count = pltpu.SemaphoreType.DMA, pltpu.VMEM, tokens.shape[0]
    width, hidden = wholes[4].shape
    shape = jax.ShapeDtypeStruct
    f32 = jnp.float32
    results = [*[shape((count, width), low_type)] * 3, shape((count, 128), f32), *[shape((count, width), low_type)] * 4,
               shape((count, hidden), low_type), shape((count, width), f32), shape((8, width), f32),
               *[shape((count, width), f32)] * 2, shape(((width * 8 + hidden) // 128 + 8, 128), f32)]
    in_vmem = pl.BlockSpec(memory_space=pltpu.VMEM)
    found = pl.pallas_call(
        functools.partial(forward_kernel, rows, cols, entries, lengths, ahead),
        out_shape=(*wholes, wholes[5], *results),
        in_specs=[in_vmem] * 11,
        out_specs=[pl.BlockSpec(memory_space=pl.ANY)] * 7 + [in_vmem] * len(results),
        scratch_shapes=[vm(w.shape, low_type) for w in wholes] + [
            vm((rows * cols, *vec.shape), vec.dtype), vm((16, hidden), f32), vm((8, 128), f32),
            vm((count, hidden), low_type), vm((24, width), f32), vm((2, 256, 1024), low_type), dma((2,)),
            dma((number, cols)), dma((number, cols)), dma((number, rows, cols)), dma((number, rows, cols, 2)), dma((rows * cols,)),
            dma((number, cols, 2)), dma((number, cols)), dma((number, rows, cols)), dma((number, rows, cols, 2)), dma((rows * cols,)),
            dma((6,)), dma,
        ],
        compiler_params=pltpu.CompilerParams(collective_id=0, has_side_effects=True, vmem_limit_bytes=65400 * 1024),
        name="forward_all",
    )(*blocks, vec, tokens, cotangent, seg.reshape(-1, 1), seg.reshape(1, -1))
    return found[:6], found[6], found[7:]


RL = (0, 2, 4, 6, 8, 9)
PARTS = (1, 1, 1, 1, 2, 2)

def reduce_entries(heights, order):
    found = []
    for m in order:
        height = heights[m]
        for i in range(PARTS[m]):
            base, size = i * height // PARTS[m], height // PARTS[m]
            found.append((m, True, base, size // 8))
            found.append((m, False, base + size // 2, size // 4))
    return found


def add_into(into, other):
    height, width = into.shape
    rows = max(16, min(height, 65536 // width // 16 * 16))
    while height % rows:
        rows -= 16

    @pl.loop(0, height // rows)
    def _(i):
        at = pl.ds(pl.multiple_of(i * rows, rows), rows)
        into[at, :] = into[at, :] + other[at, :]


def backward_kernel(rows, cols, entries, *refs):
    refs = list(refs)
    take = lambda n: [refs.pop(0) for _ in range(n)]
    number, count = len(entries), 6
    outer_term, whole_in = take(1)[0], take(6)
    q_in, k_in, v_in, token_in, ctx_in, h1r_in, low_in, gp_in, dz_in = take(9)
    stat, n1, gain, seg_col, seg_row, vec_in = take(6)
    full, (vec_out, grad_tokens), (output_term, inner_term) = take(count), take(2), take(2)
    acc, c_land, y_land, x_land, z_land, f_land = (take(number) for _ in range(6))
    big, quad, grads, dctx, key_sum, value_sum, hidden_sums, sums, vec, v_acc, v_pair, v_cols = take(12)
    (load_sem, c_in, y_in, x_in, z_in, f_in, g_in, vp_in, vc_in,
     c_out, y_out, x_out, z_out, f_out, g_out, vp_out, vc_out, big_sem, quad_sem, grad_sem, dz_sem, stage_sem) = refs
    terms = [big.at[0], big.at[1], big.at[2], output_term, inner_term, outer_term]
    q, k, v, token_low = (quad.at[i] for i in range(4))
    grads = [grads.at[i] for i in range(3)]
    whole = big.at[3]
    staged = [dctx.at[:256, :], dctx.at[256:512, :]]
    begun = set()
    row, col, dp, core, side = place()
    group_barrier(rows, cols)
    sends = Sends()
    other = 1 - row
    x_dev, y_dev, c_dev = {"row": other}, y_peer(dp), core_peer(dp)

    def band(e, of_row, of_core):
        m, paired, base, part = entries[e]
        height = terms[m].shape[0] // rows
        size = 2 * part if paired else part
        start = of_row * height + base + of_core * size
        return terms[m].at[pl.ds(pl.multiple_of(start, 16), size), :]

    def load(e):
        return [pltpu.make_async_copy(band(e, r, core), acc[e].at[r], load_sem.at[e, r]) for r in range(rows)]

    def begin(e):
        for r in range(rows):
            sends.start(None, band(e, r, 1 - core), c_land[e].at[r], c_out.at[e, r], c_in.at[e, r], c_dev)
        for copy in load(e):
            copy.start()

    def begin_matrix(m):
        begun.add(m)
        for e in range(number):
            if entries[e][0] == m:
                begin(e)

    begin_matrix(5)
    dz_copy = pltpu.make_async_copy(dz_in, grad_tokens, dz_sem)
    dz_copy.start()

    def fetch(m):
        return pltpu.make_async_copy(whole_in[m], whole, big_sem.at[3])

    def fetch_block(m, b):
        part = whole_in[m].at[b * 1024 : b * 1024 + 1024, :] if m == 5 else whole_in[m].at[:, b * 1024 : b * 1024 + 1024]
        return pltpu.make_async_copy(part, big.at[b], big_sem.at[b])

    def slope_block(b):
        return pltpu.make_async_copy(gp_in.at[:, b * 1024 : b * 1024 + 1024], quad.at[b], quad_sem.at[b])

    def to_grads(i, ref):
        return pltpu.make_async_copy(ref, grads[i], grad_sem.at[i])

    def to_quad(i):
        return pltpu.make_async_copy((q_in, k_in, v_in, token_in)[i], quad.at[i], quad_sem.at[i])

    to_grads(0, low_in).start()
    for b in range(4):
        fetch_block(5, b).start()
        slope_block(b).start()
    to_grads(1, h1r_in).start()
    to_grads(2, ctx_in).start()
    token_count = dctx.shape[0]
    f32 = jnp.float32

    def hidden_gradient(b):
        if b == 0:
            to_grads(0, low_in).wait()
        fetch_block(5, b).wait()
        slope_block(b).wait()

        @pl.loop(0, 4)
        def _(j):
            at = pl.ds(pl.multiple_of(j * 256, 256), 256)
            act = lax.dot_general(grads[0][...], big[b, at, :], (((1,), (1,)), ((), ())), preferred_element_type=f32)
            low = (act * quad[b, :, at].astype(f32)).astype(low_type)
            quad[b, :, at] = low
            hidden_sums[b, :, at] = fold_rows(low.astype(f32))

        fetch_block(4, b).start()

    def inner_gradient():
        to_grads(1, h1r_in).wait()
        product_term(inner_term, grads[1], [quad.at[b] for b in range(4)], staged, stage_sem)
        begin_matrix(4)

    def back_hidden(b):
        if b == 0:
            dz_copy.wait()
        fetch_block(4, b).wait()

        @pl.loop(0, 4)
        def _(j):
            to = pl.ds(pl.multiple_of(j * 256, 256), 256)
            grad_tokens[:, to] += lax.dot_general(quad[b], big[b, to, :], (((1,), (1,)), ((), ())), preferred_element_type=f32)

        to_quad(b).start()
        if b == 3:
            fetch(3).start()

    def first_norm_back():
        sums[...] = jnp.zeros_like(sums)

        @pl.loop(0, token_count // 32)
        def _(i):
            at = pl.ds(pl.multiple_of(i * 32, 32), 32)
            place_of = lax.broadcasted_iota(jnp.int32, (32, 128), 1)
            scale = jnp.sum(jnp.where(place_of == H, stat[at, :], 0.0), axis=1, keepdims=True)
            grad, normal = grad_tokens[at, :], n1[at, :]
            scaled = grad * gain[0:1, :]
            gradient = (scaled - jnp.mean(scaled, axis=-1, keepdims=True)
                        - normal * jnp.mean(scaled * normal, axis=-1, keepdims=True)) * scale
            grad_tokens[at, :] = gradient
            low = gradient.astype(low_type)
            grads[0][at, :] = low
            for r, part in enumerate((low.astype(f32), grad * normal, grad)):
                sums[r * 8 : r * 8 + 8, :] += fold_rows(part)

    def output_gradient():
        to_grads(2, ctx_in).wait()
        product_term(output_term, grads[2], [grads[0]], staged, stage_sem)
        begin_matrix(3)

    def context_gradient():
        fetch(3).wait()

        @pl.loop(0, 4)
        def _(j):
            to = pl.ds(pl.multiple_of(j * 256, 256), 256)
            dctx[:, to] = lax.dot_general(grads[0][...], whole[to, :], (((1,), (1,)), ((), ())),
                                          preferred_element_type=f32).astype(low_type)

        fetch(0).start()
        for i in range(4):
            to_quad(i).wait()

    def attend_back(pair, half):
        lanes = slice(pair * 128, pair * 128 + 128)
        lane = lax.broadcasted_iota(jnp.int32, (1, 128), 1)
        place_of = lax.broadcasted_iota(jnp.int32, (128, 128), 1)
        if half == 0:
            key_sum[...] = jnp.zeros_like(key_sum)
            value_sum[...] = jnp.zeros_like(value_sum)

        @pl.loop(half * 2, half * 2 + 2)
        def _(i):
            at = pl.ds(pl.multiple_of(i * 128, 128), 128)
            same = seg_col[at, :] == seg_row[...]
            parts = []
            for a in range(2):
                mine_only = (lane < 64) == (a == 0)
                query = q[at, lanes] * jnp.where(mine_only, DH ** (-0.5), 0.0).astype(low_type)
                grad = dctx[at, lanes] * jnp.where(mine_only, 1.0, 0.0).astype(low_type)
                total = jnp.sum(jnp.where(place_of == 2 * pair + a, stat[at, :], 0.0), axis=1, keepdims=True)
                scores = lax.dot_general(query, k[:, lanes], (((1,), (1,)), ((), ())), preferred_element_type=f32)
                attend = jnp.exp(jnp.where(same, scores, neg_fill) - total)
                attend_grad = lax.dot_general(grad, v[:, lanes], (((1,), (1,)), ((), ())), preferred_element_type=f32)
                mean = jnp.sum(attend * attend_grad, axis=1, keepdims=True)
                score_low = (attend * (attend_grad - mean)).astype(low_type)
                value_sum[...] += lax.dot_general(attend.astype(low_type), grad, (((0,), (0,)), ((), ())), preferred_element_type=f32)
                key_sum[...] += lax.dot_general(score_low, query, (((0,), (0,)), ((), ())), preferred_element_type=f32)
                parts.append(jnp.dot(score_low, k[:, lanes], preferred_element_type=f32))
            grads[0][at, lanes] = (jnp.where(lane < 64, parts[0], parts[1]) * DH ** (-0.5)).astype(low_type)
        if half == 1:
            grads[1][:, lanes] = key_sum[...].astype(low_type)
            grads[2][:, lanes] = value_sum[...].astype(low_type)

    def finish_matrix(m):
        fetch(m).wait()

        @pl.loop(0, terms[m].shape[0] // 256)
        def _(i):
            at = pl.ds(pl.multiple_of(i * 256, 256), 256)
            terms[m][at, :] = lax.dot_general(token_low[:, at], grads[m][...], (((0,), (0,)), ((), ())),
                                              preferred_element_type=f32).astype(low_type)

        begin_matrix(m)

        @pl.loop(0, 4)
        def _(j):
            to = pl.ds(pl.multiple_of(j * 256, 256), 256)
            grad_tokens[:, to] += lax.dot_general(grads[m][...], whole[to, :], (((1,), (1,)), ((), ())),
                                                  preferred_element_type=f32)

        if m < 2:
            fetch(m + 1).start()

    def fill_vectors():
        vec[...] = vec_in[...]
        for start, m in ((0, 0), (8, 2)):
            total = jnp.zeros((8, grads[m].shape[1]), f32)
            for i in range(token_count // 128):
                total += fold_rows(grads[m][i * 128 : i * 128 + 128, :].astype(f32))
            put_vector(vec, start, jnp.sum(total, axis=0, keepdims=True))
        for b in range(4):
            put_vector(vec, 24 + 8 * b, jnp.sum(hidden_sums[b], axis=0, keepdims=True))
        for r, start in ((0, 16), (1, 64), (2, 72)):
            put_vector(vec, start, jnp.sum(sums[r * 8 : r * 8 + 8, :], axis=0, keepdims=True))

    def mine(e, r, of_side):
        _, paired, _, part = entries[e]
        if paired:
            return acc[e].at[r, pl.ds(pl.multiple_of(of_side * part, 16), part), :]
        return acc[e].at[r]

    def columns(ref, e, at):
        width = terms[entries[e][0]].shape[1] // cols
        return ref.at[:, pl.ds(pl.multiple_of(at * width, width), width)]

    def send_x(e):
        sends.start(None, mine(e, other, side), x_land[e], x_out.at[e], x_in.at[e], x_dev)

    def core_stage(e):
        for copy in load(e):
            copy.wait()
        for r in range(rows):
            wait_arrival(c_land[e].at[r], c_in.at[e, r], c_dev)
        if entries[e][1]:
            for r in range(rows):
                add_into(mine(e, r, 1 - side), y_view(e, r))
                sends.start(None, mine(e, r, 1 - side), y_land[e].at[r], y_out.at[e, r], y_in.at[e, r], y_dev)
            for r in range(rows):
                add_into(mine(e, r, side), y_view(e, r, side))
        else:
            add_into(acc[e].at[other], c_land[e].at[other])
            send_x(e)
            add_into(acc[e].at[row], c_land[e].at[row])

    def y_view(e, r, of_side=None):
        part = entries[e][3]
        at = 1 - side if of_side is None else of_side
        return c_land[e].at[r, pl.ds(pl.multiple_of(at * part, 16), part), :]

    def y_stage(e):
        if not entries[e][1]:
            return
        for r in (other, row):
            wait_arrival(y_land[e].at[r], y_in.at[e, r], y_dev)
            add_into(mine(e, r, side), y_land[e].at[r])
            if r is other:
                send_x(e)

    def x_stage(e):
        wait_arrival(x_land[e], x_in.at[e], x_dev)
        add_into(mine(e, row, side), x_land[e])
        for step in range(1, cols):
            for way, ok, to in ((0, col + step < cols, jnp.minimum(col + step, cols - 1)),
                                (1, col >= step, jnp.maximum(col - step, 0))):
                sends.start(ok, columns(mine(e, row, side), e, to), z_land[e].at[col],
                            z_out.at[e, step, way], z_in.at[e, col], {"col": to})

    def out_rows(e, of_core, of_side):
        m, paired, base, part = entries[e]
        start = base + ((of_core * 2 + of_side) * part if paired else of_core * part)
        return full[m].at[pl.ds(pl.multiple_of(start, 16), part), :]

    def z_stage(e):
        total = columns(mine(e, row, side), e, col)
        for step in range(1, cols):
            for ok, at in ((col + step < cols, jnp.minimum(col + step, cols - 1)),
                           (col >= step, jnp.maximum(col - step, 0))):
                @pl.when(ok)
                def _():
                    wait_arrival(z_land[e].at[at], z_in.at[e, at], {"col": at})
                    add_into(total, z_land[e].at[at])
        if entries[e][1]:
            sends.start(None, total, out_rows(e, core, side), f_out.at[e], f_in.at[e], y_dev)
            sends.start(None, total, out_rows(e, core, side), g_out.at[e, 0], g_in.at[e, 0], c_dev)
            out_rows(e, core, side)[...] = total[...]
        else:
            sends.start(None, total, f_land[e], f_out.at[e], f_in.at[e], y_dev)

    def final_stage(e):
        m = entries[e][0]
        if entries[e][1]:
            piece = out_rows(e, core, 1 - side)
            wait_arrival(piece, f_in.at[e], y_dev)
            sends.start(None, piece, piece, g_out.at[e, 1], g_in.at[e, 1], c_dev)
        else:
            total = columns(mine(e, row, side), e, col)
            wait_arrival(f_land[e], f_in.at[e], y_dev)
            piece = out_rows(e, core, side)
            piece[...] = total[...] + f_land[e][...]
            sends.start(None, piece, piece, g_out.at[e, 0], g_in.at[e, 0], c_dev)

    def out_stage(e):
        m = entries[e][0]
        wait_arrival(out_rows(e, 1 - core, side), g_in.at[e, 0], c_dev)
        if entries[e][1]:
            wait_arrival(out_rows(e, 1 - core, 1 - side), g_in.at[e, 1], c_dev)

    v_rows = v_acc.shape[1]
    merge = lambda a, b: jnp.concatenate([a[: v_rows - 8] + b[: v_rows - 8], jnp.maximum(a[v_rows - 8 :], b[v_rows - 8 :])])
    v_devs = (c_dev, y_dev, x_dev)

    def vec_send(k):
        src = vec if k == 0 else v_acc.at[k - 1]
        sends.start(None, src, v_pair.at[k], vp_out.at[k], vp_in.at[k], v_devs[k])

    def vec_merge(k):
        wait_arrival(v_pair.at[k], vp_in.at[k], v_devs[k])
        before = vec[...] if k == 0 else v_acc_load(k - 1)
        v_acc.at[k][...] = merge(before, v_pair[k])

    def v_acc_load(k):
        return v_acc[k]

    def vec_cols():
        for step in range(1, cols):
            to = (col + step) % cols
            sends.start(None, v_acc.at[2], v_cols.at[col], vc_out.at[step], vc_in.at[col], {"col": to})
        v_cols[pl.ds(col, 1)] = v_acc[2][None]

    def vec_last():
        for step in range(1, cols):
            at = (col + step) % cols
            wait_arrival(v_cols.at[at], vc_in.at[at], {"col": at})
        total = v_cols[0]
        for k in range(1, cols):
            total = merge(total, v_cols[k])
        vec_out[...] = total

    steps = [lambda: vec_send(0), lambda: (vec_merge(0), vec_send(1)), lambda: (vec_merge(1), vec_send(2)),
             lambda: (vec_merge(2), vec_cols()), vec_last]
    lags = list(zip(RL, (core_stage, y_stage, x_stage, z_stage, final_stage, out_stage)))
    work = [lambda b=b: hidden_gradient(b) for b in range(4)] + [inner_gradient]
    work += [lambda b=b: back_hidden(b) for b in range(4)] + [first_norm_back, output_gradient, context_gradient]
    work += [lambda pair=pair, half=half: attend_back(pair, half) for pair in range(H // 2) for half in range(2)]
    work += [lambda m=m: finish_matrix(m) for m in range(3)] + [fill_vectors]
    first_late = min(e for e in range(number) if entries[e][0] < 3)
    for tick in range(number + lags[-1][0]):
        for lag, stage in lags:
            if 0 <= tick - lag < number:
                if stage is core_stage:
                    while work and (entries[tick][0] not in begun or tick >= first_late):
                        work.pop(0)()
                stage(tick - lag)
                if work:
                    work.pop(0)()
        if 0 <= tick - first_late < len(steps):
            steps[tick - first_late]()
    sends.finish()


def backward_all(outer_term, wholes, found, seg):
    rows, cols = lax.axis_size("row"), lax.axis_size("col")
    q, k, v, stat, token_low, ctx, h1r, low_grad, gp, n1, gain, dz, vec = found
    shapes = [w.shape for w in wholes]
    count = len(shapes)
    heights = [s[0] // rows for s in shapes]
    widths = [s[1] for s in shapes]
    entries = reduce_entries(heights, (5, 4, 3, 0, 1, 2))
    number = len(entries)
    sizes = [(2 * part if paired else part, part, widths[m]) for m, paired, _, part in entries]
    vm, dma, f32 = pltpu.VMEM, pltpu.SemaphoreType.DMA, jnp.float32
    scratch = (
        [vm((rows, band, width), low_type) for band, _, width in sizes]
        + [vm((rows, band, width), low_type) for band, _, width in sizes]
        + [vm((rows, part, width) if entries[e][1] else (rows, 16, 128), low_type) for e, (_, part, width) in enumerate(sizes)]
        + [vm((part, width), low_type) for _, part, width in sizes]
        + [vm((cols, part, width // cols), low_type) for _, part, width in sizes]
        + [vm((part, width // cols), low_type) for _, part, width in sizes]
        + [vm((4, *wholes[0].shape), low_type), vm((4, *q.shape), low_type), vm((3, *q.shape), low_type), vm(q.shape, low_type),
           vm((q.shape[0], 128), f32), vm((q.shape[0], 128), f32), vm((4, 8, q.shape[1]), f32), vm((24, q.shape[1]), f32),
           vm(vec.shape, f32)]
        + [vm((3, *vec.shape), f32), vm((3, *vec.shape), f32), vm((cols, *vec.shape), f32)]
        + [dma((number, rows)), dma((number, rows)), dma((number, rows)), dma((number,)), dma((number, cols)),
           dma((number,)), dma((number, 2)), dma((3,)), dma((cols,)),
           dma((number, rows)), dma((number, rows)), dma((number,)), dma((number, cols, 2)),
           dma((number,)), dma((number, 2)), dma((3,)), dma((cols,)), dma((4,)), dma((4,)), dma((3,)), dma, dma((2,))]
    )
    blocks = [jax.ShapeDtypeStruct((heights[m], widths[m] // cols), low_type) for m in range(count)]
    anywhere, in_vmem = pl.BlockSpec(memory_space=pl.ANY), pl.BlockSpec(memory_space=pltpu.VMEM)
    found = pl.pallas_call(
        functools.partial(backward_kernel, rows, cols, entries),
        out_shape=(*blocks, jax.ShapeDtypeStruct(vec.shape, f32), jax.ShapeDtypeStruct(dz.shape, f32),
                   *(jax.ShapeDtypeStruct(w.shape, low_type) for w in wholes[3:5])),
        in_specs=[anywhere] * 16 + [in_vmem] * 6,
        out_specs=[in_vmem] * 8 + [anywhere] * 2,
        scratch_shapes=scratch,
        compiler_params=pltpu.CompilerParams(collective_id=1, has_side_effects=True, vmem_limit_bytes=65400 * 1024),
        name="backward_all",
    )(outer_term, *wholes, q, k, v, token_low, ctx, h1r, low_grad, gp, dz, stat, n1, gain, seg.reshape(-1, 1), seg.reshape(1, -1), vec)
    return found[:6], found[6], found[7]


def finish_kernel(cols, lengths, spread, *refs):
    refs = list(refs)
    take = lambda n: [refs.pop(0) for _ in range(n)]
    blocks, (vec, weight_query, weight_key, tau_num, tau_den) = take(6), take(5)
    block_outs, vector_outs, (peak_out, clipped_query, clipped_key) = take(6), take(len(lengths)), take(3)
    col = lax.axis_index("col")
    at = lax.axis_index("row") * cols + col
    for block, out in zip(blocks, block_outs):
        step = min(block.shape[0], 65536 // block.shape[1])

        @pl.loop(0, block.shape[0] // step)
        def _(i):
            some = pl.ds(pl.multiple_of(i * step, step), step)
            out[some, :] = block[some, :].astype(jnp.float32)

    start = 0
    for n, whole, out in zip(lengths, spread, vector_outs):
        if n >= 128:
            for j in range(n // 128):
                out[:, j * 128 : j * 128 + 128] = vec[pl.ds(start + at * (n // 128) + j, 1), :]
        else:
            per = 128 // n
            found = vec[pl.ds(start + at // per, 1), :]
            total = found[:, :n]
            for s in range(1, per):
                total = jnp.where(at % per == s, found[:, s * n : s * n + n], total)
            out[...] = total
        start += whole // 128
    peak = vec[start : start + 1, :]
    peak_out[...] = peak[:, :H]
    tau = tau_num[...].astype(jnp.float32) / tau_den[...].astype(jnp.float32)
    factor = jnp.sqrt(tau / jnp.maximum(peak, tau))
    width = weight_query.shape[1]
    head_of = (col * width + lax.broadcasted_iota(jnp.int32, (1, width), 1)) // DH
    by_column = jnp.zeros((1, width), jnp.float32)
    for h in range(H):
        by_column = jnp.where(head_of == h, factor[:, h : h + 1], by_column)
    for source, out in ((weight_query, clipped_query), (weight_key, clipped_key)):
        @pl.loop(0, source.shape[0] // 64)
        def _(i):
            some = pl.ds(pl.multiple_of(i * 64, 64), 64)
            out[some, :] = source[some, :] * by_column


def finish_all(blocks, vec, weight_query, weight_key, tau_num, tau_den, lengths, spread):
    shape, f32 = jax.ShapeDtypeStruct, jnp.float32
    in_vmem = pl.BlockSpec(memory_space=pltpu.VMEM)
    shapes = [b.shape for b in blocks] + [(1, n) for n in lengths] + [(1, H), weight_query.shape, weight_key.shape]
    found = pl.pallas_call(
        functools.partial(finish_kernel, lax.axis_size("col"), lengths, spread),
        out_shape=[shape(s, f32) for s in shapes],
        in_specs=[in_vmem] * 11,
        out_specs=[in_vmem] * len(shapes),
        compiler_params=pltpu.CompilerParams(vmem_limit_bytes=40000 * 1024),
        name="finish",
    )(*blocks, vec, weight_query, weight_key, tau_num.reshape(1, 1), tau_den.reshape(1, 1))
    return found[:6], [v.reshape(-1) for v in found[6:-2]], found[-2:]


def pad_rows(vector):
    short = -vector.shape[0] % 128
    return jnp.pad(vector, (0, short)).reshape(-1, 128)


def on_device(tokens, segment_ids, cotangent, weight_query, weight_key, weight_value, weight_output, weight_inner,
              weight_outer, bias_query, bias_value, bias_output, bias_inner, bias_outer, gain_attn, shift_attn,
              gain_block, shift_block, tau_num, tau_den):
    rows, cols = lax.axis_size("row"), lax.axis_size("col")
    groups = rows * cols
    matrices = (weight_query, weight_key, weight_value, weight_output, weight_inner, weight_outer)
    vectors = (bias_query, bias_value, bias_output, bias_inner, bias_outer, gain_attn, shift_attn, gain_block, shift_block)
    lengths = [v.shape[0] for v in vectors]
    spread = [n * groups for n in lengths]
    flat = jnp.concatenate([pad_rows(v) for v in vectors]).astype(low_type)
    flat = jnp.pad(flat, ((0, -flat.shape[0] % 16), (0, 0)))
    wholes, outer_term, found = forward_all(matrices, flat, lengths, tokens, cotangent, segment_ids)
    q, k, v, stat, token_low, ctx, h1r, low_grad, gp, n1, gain, output, dz, vec_terms = found
    low_blocks, vec_total, grad_tokens = backward_all(
        outer_term, wholes, (q, k, v, stat, token_low, ctx, h1r, low_grad, gp, n1, gain, dz, vec_terms), segment_ids)
    low_blocks, vec_total = sum_groups(low_blocks, vec_total)
    block_grads, owned, clipped = finish_all(
        low_blocks, vec_total, weight_query, weight_key, tau_num, tau_den, lengths, spread)
    return (output, grad_tokens, *block_grads, *owned, *clipped)


def sum_groups(blocks, vec):
    count = lax.axis_size("dp")
    if count <= 4:
        return blocks, vec
    blocks = [b.astype(jnp.float32) for b in blocks]
    totals, vec_sum = list(blocks), vec
    split = vec.shape[0] - 8
    for step in range(4, count, 4):
        shift = [(i, (i + step) % count) for i in range(count)]
        totals = [t + lax.ppermute(b, "dp", shift) for t, b in zip(totals, blocks)]
        moved = lax.ppermute(vec, "dp", shift)
        vec_sum = jnp.concatenate([vec_sum[:split] + moved[:split], jnp.maximum(vec_sum[split:], moved[split:])])
    return totals, vec_sum


def solution(mesh):
    tokens_spec, block_spec, vector_spec = P(("dp", "row", "col"), None), P("row", "col"), P(("row", "col"))
    in_specs = (tokens_spec, P(("dp", "row", "col")), tokens_spec, *(block_spec,) * 6, *(vector_spec,) * 9, P(), P())
    out_specs = (tokens_spec, tokens_spec, *(block_spec,) * 6, *(vector_spec,) * 9, P(), block_spec, block_spec)
    return jax.shard_map(on_device, mesh=mesh, in_specs=in_specs, out_specs=out_specs, check_vma=False)
```

```python
import functools
import jax
import jax.numpy as jnp
from jax import lax
from jax.experimental import pallas as pl
from jax.experimental.pallas import tpu as pltpu
from jax.sharding import PartitionSpec as P

MESH = pl.DeviceIdType.MESH

LAGS = (0, 4, 9)
SEQ, H, DH = 512, 16, 64
norm_eps = 1e-12
neg_fill = -1e30
low_type = jnp.bfloat16

def place():
    dp = lax.axis_index("dp")
    return lax.axis_index("row"), lax.axis_index("col"), dp, dp % 2, (dp // 2) % 2


def core_peer(dp):
    return {"dp": dp + 1 - 2 * (dp % 2)}


def y_peer(dp):
    side = (dp // 2) % 2
    return {"dp": dp + 2 - 4 * side}


class Sends:
    def __init__(self):
        self.items = []

    def start(self, when, src, dst, send_sem, recv_sem, device):
        copy = pltpu.make_async_remote_copy(
            src_ref=src, dst_ref=dst, send_sem=send_sem, recv_sem=recv_sem,
            device_id=device, device_id_type=MESH,
        )
        self.items.append((when, copy))
        if when is None:
            copy.start()
        else:
            pl.when(when)(copy.start)

    def finish(self):
        for when, copy in self.items:
            if when is None:
                copy.wait_send()
            else:
                pl.when(when)(copy.wait_send)


def wait_arrival(dst, recv_sem, device):
    pltpu.make_async_remote_copy(
        src_ref=dst, dst_ref=dst, send_sem=recv_sem, recv_sem=recv_sem,
        device_id=device, device_id_type=MESH,
    ).wait_recv()


def group_barrier(rows, cols):
    row, col, dp, _, _ = place()
    barrier = pltpu.get_barrier_semaphore()
    peers = [core_peer(dp), y_peer(dp)]
    mine = row * cols + col
    for step in range(1, rows * cols):
        other = (mine + step) % (rows * cols)
        peers.append({"row": other // cols, "col": other % cols})
    for peer in peers:
        pl.semaphore_signal(barrier, inc=1, device_id=peer, device_id_type=MESH)
    pl.semaphore_wait(barrier, len(peers))


def entries_of(heights):
    found = []
    for m, height in enumerate(heights):
        found.append((m, True, 0, height * 3 // 16))
        found.append((m, False, height * 3 // 4, height // 8))
    return found


def assemble_vectors(vecs, full_vec, lengths):
    groups = vecs.shape[0]
    for d in range(groups):
        rows_of = vecs[d].astype(jnp.float32)
        at = 0
        for i, n in enumerate(lengths):
            for part in range(-(-n // 128)):
                width = min(128, n - part * 128)
                start = d * n + part * 128
                full_vec[i : i + 1, start : start + width] = rows_of[at : at + 1, :width]
                at += 1


def row_stats(values):
    center = values - jnp.mean(values, axis=-1, keepdims=True)
    spread = jnp.mean(center * center, axis=-1, keepdims=True)
    scale = lax.rsqrt(spread + norm_eps)
    return center * scale, scale


def put_vector(ref, start, total):
    for r in range(total.shape[1] // 128):
        ref[start + r : start + r + 1, :] = total[:, r * 128 : r * 128 + 128]


def fold_rows(values):
    return values.reshape(values.shape[0] // 8, 8, values.shape[1]).sum(axis=0)


def product_term(into, left, rights, staged, stage_sem):
    tiles = left.shape[1] // 256

    def send(slot, r, c):
        rows = pl.ds(pl.multiple_of(r * 256, 256), 256)
        return pltpu.make_async_copy(staged[slot], into.at[rows, c * 1024 : c * 1024 + 1024], stage_sem.at[slot])

    for c, right in enumerate(rights):
        @pl.loop(0, tiles // 2)
        def _(i):
            for slot in range(2):
                r = i * 2 + slot
                if c == 0:
                    pl.when(i > 0)(lambda: send(slot, r, c).wait())
                else:
                    send(slot, r, c).wait()
                staged[slot][...] = lax.dot_general(left[:, pl.ds(pl.multiple_of(r * 256, 256), 256)], right[...],
                                               (((0,), (0,)), ((), ())), preferred_element_type=jnp.float32).astype(low_type)
                send(slot, r, c).start()
    for slot in range(2):
        send(slot, 0, 0).wait()


def spread_segments(seg_row, seg_col):
    for i in range(seg_row.shape[1] // 128):
        seg_col[i * 128 : i * 128 + 128, :] = jnp.broadcast_to(seg_row[:, i * 128 : i * 128 + 128], (128, 128)).T


def pack_vectors(vectors, wide, vec):
    wide[...] = jnp.zeros_like(wide)
    at = 0
    for v in vectors:
        n = v.shape[1]
        for part in range(-(-n // 128)):
            width = min(128, n - part * 128)
            wide[at : at + 1, :width] = v[:, part * 128 : part * 128 + width]
            at += 1
    vec[...] = wide[...].astype(low_type)


def forward_kernel(rows, cols, entries, lengths, ahead, *refs):
    refs = list(refs)
    take = lambda n: [refs.pop(0) for _ in range(n)]
    blocks = take(6)
    vectors, (tokens, cotangent, seg_row) = take(9), take(3)
    wholes_out, outer_term = take(6), take(1)[0]
    (q, k, v, stat, token_low, ctx, h1r, low_grad, gp, n1, gain, output, dz, vec_terms) = take(14)
    wholes = take(6)
    (vecs, full_vec, peak, g, sums, staged, seg_col, wide_vec, vec) = take(9)
    (stage_sem, z_in, x_in, y_in, c_in, v_in, z_out, x_out, y_out, c_out, v_out, out_sem, own_vec) = refs
    count, number = 6, len(entries)
    row, col, dp, core, side = place()
    other = 1 - row
    mine = row * cols + col
    x_dev, y_dev, c_dev = {"row": other}, y_peer(dp), core_peer(dp)
    sends = Sends()

    for m in range(count):
        height, width = blocks[m].shape
        step = 32768 // width
        to_col = pl.ds(pl.multiple_of(col * width, width), width)

        @pl.loop(0, height // step)
        def _(i):
            wholes[m][pl.ds(pl.multiple_of(row * height + i * step, step), step), to_col] = (
                blocks[m][pl.ds(pl.multiple_of(i * step, step), step), :].astype(low_type))

    pack_vectors(vectors, wide_vec, vec)
    group_barrier(rows, cols)
    for step in range(1, rows * cols):
        peer = (mine + step) % (rows * cols)
        sends.start(None, vec, vecs.at[mine], v_out.at[step], v_in.at[mine], {"row": peer // cols, "col": peer % cols})

    def region(e, of_row, of_col, of_core, of_side):
        m, paired, base, part = entries[e]
        height, width = blocks[m].shape
        start = of_row * height + base + ((of_core * 2 + of_side) * part if paired else of_core * part)
        return wholes[m].at[pl.ds(pl.multiple_of(start, 16), part), pl.ds(pl.multiple_of(of_col * width, width), width)]

    def send_own(e):
        piece = region(e, row, col, core, side)
        sends.start(col + 1 < cols, piece, piece, z_out.at[e, 1, 0], z_in.at[e, col], {"col": jnp.minimum(col + 1, cols - 1)})
        sends.start(col >= 1, piece, piece, z_out.at[e, 1, 1], z_in.at[e, col], {"col": jnp.maximum(col - 1, 0)})
        sends.start(None, piece, piece, x_out.at[e, col], x_in.at[e, col], x_dev)

    def share(e, of_row, of_col, when):
        piece = region(e, of_row, of_col, core, side)
        if entries[e][1]:
            sends.start(when, piece, piece, y_out.at[e, of_row, of_col], y_in.at[e, of_row, of_col], y_dev)
        sends.start(when, piece, piece, c_out.at[e, of_row, of_col, 0], c_in.at[e, of_row, of_col, 0], c_dev)

    def columns(step):
        if step == 0:
            return [(None, col)]
        return [(col >= step, jnp.maximum(col - step, 0)), (col + step < cols, jnp.minimum(col + step, cols - 1))]

    def guarded(when, body):
        if when is None:
            body()
        else:
            pl.when(when)(body)

    def z_stage(e, step):
        if step == 0:
            if e + ahead < number:
                send_own(e + ahead)
            return
        onward = ((col + 1 < cols, jnp.minimum(col + 1, cols - 1)), (col >= 1, jnp.maximum(col - 1, 0)))
        for way, (when, at) in enumerate(columns(step)):
            piece = region(e, row, at, core, side)
            guarded(when, lambda: wait_arrival(piece, z_in.at[e, at], {"col": col}))
            if step + 1 < cols:
                sends.start(jnp.logical_and(when, onward[way][0]), piece, piece, z_out.at[e, step + 1, way], z_in.at[e, at],
                            {"col": onward[way][1]})
            sends.start(when, piece, piece, x_out.at[e, at], x_in.at[e, at], x_dev)
            share(e, row, at, when)

    def x_stage(e, step):
        for when, at in columns(step):
            piece = region(e, other, at, core, side)
            guarded(when, lambda: wait_arrival(piece, x_in.at[e, at], x_dev))
            share(e, other, at, when)

    def y_stage(e, step):
        if not entries[e][1]:
            return
        for when, at in columns(step):
            for of_row in (row, other):
                if step == 0 and of_row is row:
                    continue
                piece = region(e, of_row, at, core, 1 - side)
                guarded(when, lambda: wait_arrival(piece, y_in.at[e, of_row, at], y_dev))
                sends.start(when, piece, piece, c_out.at[e, of_row, at, 1], c_in.at[e, of_row, at, 1], c_dev)

    def c_stage(e, step):
        for when, at in columns(step):
            for of_row in (row, other):
                if step == 0 and of_row is row:
                    continue
                piece = region(e, of_row, at, 1 - core, side)
                guarded(when, lambda: wait_arrival(piece, c_in.at[e, of_row, at, 0], c_dev))
                if entries[e][1]:
                    far = region(e, of_row, at, 1 - core, 1 - side)
                    guarded(when, lambda: wait_arrival(far, c_in.at[e, of_row, at, 1], c_dev))

    def keep(m):
        return pltpu.make_async_copy(wholes[m], wholes_out[m], out_sem.at[m])

    def complete(m):
        for e in range(number):
            if entries[e][0] == m:
                for step in range(cols):
                    c_stage(e, step)
        keep(m).start()

    tokens_count = tokens.shape[0]

    def cast_tokens():
        @pl.loop(0, tokens_count // 64)
        def _(i):
            at = pl.ds(pl.multiple_of(i * 64, 64), 64)
            token_low[at, :] = tokens[at, :].astype(low_type)

    def finish_vectors():
        for step in range(1, rows * cols):
            peer = (mine + step) % (rows * cols)
            wait_arrival(vecs.at[peer], v_in.at[peer], {"row": peer // cols, "col": peer % cols})
        keep_vec.wait()
        assemble_vectors(vecs, full_vec, lengths)

    def project(m, into, bias):
        @pl.loop(0, into.shape[1] // 256)
        def _(j):
            at = pl.ds(pl.multiple_of(j * 256, 256), 256)
            total = jnp.dot(token_low[...], wholes[m][:, at], preferred_element_type=jnp.float32)
            if bias is not None:
                total = total + full_vec[bias : bias + 1, at]
            into[:, at] = total.astype(low_type)

    def start_attention():
        stat[...] = jnp.zeros_like(stat)
        spread_segments(seg_row, seg_col)
        peak[...] = jnp.full(peak.shape, neg_fill, jnp.float32)

    def attend(pair, half):
        lanes = slice(pair * 128, pair * 128 + 128)
        lane = lax.broadcasted_iota(jnp.int32, (1, 128), 1)
        place_of = lax.broadcasted_iota(jnp.int32, (128, 128), 1)
        peak_place = lax.broadcasted_iota(jnp.int32, peak.shape, 1)

        @pl.loop(half * 2, half * 2 + 2)
        def _(i):
            at = pl.ds(pl.multiple_of(i * 128, 128), 128)
            same = seg_col[at, 0:1] == seg_row[...]
            parts = []
            for a in range(2):
                head = 2 * pair + a
                keep_lanes = jnp.where((lane < 64) == (a == 0), DH ** (-0.5), 0.0).astype(low_type)
                scores = lax.dot_general(q[at, lanes] * keep_lanes, k[:, lanes], (((1,), (1,)), ((), ())),
                                         preferred_element_type=jnp.float32)
                scores = jnp.where(same, scores, neg_fill)
                top = jnp.max(scores, axis=1, keepdims=True)
                raised = jnp.exp(scores - top)
                total = jnp.sum(raised, axis=1, keepdims=True)
                attend_low = (raised * (1.0 / total)).astype(low_type)
                parts.append(jnp.dot(attend_low, v[:, lanes], preferred_element_type=jnp.float32))
                stat[at, :] = jnp.where(place_of == head, top + jnp.log(total), stat[at, :])
                peak[...] = jnp.where(peak_place == head, jnp.maximum(peak[...], jnp.max(top, axis=0, keepdims=True)), peak[...])
            ctx[at, lanes] = jnp.where(lane < 64, parts[0], parts[1]).astype(low_type)

    def first_norm(i):
        at = slice(i * 256, i * 256 + 256)
        place_of = lax.broadcasted_iota(jnp.int32, (256, 128), 1)

        @pl.loop(0, 4)
        def _(j):
            to = pl.ds(pl.multiple_of(j * 256, 256), 256)
            n1[at, to] = (tokens[at, to] + jnp.dot(ctx[at, :], wholes[3][:, to], preferred_element_type=jnp.float32)
                          + full_vec[2:3, to])

        @pl.loop(0, 8)
        def _(j):
            some = pl.ds(pl.multiple_of(i * 256 + j * 32, 32), 32)
            normal, scale = row_stats(n1[some, :])
            n1[some, :] = normal
            h1r[some, :] = (normal * full_vec[5:6, :1024] + full_vec[6:7, :1024]).astype(low_type)
            stat[some, :] = jnp.where(place_of[:32] == H, scale, stat[some, :])

    def hidden(lo, hi):
        @pl.loop(lo, hi)
        def _(j):
            at = pl.ds(pl.multiple_of(j * 256, 256), 256)
            u = jnp.dot(h1r[...], wholes[4][:, at], preferred_element_type=jnp.float32) + full_vec[3:4, at]
            below = 0.5 + 0.5 * lax.erf(u * 0.7071067811865476)
            g[:, at] = (u * below).astype(low_type)
            gp[:, at] = (below + u * (0.3989422804014327 * jnp.exp(-0.5 * u * u))).astype(low_type)

    def outer_product(step):
        here = slice(step * 1024, step * 1024 + 1024)

        @pl.loop(0, 4)
        def _(j):
            to = pl.ds(pl.multiple_of(j * 256, 256), 256)
            term = jnp.dot(g[:, here], wholes[5][here, to], preferred_element_type=jnp.float32)
            if step == 0:
                output[:, to] = term + (n1[:, to] * full_vec[5:6, to] + full_vec[6:7, to]) + full_vec[4:5, to]
            else:
                output[:, to] += term

    def second_norm():
        sums[...] = jnp.zeros_like(sums)

        @pl.loop(0, tokens_count // 32)
        def _(i):
            at = pl.ds(pl.multiple_of(i * 32, 32), 32)
            normal, scale = row_stats(output[at, :])
            grad = cotangent[at, :]
            scaled = grad * full_vec[7:8, :1024]
            gradient = (scaled - jnp.mean(scaled, axis=-1, keepdims=True)
                        - normal * jnp.mean(scaled * normal, axis=-1, keepdims=True)) * scale
            output[at, :] = normal * full_vec[7:8, :1024] + full_vec[8:9, :1024]
            dz[at, :] = gradient
            low = gradient.astype(low_type)
            low_grad[at, :] = low
            add_sums((low.astype(jnp.float32), grad * normal, grad), (0, 1, 2))

    def add_sums(parts, places):
        for part, r in zip(parts, places):
            sums[r * 8 : r * 8 + 8, :] += part.reshape(part.shape[0] // 8, 8, part.shape[1]).sum(axis=0)

    def collect_sums():
        vec_terms[...] = jnp.zeros_like(vec_terms)
        last_rows = vec_terms.shape[0] - 8
        for r, start in ((0, last_rows - 40), (1, last_rows - 16), (2, last_rows - 8)):
            put_vector(vec_terms, start, jnp.sum(sums[r * 8 : r * 8 + 8, :], axis=0, keepdims=True))
        vec_terms[last_rows:, :] = peak[...]
        gain[...] = jnp.broadcast_to(full_vec[5:6, : gain.shape[1]], gain.shape)

    for e in range(ahead):
        send_own(e)
    keep_vec = pltpu.make_async_copy(vec, vecs.at[mine], own_vec)
    keep_vec.start()
    items = [(e, step) for e in range(number) for step in range(cols)]
    last = len(items) + LAGS[2]

    def ready(m):
        return min((2 * m + 2) * cols + LAGS[2] + 2, last)

    work = [(2, cast_tokens), (4, finish_vectors)]
    for m, into, bias in ((0, q, 0), (1, k, None), (2, v, 1)):
        work.append((ready(m), lambda m=m, into=into, bias=bias: (complete(m), project(m, into, bias))))
    work.append((ready(2), start_attention))
    work += [(ready(2) + 1 + (2 * pair + half) * cols // 4, lambda pair=pair, half=half: attend(pair, half))
             for pair in range(H // 2) for half in range(2)]
    work += [(ready(3), lambda: complete(3)), (ready(3), lambda: first_norm(0)), (ready(3), lambda: first_norm(1))]
    work.append((ready(4), lambda: complete(4)))
    work += [(ready(4) + lo // 2, lambda lo=lo: hidden(lo, lo + 2)) for lo in range(0, 16, 2)]
    work += [(ready(5), lambda: complete(5))] + [(ready(5), lambda s=s: outer_product(s)) for s in range(4)]
    end = ready(5)
    work += [(end, second_norm), (end, lambda: product_term(outer_term, g, [low_grad], [staged.at[0], staged.at[1]], stage_sem)), (end, collect_sums)]

    for tick in range(last + 1):
        for lag, stage in zip(LAGS[:3], (z_stage, x_stage, y_stage)):
            if 0 <= tick - lag < len(items):
                stage(*items[tick - lag])
        while work and (work[0][0] <= tick or tick == last):
            work.pop(0)[1]()
    for m in range(count):
        keep(m).wait()
    sends.finish()


def forward_all(blocks, vectors, lengths, tokens, cotangent, seg, ahead=3):
    rows, cols = lax.axis_size("row"), lax.axis_size("col")
    wholes = [jax.ShapeDtypeStruct((b.shape[0] * rows, b.shape[1] * cols), low_type) for b in blocks]
    entries = entries_of([b.shape[0] for b in blocks])
    number = len(entries)
    dma, vm, count = pltpu.SemaphoreType.DMA, pltpu.VMEM, tokens.shape[0]
    width, hidden = wholes[4].shape
    shape = jax.ShapeDtypeStruct
    f32 = jnp.float32
    results = [*[shape((count, width), low_type)] * 3, shape((count, 128), f32), *[shape((count, width), low_type)] * 4,
               shape((count, hidden), low_type), shape((count, width), f32), shape((8, width), f32),
               *[shape((count, width), f32)] * 2, shape(((width * 8 + hidden) // 128 + 8, 128), f32)]
    in_vmem = pl.BlockSpec(memory_space=pltpu.VMEM)
    found = pl.pallas_call(
        functools.partial(forward_kernel, rows, cols, entries, lengths, ahead),
        out_shape=(*wholes, wholes[5], *results),
        in_specs=[in_vmem] * 18,
        out_specs=[pl.BlockSpec(memory_space=pl.ANY)] * 7 + [in_vmem] * len(results),
        scratch_shapes=[vm(w.shape, low_type) for w in wholes] + [
            vm((rows * cols, 16, 128), low_type), vm((16, hidden), f32), vm((8, 128), f32),
            vm((count, hidden), low_type), vm((24, width), f32), vm((2, 256, 1024), low_type), vm((count, 128), jnp.int32),
            vm((16, 128), f32), vm((16, 128), low_type), dma((2,)),
            dma((number, cols)), dma((number, cols)), dma((number, rows, cols)), dma((number, rows, cols, 2)), dma((rows * cols,)),
            dma((number, cols, 2)), dma((number, cols)), dma((number, rows, cols)), dma((number, rows, cols, 2)), dma((rows * cols,)),
            dma((6,)), dma,
        ],
        compiler_params=pltpu.CompilerParams(collective_id=0, has_side_effects=True, vmem_limit_bytes=65400 * 1024),
        name="forward_all",
    )(*blocks, *(v.reshape(1, -1) for v in vectors), tokens, cotangent, seg.reshape(1, -1))
    return found[:6], found[6], found[7:]


RL = (0, 2, 4, 6, 8, 9)
ALONE = (0, None, 2, 4, 6, 7)
PARTS = (1, 1, 1, 1, 2, 2)

def reduce_entries(heights, order):
    found = []
    for m in order:
        height = heights[m]
        for i in range(PARTS[m]):
            base, size = i * height // PARTS[m], height // PARTS[m]
            found.append((m, False, base + size // 2, size // 4))
            found.append((m, True, base, size // 8))
    return found


def add_into(into, other):
    height, width = into.shape
    rows = max(16, min(height, 65536 // width // 16 * 16))
    while height % rows:
        rows -= 16

    @pl.loop(0, height // rows)
    def _(i):
        at = pl.ds(pl.multiple_of(i * rows, rows), rows)
        into[at, :] = into[at, :] + other[at, :]


def backward_kernel(rows, cols, entries, *refs):
    refs = list(refs)
    take = lambda n: [refs.pop(0) for _ in range(n)]
    number, count = len(entries), 6
    outer_term, whole_in = take(1)[0], take(6)
    q_in, k_in, v_in, token_in, ctx_in, h1r_in, low_in, gp_in, dz_in = take(9)
    stat, n1, gain, seg_row, vec_in = take(5)
    full, (vec_out, grad_tokens), (output_term, inner_term) = take(count), take(2), take(2)
    acc, c_land, y_land, x_land, z_land, f_land = (take(number) for _ in range(6))
    big, quad, grads, dctx, key_sum, value_sum, hidden_sums, sums, vec, v_acc, v_pair, v_cols, seg_col = take(13)
    (load_sem, c_in, y_in, x_in, z_in, f_in, g_in, vp_in, vc_in,
     c_out, y_out, x_out, z_out, f_out, g_out, vp_out, vc_out, big_sem, quad_sem, grad_sem, dz_sem, stage_sem) = refs
    terms = [big.at[0], big.at[1], big.at[2], output_term, inner_term, outer_term]
    q, k, v, token_low = (quad.at[i] for i in range(4))
    grads = [grads.at[i] for i in range(3)]
    whole = big.at[3]
    staged = [dctx.at[:256, :], dctx.at[256:512, :]]
    begun = set()
    row, col, dp, core, side = place()
    group_barrier(rows, cols)
    sends = Sends()
    other = 1 - row
    x_dev, y_dev, c_dev = {"row": other}, y_peer(dp), core_peer(dp)

    def band(e, of_row, of_core):
        m, paired, base, part = entries[e]
        height = terms[m].shape[0] // rows
        size = 2 * part if paired else part
        start = of_row * height + base + of_core * size
        return terms[m].at[pl.ds(pl.multiple_of(start, 16), size), :]

    def load(e):
        return [pltpu.make_async_copy(band(e, r, core), acc[e].at[r], load_sem.at[e, r]) for r in range(rows)]

    def begin(e):
        for r in range(rows):
            sends.start(None, band(e, r, 1 - core), c_land[e].at[r], c_out.at[e, r], c_in.at[e, r], c_dev)
        for copy in load(e):
            copy.start()

    def begin_matrix(m):
        begun.add(m)
        for e in range(number):
            if entries[e][0] == m:
                begin(e)

    begin_matrix(5)
    dz_copy = pltpu.make_async_copy(dz_in, grad_tokens, dz_sem)
    dz_copy.start()

    def fetch(m):
        return pltpu.make_async_copy(whole_in[m], whole, big_sem.at[3])

    def fetch_block(m, b):
        part = whole_in[m].at[b * 1024 : b * 1024 + 1024, :] if m == 5 else whole_in[m].at[:, b * 1024 : b * 1024 + 1024]
        return pltpu.make_async_copy(part, big.at[b], big_sem.at[b])

    def slope_block(b):
        return pltpu.make_async_copy(gp_in.at[:, b * 1024 : b * 1024 + 1024], quad.at[b], quad_sem.at[b])

    def to_grads(i, ref):
        return pltpu.make_async_copy(ref, grads[i], grad_sem.at[i])

    def to_quad(i):
        return pltpu.make_async_copy((q_in, k_in, v_in, token_in)[i], quad.at[i], quad_sem.at[i])

    to_grads(0, low_in).start()
    for b in range(4):
        fetch_block(5, b).start()
        slope_block(b).start()
    to_grads(1, h1r_in).start()
    to_grads(2, ctx_in).start()
    token_count = dctx.shape[0]
    f32 = jnp.float32

    def hidden_gradient(b):
        if b == 0:
            to_grads(0, low_in).wait()
        fetch_block(5, b).wait()
        slope_block(b).wait()

        @pl.loop(0, 4)
        def _(j):
            at = pl.ds(pl.multiple_of(j * 256, 256), 256)
            act = lax.dot_general(grads[0][...], big[b, at, :], (((1,), (1,)), ((), ())), preferred_element_type=f32)
            low = (act * quad[b, :, at].astype(f32)).astype(low_type)
            quad[b, :, at] = low
            hidden_sums[b, :, at] = fold_rows(low.astype(f32))

        fetch_block(4, b).start()

    def inner_gradient():
        to_grads(1, h1r_in).wait()
        product_term(inner_term, grads[1], [quad.at[b] for b in range(4)], staged, stage_sem)
        begin_matrix(4)

    def back_hidden(b):
        if b == 0:
            dz_copy.wait()
        fetch_block(4, b).wait()

        @pl.loop(0, 4)
        def _(j):
            to = pl.ds(pl.multiple_of(j * 256, 256), 256)
            grad_tokens[:, to] += lax.dot_general(quad[b], big[b, to, :], (((1,), (1,)), ((), ())), preferred_element_type=f32)

        to_quad(b).start()
        if b == 3:
            fetch(3).start()

    def first_norm_back():
        sums[...] = jnp.zeros_like(sums)

        @pl.loop(0, token_count // 32)
        def _(i):
            at = pl.ds(pl.multiple_of(i * 32, 32), 32)
            place_of = lax.broadcasted_iota(jnp.int32, (32, 128), 1)
            scale = jnp.sum(jnp.where(place_of == H, stat[at, :], 0.0), axis=1, keepdims=True)
            grad, normal = grad_tokens[at, :], n1[at, :]
            scaled = grad * gain[0:1, :]
            gradient = (scaled - jnp.mean(scaled, axis=-1, keepdims=True)
                        - normal * jnp.mean(scaled * normal, axis=-1, keepdims=True)) * scale
            grad_tokens[at, :] = gradient
            low = gradient.astype(low_type)
            grads[0][at, :] = low
            for r, part in enumerate((low.astype(f32), grad * normal, grad)):
                sums[r * 8 : r * 8 + 8, :] += fold_rows(part)

    def output_gradient():
        to_grads(2, ctx_in).wait()
        product_term(output_term, grads[2], [grads[0]], staged, stage_sem)
        begin_matrix(3)

    def context_gradient():
        fetch(3).wait()

        @pl.loop(0, 4)
        def _(j):
            to = pl.ds(pl.multiple_of(j * 256, 256), 256)
            dctx[:, to] = lax.dot_general(grads[0][...], whole[to, :], (((1,), (1,)), ((), ())),
                                          preferred_element_type=f32).astype(low_type)

        spread_segments(seg_row, seg_col)
        fetch(0).start()
        for i in range(4):
            to_quad(i).wait()

    def attend_back(pair, half):
        lanes = slice(pair * 128, pair * 128 + 128)
        lane = lax.broadcasted_iota(jnp.int32, (1, 128), 1)
        place_of = lax.broadcasted_iota(jnp.int32, (128, 128), 1)
        if half == 0:
            key_sum[...] = jnp.zeros_like(key_sum)
            value_sum[...] = jnp.zeros_like(value_sum)

        @pl.loop(half * 2, half * 2 + 2)
        def _(i):
            at = pl.ds(pl.multiple_of(i * 128, 128), 128)
            same = seg_col[at, 0:1] == seg_row[...]
            parts = []
            for a in range(2):
                mine_only = (lane < 64) == (a == 0)
                query = q[at, lanes] * jnp.where(mine_only, DH ** (-0.5), 0.0).astype(low_type)
                grad = dctx[at, lanes] * jnp.where(mine_only, 1.0, 0.0).astype(low_type)
                total = jnp.sum(jnp.where(place_of == 2 * pair + a, stat[at, :], 0.0), axis=1, keepdims=True)
                scores = lax.dot_general(query, k[:, lanes], (((1,), (1,)), ((), ())), preferred_element_type=f32)
                attend = jnp.exp(jnp.where(same, scores, neg_fill) - total)
                attend_grad = lax.dot_general(grad, v[:, lanes], (((1,), (1,)), ((), ())), preferred_element_type=f32)
                mean = jnp.sum(attend * attend_grad, axis=1, keepdims=True)
                score_low = (attend * (attend_grad - mean)).astype(low_type)
                value_sum[...] += lax.dot_general(attend.astype(low_type), grad, (((0,), (0,)), ((), ())), preferred_element_type=f32)
                key_sum[...] += lax.dot_general(score_low, query, (((0,), (0,)), ((), ())), preferred_element_type=f32)
                parts.append(jnp.dot(score_low, k[:, lanes], preferred_element_type=f32))
            grads[0][at, lanes] = (jnp.where(lane < 64, parts[0], parts[1]) * DH ** (-0.5)).astype(low_type)
        if half == 1:
            grads[1][:, lanes] = key_sum[...].astype(low_type)
            grads[2][:, lanes] = value_sum[...].astype(low_type)

    def finish_matrix(m):
        fetch(m).wait()

        @pl.loop(0, terms[m].shape[0] // 256)
        def _(i):
            at = pl.ds(pl.multiple_of(i * 256, 256), 256)
            terms[m][at, :] = lax.dot_general(token_low[:, at], grads[m][...], (((0,), (0,)), ((), ())),
                                              preferred_element_type=f32).astype(low_type)

        begin_matrix(m)

        @pl.loop(0, 4)
        def _(j):
            to = pl.ds(pl.multiple_of(j * 256, 256), 256)
            grad_tokens[:, to] += lax.dot_general(grads[m][...], whole[to, :], (((1,), (1,)), ((), ())),
                                                  preferred_element_type=f32)

        if m < 2:
            fetch(m + 1).start()

    def fill_vectors():
        vec[...] = vec_in[...]
        for start, m in ((0, 0), (8, 2)):
            total = jnp.zeros((8, grads[m].shape[1]), f32)
            for i in range(token_count // 128):
                total += fold_rows(grads[m][i * 128 : i * 128 + 128, :].astype(f32))
            put_vector(vec, start, jnp.sum(total, axis=0, keepdims=True))
        for b in range(4):
            put_vector(vec, 24 + 8 * b, jnp.sum(hidden_sums[b], axis=0, keepdims=True))
        for r, start in ((0, 16), (1, 64), (2, 72)):
            put_vector(vec, start, jnp.sum(sums[r * 8 : r * 8 + 8, :], axis=0, keepdims=True))

    def mine(e, r, of_side):
        _, paired, _, part = entries[e]
        if paired:
            return acc[e].at[r, pl.ds(pl.multiple_of(of_side * part, 16), part), :]
        return acc[e].at[r]

    def columns(ref, e, at):
        width = terms[entries[e][0]].shape[1] // cols
        return ref.at[:, pl.ds(pl.multiple_of(at * width, width), width)]

    def send_x(e):
        sends.start(None, mine(e, other, side), x_land[e], x_out.at[e], x_in.at[e], x_dev)

    def core_stage(e):
        for copy in load(e):
            copy.wait()
        for r in range(rows):
            wait_arrival(c_land[e].at[r], c_in.at[e, r], c_dev)
        if entries[e][1]:
            for r in range(rows):
                add_into(mine(e, r, 1 - side), y_view(e, r))
                sends.start(None, mine(e, r, 1 - side), y_land[e].at[r], y_out.at[e, r], y_in.at[e, r], y_dev)
            for r in range(rows):
                add_into(mine(e, r, side), y_view(e, r, side))
        else:
            add_into(acc[e].at[other], c_land[e].at[other])
            send_x(e)
            add_into(acc[e].at[row], c_land[e].at[row])

    def y_view(e, r, of_side=None):
        part = entries[e][3]
        at = 1 - side if of_side is None else of_side
        return c_land[e].at[r, pl.ds(pl.multiple_of(at * part, 16), part), :]

    def y_stage(e):
        if not entries[e][1]:
            return
        for r in (other, row):
            wait_arrival(y_land[e].at[r], y_in.at[e, r], y_dev)
            add_into(mine(e, r, side), y_land[e].at[r])
            if r is other:
                send_x(e)

    def x_stage(e):
        wait_arrival(x_land[e], x_in.at[e], x_dev)
        add_into(mine(e, row, side), x_land[e])
        for step in range(1, cols):
            for way, ok, to in ((0, col + step < cols, jnp.minimum(col + step, cols - 1)),
                                (1, col >= step, jnp.maximum(col - step, 0))):
                sends.start(ok, columns(mine(e, row, side), e, to), z_land[e].at[col],
                            z_out.at[e, step, way], z_in.at[e, col], {"col": to})

    def out_rows(e, of_core, of_side):
        m, paired, base, part = entries[e]
        start = base + ((of_core * 2 + of_side) * part if paired else of_core * part)
        return full[m].at[pl.ds(pl.multiple_of(start, 16), part), :]

    def z_stage(e):
        total = columns(mine(e, row, side), e, col)
        for step in range(1, cols):
            for ok, at in ((col + step < cols, jnp.minimum(col + step, cols - 1)),
                           (col >= step, jnp.maximum(col - step, 0))):
                @pl.when(ok)
                def _():
                    wait_arrival(z_land[e].at[at], z_in.at[e, at], {"col": at})
                    add_into(total, z_land[e].at[at])
        if entries[e][1]:
            sends.start(None, total, out_rows(e, core, side), f_out.at[e], f_in.at[e], y_dev)
            sends.start(None, total, out_rows(e, core, side), g_out.at[e, 0], g_in.at[e, 0], c_dev)
            out_rows(e, core, side)[...] = total[...]
        else:
            sends.start(None, total, f_land[e], f_out.at[e], f_in.at[e], y_dev)

    def final_stage(e):
        m = entries[e][0]
        if entries[e][1]:
            piece = out_rows(e, core, 1 - side)
            wait_arrival(piece, f_in.at[e], y_dev)
            sends.start(None, piece, piece, g_out.at[e, 1], g_in.at[e, 1], c_dev)
        else:
            total = columns(mine(e, row, side), e, col)
            wait_arrival(f_land[e], f_in.at[e], y_dev)
            piece = out_rows(e, core, side)
            piece[...] = total[...] + f_land[e][...]
            sends.start(None, piece, piece, g_out.at[e, 0], g_in.at[e, 0], c_dev)

    def out_stage(e):
        m = entries[e][0]
        wait_arrival(out_rows(e, 1 - core, side), g_in.at[e, 0], c_dev)
        if entries[e][1]:
            wait_arrival(out_rows(e, 1 - core, 1 - side), g_in.at[e, 1], c_dev)

    v_rows = v_acc.shape[1]
    merge = lambda a, b: jnp.concatenate([a[: v_rows - 8] + b[: v_rows - 8], jnp.maximum(a[v_rows - 8 :], b[v_rows - 8 :])])
    v_devs = (c_dev, y_dev, x_dev)

    def vec_send(k):
        src = vec if k == 0 else v_acc.at[k - 1]
        sends.start(None, src, v_pair.at[k], vp_out.at[k], vp_in.at[k], v_devs[k])

    def vec_merge(k):
        wait_arrival(v_pair.at[k], vp_in.at[k], v_devs[k])
        before = vec[...] if k == 0 else v_acc_load(k - 1)
        v_acc.at[k][...] = merge(before, v_pair[k])

    def v_acc_load(k):
        return v_acc[k]

    def vec_cols():
        for step in range(1, cols):
            to = (col + step) % cols
            sends.start(None, v_acc.at[2], v_cols.at[col], vc_out.at[step], vc_in.at[col], {"col": to})
        v_cols[pl.ds(col, 1)] = v_acc[2][None]

    def vec_last():
        for step in range(1, cols):
            at = (col + step) % cols
            wait_arrival(v_cols.at[at], vc_in.at[at], {"col": at})
        total = v_cols[0]
        for k in range(1, cols):
            total = merge(total, v_cols[k])
        vec_out[...] = total

    steps = [lambda: vec_send(0), lambda: (vec_merge(0), vec_send(1)), lambda: (vec_merge(1), vec_send(2)),
             lambda: (vec_merge(2), vec_cols()), vec_last]
    stages = (core_stage, y_stage, x_stage, z_stage, final_stage, out_stage)
    work = [lambda b=b: hidden_gradient(b) for b in range(4)] + [inner_gradient]
    work += [lambda b=b: back_hidden(b) for b in range(4)] + [first_norm_back, output_gradient, context_gradient]
    work += [lambda pair=pair, half=half: attend_back(pair, half) for pair in range(H // 2) for half in range(2)]
    work += [lambda m=m: finish_matrix(m) for m in range(3)] + [fill_vectors]
    first_late = min(e for e in range(number) if entries[e][0] < 3)
    calls = [(e + lag, depth, e) for e in range(number)
             for depth, lag in enumerate(RL if entries[e][1] else ALONE) if lag is not None]
    for tick in range(1 + max(calls)[0]):
        for _, depth, e in sorted(call for call in calls if call[0] == tick):
            if depth == 0:
                while work and (entries[e][0] not in begun or e >= first_late):
                    work.pop(0)()
            stages[depth](e)
            if work:
                work.pop(0)()
        if 0 <= tick - first_late < len(steps):
            steps[tick - first_late]()
    sends.finish()


def backward_all(outer_term, wholes, found, seg):
    rows, cols = lax.axis_size("row"), lax.axis_size("col")
    q, k, v, stat, token_low, ctx, h1r, low_grad, gp, n1, gain, dz, vec = found
    shapes = [w.shape for w in wholes]
    count = len(shapes)
    heights = [s[0] // rows for s in shapes]
    widths = [s[1] for s in shapes]
    entries = reduce_entries(heights, (5, 4, 3, 0, 1, 2))
    number = len(entries)
    sizes = [(2 * part if paired else part, part, widths[m]) for m, paired, _, part in entries]
    vm, dma, f32 = pltpu.VMEM, pltpu.SemaphoreType.DMA, jnp.float32
    scratch = (
        [vm((rows, band, width), low_type) for band, _, width in sizes]
        + [vm((rows, band, width), low_type) for band, _, width in sizes]
        + [vm((rows, part, width) if entries[e][1] else (rows, 16, 128), low_type) for e, (_, part, width) in enumerate(sizes)]
        + [vm((part, width), low_type) for _, part, width in sizes]
        + [vm((cols, part, width // cols), low_type) for _, part, width in sizes]
        + [vm((part, width // cols), low_type) for _, part, width in sizes]
        + [vm((4, *wholes[0].shape), low_type), vm((4, *q.shape), low_type), vm((3, *q.shape), low_type), vm(q.shape, low_type),
           vm((q.shape[0], 128), f32), vm((q.shape[0], 128), f32), vm((4, 8, q.shape[1]), f32), vm((24, q.shape[1]), f32),
           vm(vec.shape, f32)]
        + [vm((3, *vec.shape), f32), vm((3, *vec.shape), f32), vm((cols, *vec.shape), f32), vm((q.shape[0], 128), jnp.int32)]
        + [dma((number, rows)), dma((number, rows)), dma((number, rows)), dma((number,)), dma((number, cols)),
           dma((number,)), dma((number, 2)), dma((3,)), dma((cols,)),
           dma((number, rows)), dma((number, rows)), dma((number,)), dma((number, cols, 2)),
           dma((number,)), dma((number, 2)), dma((3,)), dma((cols,)), dma((4,)), dma((4,)), dma((3,)), dma, dma((2,))]
    )
    blocks = [jax.ShapeDtypeStruct((heights[m], widths[m] // cols), low_type) for m in range(count)]
    anywhere, in_vmem = pl.BlockSpec(memory_space=pl.ANY), pl.BlockSpec(memory_space=pltpu.VMEM)
    found = pl.pallas_call(
        functools.partial(backward_kernel, rows, cols, entries),
        out_shape=(*blocks, jax.ShapeDtypeStruct(vec.shape, f32), jax.ShapeDtypeStruct(dz.shape, f32),
                   *(jax.ShapeDtypeStruct(w.shape, low_type) for w in wholes[3:5])),
        in_specs=[anywhere] * 16 + [in_vmem] * 5,
        out_specs=[in_vmem] * 8 + [anywhere] * 2,
        scratch_shapes=scratch,
        compiler_params=pltpu.CompilerParams(collective_id=1, has_side_effects=True, vmem_limit_bytes=65400 * 1024),
        name="backward_all",
    )(outer_term, *wholes, q, k, v, token_low, ctx, h1r, low_grad, gp, dz, stat, n1, gain, seg.reshape(1, -1), vec)
    return found[:6], found[6], found[7]


def finish_kernel(cols, lengths, spread, *refs):
    refs = list(refs)
    take = lambda n: [refs.pop(0) for _ in range(n)]
    far, (tau_num, tau_den) = take(9), take(2)
    block_outs, vector_outs, (peak_out, clipped_query, clipped_key) = take(6), take(len(lengths)), take(3)
    near, sem = take(9), refs[0]
    copies = [pltpu.make_async_copy(a, b, sem.at[i]) for i, (a, b) in enumerate(zip(far, near))]
    for copy in copies:
        copy.start()
    blocks, (vec, weight_query, weight_key) = near[:6], near[6:]
    col = lax.axis_index("col")
    at = lax.axis_index("row") * cols + col
    for copy, block, out in zip(copies, blocks, block_outs):
        copy.wait()
        step = min(block.shape[0], 65536 // block.shape[1])

        @pl.loop(0, block.shape[0] // step)
        def _(i):
            some = pl.ds(pl.multiple_of(i * step, step), step)
            out[some, :] = block[some, :].astype(jnp.float32)

    for copy in copies[6:]:
        copy.wait()
    start = 0
    for n, whole, out in zip(lengths, spread, vector_outs):
        if n >= 128:
            for j in range(n // 128):
                out[:, j * 128 : j * 128 + 128] = vec[pl.ds(start + at * (n // 128) + j, 1), :]
        else:
            per = 128 // n
            found = vec[pl.ds(start + at // per, 1), :]
            total = found[:, :n]
            for s in range(1, per):
                total = jnp.where(at % per == s, found[:, s * n : s * n + n], total)
            out[...] = total
        start += whole // 128
    peak = vec[start : start + 1, :]
    peak_out[...] = peak[:, :H]
    tau = tau_num[...].astype(jnp.float32) / tau_den[...].astype(jnp.float32)
    factor = jnp.sqrt(tau / jnp.maximum(peak, tau))
    width = weight_query.shape[1]
    head_of = (col * width + lax.broadcasted_iota(jnp.int32, (1, width), 1)) // DH
    by_column = jnp.zeros((1, width), jnp.float32)
    for h in range(H):
        by_column = jnp.where(head_of == h, factor[:, h : h + 1], by_column)
    for source, out in ((weight_query, clipped_query), (weight_key, clipped_key)):
        @pl.loop(0, source.shape[0] // 64)
        def _(i):
            some = pl.ds(pl.multiple_of(i * 64, 64), 64)
            out[some, :] = source[some, :] * by_column


def finish_all(blocks, vec, weight_query, weight_key, tau_num, tau_den, lengths, spread):
    shape, f32 = jax.ShapeDtypeStruct, jnp.float32
    in_vmem = pl.BlockSpec(memory_space=pltpu.VMEM)
    shapes = [b.shape for b in blocks] + [(1, n) for n in lengths] + [(1, H), weight_query.shape, weight_key.shape]
    found = pl.pallas_call(
        functools.partial(finish_kernel, lax.axis_size("col"), lengths, spread),
        out_shape=[shape(s, f32) for s in shapes],
        in_specs=[pl.BlockSpec(memory_space=pl.ANY)] * 9 + [in_vmem] * 2,
        out_specs=[in_vmem] * len(shapes),
        scratch_shapes=[pltpu.VMEM(a.shape, a.dtype) for a in (*blocks, vec, weight_query, weight_key)] + [pltpu.SemaphoreType.DMA((9,))],
        compiler_params=pltpu.CompilerParams(vmem_limit_bytes=65400 * 1024),
        name="finish",
    )(*blocks, vec, weight_query, weight_key, tau_num.reshape(1, 1), tau_den.reshape(1, 1))
    return found[:6], [v.reshape(-1) for v in found[6:-2]], found[-2:]


def on_device(tokens, segment_ids, cotangent, weight_query, weight_key, weight_value, weight_output, weight_inner,
              weight_outer, bias_query, bias_value, bias_output, bias_inner, bias_outer, gain_attn, shift_attn,
              gain_block, shift_block, tau_num, tau_den):
    rows, cols = lax.axis_size("row"), lax.axis_size("col")
    groups = rows * cols
    matrices = (weight_query, weight_key, weight_value, weight_output, weight_inner, weight_outer)
    vectors = (bias_query, bias_value, bias_output, bias_inner, bias_outer, gain_attn, shift_attn, gain_block, shift_block)
    lengths = [v.shape[0] for v in vectors]
    spread = [n * groups for n in lengths]
    wholes, outer_term, found = forward_all(matrices, vectors, lengths, tokens, cotangent, segment_ids)
    q, k, v, stat, token_low, ctx, h1r, low_grad, gp, n1, gain, output, dz, vec_terms = found
    low_blocks, vec_total, grad_tokens = backward_all(
        outer_term, wholes, (q, k, v, stat, token_low, ctx, h1r, low_grad, gp, n1, gain, dz, vec_terms), segment_ids)
    low_blocks, vec_total = sum_groups(low_blocks, vec_total)
    block_grads, owned, clipped = finish_all(
        low_blocks, vec_total, weight_query, weight_key, tau_num, tau_den, lengths, spread)
    return (output, grad_tokens, *block_grads, *owned, *clipped)


def sum_groups(blocks, vec):
    count = lax.axis_size("dp")
    if count <= 4:
        return blocks, vec
    blocks = [b.astype(jnp.float32) for b in blocks]
    totals, vec_sum = list(blocks), vec
    split = vec.shape[0] - 8
    for step in range(4, count, 4):
        shift = [(i, (i + step) % count) for i in range(count)]
        totals = [t + lax.ppermute(b, "dp", shift) for t, b in zip(totals, blocks)]
        moved = lax.ppermute(vec, "dp", shift)
        vec_sum = jnp.concatenate([vec_sum[:split] + moved[:split], jnp.maximum(vec_sum[split:], moved[split:])])
    return totals, vec_sum


def solution(mesh):
    tokens_spec, block_spec, vector_spec = P(("dp", "row", "col"), None), P("row", "col"), P(("row", "col"))
    in_specs = (tokens_spec, P(("dp", "row", "col")), tokens_spec, *(block_spec,) * 6, *(vector_spec,) * 9, P(), P())
    out_specs = (tokens_spec, tokens_spec, *(block_spec,) * 6, *(vector_spec,) * 9, P(), block_spec, block_spec)
    return jax.shard_map(on_device, mesh=mesh, in_specs=in_specs, out_specs=out_specs, check_vma=False)
```

```python
import functools
import jax
import jax.numpy as jnp
from jax import lax
from jax.experimental import pallas as pl
from jax.experimental.pallas import tpu as pltpu
from jax.sharding import PartitionSpec as P

MESH = pl.DeviceIdType.MESH

LAGS = (0, 4, 9)
SEQ, H, DH = 512, 16, 64
norm_eps = 1e-12
neg_fill = -1e30
low_type = jnp.bfloat16

def place():
    dp = lax.axis_index("dp")
    return lax.axis_index("row"), lax.axis_index("col"), dp, dp % 2, (dp // 2) % 2


def core_peer(dp):
    return {"dp": dp + 1 - 2 * (dp % 2)}


def y_peer(dp):
    side = (dp // 2) % 2
    return {"dp": dp + 2 - 4 * side}


class Sends:
    def __init__(self):
        self.items = []

    def start(self, when, src, dst, send_sem, recv_sem, device):
        copy = pltpu.make_async_remote_copy(
            src_ref=src, dst_ref=dst, send_sem=send_sem, recv_sem=recv_sem,
            device_id=device, device_id_type=MESH,
        )
        self.items.append((when, copy))
        if when is None:
            copy.start()
        else:
            pl.when(when)(copy.start)

    def finish(self):
        for when, copy in self.items:
            if when is None:
                copy.wait_send()
            else:
                pl.when(when)(copy.wait_send)


def wait_arrival(dst, recv_sem, device):
    pltpu.make_async_remote_copy(
        src_ref=dst, dst_ref=dst, send_sem=recv_sem, recv_sem=recv_sem,
        device_id=device, device_id_type=MESH,
    ).wait_recv()


def group_barrier(rows, cols):
    row, col, dp, _, _ = place()
    barrier = pltpu.get_barrier_semaphore()
    peers = [core_peer(dp), y_peer(dp)]
    mine = row * cols + col
    for step in range(1, rows * cols):
        other = (mine + step) % (rows * cols)
        peers.append({"row": other // cols, "col": other % cols})
    for peer in peers:
        pl.semaphore_signal(barrier, inc=1, device_id=peer, device_id_type=MESH)
    pl.semaphore_wait(barrier, len(peers))


def entries_of(heights):
    found = []
    for m, height in enumerate(heights):
        found.append((m, False, height * 3 // 4, height // 8))
        found.append((m, True, 0, height * 3 // 16))
    return found


def assemble_vectors(vecs, full_vec, lengths):
    groups = vecs.shape[0]
    for d in range(groups):
        rows_of = vecs[d].astype(jnp.float32)
        at = 0
        for i, n in enumerate(lengths):
            for part in range(-(-n // 128)):
                width = min(128, n - part * 128)
                start = d * n + part * 128
                full_vec[i : i + 1, start : start + width] = rows_of[at : at + 1, :width]
                at += 1


def row_stats(values):
    center = values - jnp.mean(values, axis=-1, keepdims=True)
    spread = jnp.mean(center * center, axis=-1, keepdims=True)
    scale = lax.rsqrt(spread + norm_eps)
    return center * scale, scale


def put_vector(ref, start, total):
    for r in range(total.shape[1] // 128):
        ref[start + r : start + r + 1, :] = total[:, r * 128 : r * 128 + 128]


def fold_rows(values):
    return values.reshape(values.shape[0] // 8, 8, values.shape[1]).sum(axis=0)


def product_term(into, left, rights, staged, stage_sem):
    tiles = left.shape[1] // 256

    def send(slot, r, c):
        rows = pl.ds(pl.multiple_of(r * 256, 256), 256)
        return pltpu.make_async_copy(staged[slot], into.at[rows, c * 1024 : c * 1024 + 1024], stage_sem.at[slot])

    for c, right in enumerate(rights):
        @pl.loop(0, tiles // 2)
        def _(i):
            for slot in range(2):
                r = i * 2 + slot
                if c == 0:
                    pl.when(i > 0)(lambda: send(slot, r, c).wait())
                else:
                    send(slot, r, c).wait()
                staged[slot][...] = lax.dot_general(left[:, pl.ds(pl.multiple_of(r * 256, 256), 256)], right[...],
                                               (((0,), (0,)), ((), ())), preferred_element_type=jnp.float32).astype(low_type)
                send(slot, r, c).start()
    for slot in range(2):
        send(slot, 0, 0).wait()


def spread_segments(seg_row, seg_col):
    for i in range(seg_row.shape[1] // 128):
        seg_col[i * 128 : i * 128 + 128, :] = jnp.broadcast_to(seg_row[:, i * 128 : i * 128 + 128], (128, 128)).T


def pack_vectors(vectors, wide, vec):
    wide[...] = jnp.zeros_like(wide)
    at = 0
    for v in vectors:
        n = v.shape[1]
        for part in range(-(-n // 128)):
            width = min(128, n - part * 128)
            wide[at : at + 1, :width] = v[:, part * 128 : part * 128 + width]
            at += 1
    vec[...] = wide[...].astype(low_type)


def forward_kernel(rows, cols, entries, lengths, ahead, *refs):
    refs = list(refs)
    take = lambda n: [refs.pop(0) for _ in range(n)]
    blocks = take(6)
    vectors, (tokens, cotangent, seg_row) = take(9), take(3)
    wholes_out, outer_term = take(6), take(1)[0]
    (q, k, v, stat, token_low, ctx, h1r, low_grad, gp, n1, gain, output, dz, vec_terms) = take(14)
    wholes = take(6)
    (vecs, full_vec, peak, g, sums, staged, seg_col, wide_vec, vec) = take(9)
    (stage_sem, z_in, x_in, y_in, c_in, v_in, z_out, x_out, y_out, c_out, v_out, out_sem, own_vec) = refs
    count, number = 6, len(entries)
    row, col, dp, core, side = place()
    other = 1 - row
    mine = row * cols + col
    x_dev, y_dev, c_dev = {"row": other}, y_peer(dp), core_peer(dp)
    sends = Sends()

    for m in range(count):
        height, width = blocks[m].shape
        step = 32768 // width
        to_col = pl.ds(pl.multiple_of(col * width, width), width)

        @pl.loop(0, height // step)
        def _(i):
            wholes[m][pl.ds(pl.multiple_of(row * height + i * step, step), step), to_col] = (
                blocks[m][pl.ds(pl.multiple_of(i * step, step), step), :].astype(low_type))

    pack_vectors(vectors, wide_vec, vec)
    group_barrier(rows, cols)
    for step in range(1, rows * cols):
        peer = (mine + step) % (rows * cols)
        sends.start(None, vec, vecs.at[mine], v_out.at[step], v_in.at[mine], {"row": peer // cols, "col": peer % cols})

    def region(e, of_row, of_col, of_core, of_side):
        m, paired, base, part = entries[e]
        height, width = blocks[m].shape
        start = of_row * height + base + ((of_core * 2 + of_side) * part if paired else of_core * part)
        return wholes[m].at[pl.ds(pl.multiple_of(start, 16), part), pl.ds(pl.multiple_of(of_col * width, width), width)]

    def send_own(e):
        piece = region(e, row, col, core, side)
        sends.start(col + 1 < cols, piece, piece, z_out.at[e, 1, 0], z_in.at[e, col], {"col": jnp.minimum(col + 1, cols - 1)})
        sends.start(col >= 1, piece, piece, z_out.at[e, 1, 1], z_in.at[e, col], {"col": jnp.maximum(col - 1, 0)})
        sends.start(None, piece, piece, x_out.at[e, col], x_in.at[e, col], x_dev)

    def share(e, of_row, of_col, when):
        piece = region(e, of_row, of_col, core, side)
        if entries[e][1]:
            sends.start(when, piece, piece, y_out.at[e, of_row, of_col], y_in.at[e, of_row, of_col], y_dev)
        sends.start(when, piece, piece, c_out.at[e, of_row, of_col, 0], c_in.at[e, of_row, of_col, 0], c_dev)

    def columns(step):
        if step == 0:
            return [(None, col)]
        return [(col >= step, jnp.maximum(col - step, 0)), (col + step < cols, jnp.minimum(col + step, cols - 1))]

    def guarded(when, body):
        if when is None:
            body()
        else:
            pl.when(when)(body)

    def z_stage(e, step):
        if step == 0:
            if e + ahead < number:
                send_own(e + ahead)
            return
        onward = ((col + 1 < cols, jnp.minimum(col + 1, cols - 1)), (col >= 1, jnp.maximum(col - 1, 0)))
        for way, (when, at) in enumerate(columns(step)):
            piece = region(e, row, at, core, side)
            guarded(when, lambda: wait_arrival(piece, z_in.at[e, at], {"col": col}))
            if step + 1 < cols:
                sends.start(jnp.logical_and(when, onward[way][0]), piece, piece, z_out.at[e, step + 1, way], z_in.at[e, at],
                            {"col": onward[way][1]})
            sends.start(when, piece, piece, x_out.at[e, at], x_in.at[e, at], x_dev)
            share(e, row, at, when)

    def x_stage(e, step):
        for when, at in columns(step):
            piece = region(e, other, at, core, side)
            guarded(when, lambda: wait_arrival(piece, x_in.at[e, at], x_dev))
            share(e, other, at, when)

    def y_stage(e, step):
        if not entries[e][1]:
            return
        for when, at in columns(step):
            for of_row in (row, other):
                if step == 0 and of_row is row:
                    continue
                piece = region(e, of_row, at, core, 1 - side)
                guarded(when, lambda: wait_arrival(piece, y_in.at[e, of_row, at], y_dev))
                sends.start(when, piece, piece, c_out.at[e, of_row, at, 1], c_in.at[e, of_row, at, 1], c_dev)

    def c_stage(e, step):
        for when, at in columns(step):
            for of_row in (row, other):
                if step == 0 and of_row is row:
                    continue
                piece = region(e, of_row, at, 1 - core, side)
                guarded(when, lambda: wait_arrival(piece, c_in.at[e, of_row, at, 0], c_dev))
                if entries[e][1]:
                    far = region(e, of_row, at, 1 - core, 1 - side)
                    guarded(when, lambda: wait_arrival(far, c_in.at[e, of_row, at, 1], c_dev))

    def keep(m):
        return pltpu.make_async_copy(wholes[m], wholes_out[m], out_sem.at[m])

    def complete(m):
        for e in range(number):
            if entries[e][0] == m:
                for step in range(cols):
                    c_stage(e, step)
        keep(m).start()

    tokens_count = tokens.shape[0]

    def cast_tokens():
        @pl.loop(0, tokens_count // 64)
        def _(i):
            at = pl.ds(pl.multiple_of(i * 64, 64), 64)
            token_low[at, :] = tokens[at, :].astype(low_type)

    def finish_vectors():
        for step in range(1, rows * cols):
            peer = (mine + step) % (rows * cols)
            wait_arrival(vecs.at[peer], v_in.at[peer], {"row": peer // cols, "col": peer % cols})
        keep_vec.wait()
        assemble_vectors(vecs, full_vec, lengths)

    def project(m, into, bias):
        @pl.loop(0, into.shape[1] // 256)
        def _(j):
            at = pl.ds(pl.multiple_of(j * 256, 256), 256)
            total = jnp.dot(token_low[...], wholes[m][:, at], preferred_element_type=jnp.float32)
            if bias is not None:
                total = total + full_vec[bias : bias + 1, at]
            into[:, at] = total.astype(low_type)

    def start_attention():
        stat[...] = jnp.zeros_like(stat)
        spread_segments(seg_row, seg_col)
        peak[...] = jnp.full(peak.shape, neg_fill, jnp.float32)

    def attend(pair, half):
        lanes = slice(pair * 128, pair * 128 + 128)
        lane = lax.broadcasted_iota(jnp.int32, (1, 128), 1)
        place_of = lax.broadcasted_iota(jnp.int32, (128, 128), 1)
        peak_place = lax.broadcasted_iota(jnp.int32, peak.shape, 1)

        @pl.loop(half * 2, half * 2 + 2)
        def _(i):
            at = pl.ds(pl.multiple_of(i * 128, 128), 128)
            same = seg_col[at, 0:1] == seg_row[...]
            parts = []
            for a in range(2):
                head = 2 * pair + a
                keep_lanes = jnp.where((lane < 64) == (a == 0), DH ** (-0.5), 0.0).astype(low_type)
                scores = lax.dot_general(q[at, lanes] * keep_lanes, k[:, lanes], (((1,), (1,)), ((), ())),
                                         preferred_element_type=jnp.float32)
                scores = jnp.where(same, scores, neg_fill)
                top = jnp.max(scores, axis=1, keepdims=True)
                raised = jnp.exp(scores - top)
                total = jnp.sum(raised, axis=1, keepdims=True)
                attend_low = (raised * (1.0 / total)).astype(low_type)
                parts.append(jnp.dot(attend_low, v[:, lanes], preferred_element_type=jnp.float32))
                stat[at, :] = jnp.where(place_of == head, top + jnp.log(total), stat[at, :])
                peak[...] = jnp.where(peak_place == head, jnp.maximum(peak[...], jnp.max(top, axis=0, keepdims=True)), peak[...])
            ctx[at, lanes] = jnp.where(lane < 64, parts[0], parts[1]).astype(low_type)

    def first_norm(i):
        at = slice(i * 256, i * 256 + 256)
        place_of = lax.broadcasted_iota(jnp.int32, (256, 128), 1)

        @pl.loop(0, 4)
        def _(j):
            to = pl.ds(pl.multiple_of(j * 256, 256), 256)
            n1[at, to] = (tokens[at, to] + jnp.dot(ctx[at, :], wholes[3][:, to], preferred_element_type=jnp.float32)
                          + full_vec[2:3, to])

        @pl.loop(0, 8)
        def _(j):
            some = pl.ds(pl.multiple_of(i * 256 + j * 32, 32), 32)
            normal, scale = row_stats(n1[some, :])
            n1[some, :] = normal
            h1r[some, :] = (normal * full_vec[5:6, :1024] + full_vec[6:7, :1024]).astype(low_type)
            stat[some, :] = jnp.where(place_of[:32] == H, scale, stat[some, :])

    def hidden(lo, hi):
        @pl.loop(lo, hi)
        def _(j):
            at = pl.ds(pl.multiple_of(j * 256, 256), 256)
            u = jnp.dot(h1r[...], wholes[4][:, at], preferred_element_type=jnp.float32) + full_vec[3:4, at]
            below = 0.5 + 0.5 * lax.erf(u * 0.7071067811865476)
            g[:, at] = (u * below).astype(low_type)
            gp[:, at] = (below + u * (0.3989422804014327 * jnp.exp(-0.5 * u * u))).astype(low_type)

    def outer_product(step):
        here = slice(step * 1024, step * 1024 + 1024)

        @pl.loop(0, 4)
        def _(j):
            to = pl.ds(pl.multiple_of(j * 256, 256), 256)
            term = jnp.dot(g[:, here], wholes[5][here, to], preferred_element_type=jnp.float32)
            if step == 0:
                output[:, to] = term + (n1[:, to] * full_vec[5:6, to] + full_vec[6:7, to]) + full_vec[4:5, to]
            else:
                output[:, to] += term

    def second_norm():
        sums[...] = jnp.zeros_like(sums)

        @pl.loop(0, tokens_count // 32)
        def _(i):
            at = pl.ds(pl.multiple_of(i * 32, 32), 32)
            normal, scale = row_stats(output[at, :])
            grad = cotangent[at, :]
            scaled = grad * full_vec[7:8, :1024]
            gradient = (scaled - jnp.mean(scaled, axis=-1, keepdims=True)
                        - normal * jnp.mean(scaled * normal, axis=-1, keepdims=True)) * scale
            output[at, :] = normal * full_vec[7:8, :1024] + full_vec[8:9, :1024]
            dz[at, :] = gradient
            low = gradient.astype(low_type)
            low_grad[at, :] = low
            add_sums((low.astype(jnp.float32), grad * normal, grad), (0, 1, 2))

    def add_sums(parts, places):
        for part, r in zip(parts, places):
            sums[r * 8 : r * 8 + 8, :] += part.reshape(part.shape[0] // 8, 8, part.shape[1]).sum(axis=0)

    def collect_sums():
        vec_terms[...] = jnp.zeros_like(vec_terms)
        last_rows = vec_terms.shape[0] - 8
        for r, start in ((0, last_rows - 40), (1, last_rows - 16), (2, last_rows - 8)):
            put_vector(vec_terms, start, jnp.sum(sums[r * 8 : r * 8 + 8, :], axis=0, keepdims=True))
        vec_terms[last_rows:, :] = peak[...]
        gain[...] = jnp.broadcast_to(full_vec[5:6, : gain.shape[1]], gain.shape)

    for e in range(ahead):
        send_own(e)
    keep_vec = pltpu.make_async_copy(vec, vecs.at[mine], own_vec)
    keep_vec.start()
    items = [(e, step) for e in range(number) for step in range(cols)]
    last = len(items) + LAGS[2]

    def ready(m):
        return min((2 * m + 2) * cols + LAGS[2] + 2, last)

    work = [(2, cast_tokens), (4, finish_vectors)]
    for m, into, bias in ((0, q, 0), (1, k, None), (2, v, 1)):
        work.append((ready(m), lambda m=m, into=into, bias=bias: (complete(m), project(m, into, bias))))
    work.append((ready(2), start_attention))
    work += [(ready(2) + 1 + (2 * pair + half) * cols // 4, lambda pair=pair, half=half: attend(pair, half))
             for pair in range(H // 2) for half in range(2)]
    work += [(ready(3), lambda: complete(3)), (ready(3), lambda: first_norm(0)), (ready(3), lambda: first_norm(1))]
    work.append((ready(4), lambda: complete(4)))
    work += [(ready(4) + lo // 2, lambda lo=lo: hidden(lo, lo + 2)) for lo in range(0, 16, 2)]
    work += [(ready(5), lambda: complete(5))] + [(ready(5), lambda s=s: outer_product(s)) for s in range(4)]
    end = ready(5)
    work += [(end, second_norm), (end, lambda: product_term(outer_term, g, [low_grad], [staged.at[0], staged.at[1]], stage_sem)), (end, collect_sums)]

    for tick in range(last + 1):
        for lag, stage in zip(LAGS[:3], (z_stage, x_stage, y_stage)):
            if 0 <= tick - lag < len(items):
                stage(*items[tick - lag])
        while work and (work[0][0] <= tick or tick == last):
            work.pop(0)[1]()
    for m in range(count):
        keep(m).wait()
    sends.finish()


def forward_all(blocks, vectors, lengths, tokens, cotangent, seg, ahead=3):
    rows, cols = lax.axis_size("row"), lax.axis_size("col")
    wholes = [jax.ShapeDtypeStruct((b.shape[0] * rows, b.shape[1] * cols), low_type) for b in blocks]
    entries = entries_of([b.shape[0] for b in blocks])
    number = len(entries)
    dma, vm, count = pltpu.SemaphoreType.DMA, pltpu.VMEM, tokens.shape[0]
    width, hidden = wholes[4].shape
    shape = jax.ShapeDtypeStruct
    f32 = jnp.float32
    results = [*[shape((count, width), low_type)] * 3, shape((count, 128), f32), *[shape((count, width), low_type)] * 4,
               shape((count, hidden), low_type), shape((count, width), f32), shape((8, width), f32),
               *[shape((count, width), f32)] * 2, shape(((width * 8 + hidden) // 128 + 8, 128), f32)]
    in_vmem = pl.BlockSpec(memory_space=pltpu.VMEM)
    found = pl.pallas_call(
        functools.partial(forward_kernel, rows, cols, entries, lengths, ahead),
        out_shape=(*wholes, wholes[5], *results),
        in_specs=[in_vmem] * 18,
        out_specs=[pl.BlockSpec(memory_space=pl.ANY)] * 7 + [in_vmem] * len(results),
        scratch_shapes=[vm(w.shape, low_type) for w in wholes] + [
            vm((rows * cols, 16, 128), low_type), vm((16, hidden), f32), vm((8, 128), f32),
            vm((count, hidden), low_type), vm((24, width), f32), vm((2, 256, 1024), low_type), vm((count, 128), jnp.int32),
            vm((16, 128), f32), vm((16, 128), low_type), dma((2,)),
            dma((number, cols)), dma((number, cols)), dma((number, rows, cols)), dma((number, rows, cols, 2)), dma((rows * cols,)),
            dma((number, cols, 2)), dma((number, cols)), dma((number, rows, cols)), dma((number, rows, cols, 2)), dma((rows * cols,)),
            dma((6,)), dma,
        ],
        compiler_params=pltpu.CompilerParams(collective_id=0, has_side_effects=True, vmem_limit_bytes=65400 * 1024),
        name="forward_all",
    )(*blocks, *(v.reshape(1, -1) for v in vectors), tokens, cotangent, seg.reshape(1, -1))
    return found[:6], found[6], found[7:]


RL = (0, 2, 4, 6, 8, 9)
ALONE = (0, None, 2, 4, 6, 7)
PARTS = (1, 1, 1, 1, 2, 2)

def reduce_entries(heights, order):
    found = []
    for m in order:
        height = heights[m]
        for i in range(PARTS[m]):
            base, size = i * height // PARTS[m], height // PARTS[m]
            found.append((m, False, base + size // 2, size // 4))
            found.append((m, True, base, size // 8))
    return found


def add_into(into, other):
    height, width = into.shape
    rows = max(16, min(height, 65536 // width // 16 * 16))
    while height % rows:
        rows -= 16

    @pl.loop(0, height // rows)
    def _(i):
        at = pl.ds(pl.multiple_of(i * rows, rows), rows)
        into[at, :] = into[at, :] + other[at, :]


def backward_kernel(rows, cols, entries, *refs):
    refs = list(refs)
    take = lambda n: [refs.pop(0) for _ in range(n)]
    number, count = len(entries), 6
    outer_term, whole_in = take(1)[0], take(6)
    q_in, k_in, v_in, token_in, ctx_in, h1r_in, low_in, gp_in, dz_in = take(9)
    stat, n1, gain, seg_row, vec_in = take(5)
    full, (vec_out, grad_tokens), (output_term, inner_term) = take(count), take(2), take(2)
    acc, c_land, y_land, x_land, z_land, f_land = (take(number) for _ in range(6))
    big, quad, grads, dctx, key_sum, value_sum, hidden_sums, sums, vec, v_acc, v_pair, v_cols, seg_col = take(13)
    (load_sem, c_in, y_in, x_in, z_in, f_in, g_in, vp_in, vc_in,
     c_out, y_out, x_out, z_out, f_out, g_out, vp_out, vc_out, big_sem, quad_sem, grad_sem, dz_sem, stage_sem) = refs
    terms = [big.at[0], big.at[1], big.at[2], output_term, inner_term, outer_term]
    q, k, v, token_low = (quad.at[i] for i in range(4))
    grads = [grads.at[i] for i in range(3)]
    whole = big.at[3]
    staged = [dctx.at[:256, :], dctx.at[256:512, :]]
    begun = set()
    row, col, dp, core, side = place()
    group_barrier(rows, cols)
    sends = Sends()
    other = 1 - row
    x_dev, y_dev, c_dev = {"row": other}, y_peer(dp), core_peer(dp)

    def band(e, of_row, of_core):
        m, paired, base, part = entries[e]
        height = terms[m].shape[0] // rows
        size = 2 * part if paired else part
        start = of_row * height + base + of_core * size
        return terms[m].at[pl.ds(pl.multiple_of(start, 16), size), :]

    def load(e):
        return [pltpu.make_async_copy(band(e, r, core), acc[e].at[r], load_sem.at[e, r]) for r in range(rows)]

    def begin(e):
        for r in range(rows):
            sends.start(None, band(e, r, 1 - core), c_land[e].at[r], c_out.at[e, r], c_in.at[e, r], c_dev)
        for copy in load(e):
            copy.start()

    def begin_matrix(m):
        begun.add(m)
        for e in range(number):
            if entries[e][0] == m:
                begin(e)

    begin_matrix(5)
    dz_copy = pltpu.make_async_copy(dz_in, grad_tokens, dz_sem)
    dz_copy.start()

    def fetch(m):
        return pltpu.make_async_copy(whole_in[m], whole, big_sem.at[3])

    def fetch_block(m, b):
        part = whole_in[m].at[b * 1024 : b * 1024 + 1024, :] if m == 5 else whole_in[m].at[:, b * 1024 : b * 1024 + 1024]
        return pltpu.make_async_copy(part, big.at[b], big_sem.at[b])

    def slope_block(b):
        return pltpu.make_async_copy(gp_in.at[:, b * 1024 : b * 1024 + 1024], quad.at[b], quad_sem.at[b])

    def to_grads(i, ref):
        return pltpu.make_async_copy(ref, grads[i], grad_sem.at[i])

    def to_quad(i):
        return pltpu.make_async_copy((q_in, k_in, v_in, token_in)[i], quad.at[i], quad_sem.at[i])

    to_grads(0, low_in).start()
    for b in range(4):
        fetch_block(5, b).start()
        slope_block(b).start()
    to_grads(1, h1r_in).start()
    to_grads(2, ctx_in).start()
    token_count = dctx.shape[0]
    f32 = jnp.float32

    def hidden_gradient(b):
        if b == 0:
            to_grads(0, low_in).wait()
        fetch_block(5, b).wait()
        slope_block(b).wait()

        @pl.loop(0, 4)
        def _(j):
            at = pl.ds(pl.multiple_of(j * 256, 256), 256)
            act = lax.dot_general(grads[0][...], big[b, at, :], (((1,), (1,)), ((), ())), preferred_element_type=f32)
            low = (act * quad[b, :, at].astype(f32)).astype(low_type)
            quad[b, :, at] = low
            hidden_sums[b, :, at] = fold_rows(low.astype(f32))

        fetch_block(4, b).start()

    def inner_gradient():
        to_grads(1, h1r_in).wait()
        product_term(inner_term, grads[1], [quad.at[b] for b in range(4)], staged, stage_sem)
        begin_matrix(4)

    def back_hidden(b):
        if b == 0:
            dz_copy.wait()
        fetch_block(4, b).wait()

        @pl.loop(0, 4)
        def _(j):
            to = pl.ds(pl.multiple_of(j * 256, 256), 256)
            grad_tokens[:, to] += lax.dot_general(quad[b], big[b, to, :], (((1,), (1,)), ((), ())), preferred_element_type=f32)

        to_quad(b).start()
        if b == 3:
            fetch(3).start()

    def first_norm_back():
        sums[...] = jnp.zeros_like(sums)

        @pl.loop(0, token_count // 32)
        def _(i):
            at = pl.ds(pl.multiple_of(i * 32, 32), 32)
            place_of = lax.broadcasted_iota(jnp.int32, (32, 128), 1)
            scale = jnp.sum(jnp.where(place_of == H, stat[at, :], 0.0), axis=1, keepdims=True)
            grad, normal = grad_tokens[at, :], n1[at, :]
            scaled = grad * gain[0:1, :]
            gradient = (scaled - jnp.mean(scaled, axis=-1, keepdims=True)
                        - normal * jnp.mean(scaled * normal, axis=-1, keepdims=True)) * scale
            grad_tokens[at, :] = gradient
            low = gradient.astype(low_type)
            grads[0][at, :] = low
            for r, part in enumerate((low.astype(f32), grad * normal, grad)):
                sums[r * 8 : r * 8 + 8, :] += fold_rows(part)

    def output_gradient():
        to_grads(2, ctx_in).wait()
        product_term(output_term, grads[2], [grads[0]], staged, stage_sem)
        begin_matrix(3)

    def context_gradient():
        fetch(3).wait()

        @pl.loop(0, 4)
        def _(j):
            to = pl.ds(pl.multiple_of(j * 256, 256), 256)
            dctx[:, to] = lax.dot_general(grads[0][...], whole[to, :], (((1,), (1,)), ((), ())),
                                          preferred_element_type=f32).astype(low_type)

        spread_segments(seg_row, seg_col)
        fetch(0).start()
        for i in range(4):
            to_quad(i).wait()

    def attend_back(pair, half):
        lanes = slice(pair * 128, pair * 128 + 128)
        lane = lax.broadcasted_iota(jnp.int32, (1, 128), 1)
        place_of = lax.broadcasted_iota(jnp.int32, (128, 128), 1)
        if half == 0:
            key_sum[...] = jnp.zeros_like(key_sum)
            value_sum[...] = jnp.zeros_like(value_sum)

        @pl.loop(half * 2, half * 2 + 2)
        def _(i):
            at = pl.ds(pl.multiple_of(i * 128, 128), 128)
            same = seg_col[at, 0:1] == seg_row[...]
            parts = []
            for a in range(2):
                mine_only = (lane < 64) == (a == 0)
                query = q[at, lanes] * jnp.where(mine_only, DH ** (-0.5), 0.0).astype(low_type)
                grad = dctx[at, lanes] * jnp.where(mine_only, 1.0, 0.0).astype(low_type)
                total = jnp.sum(jnp.where(place_of == 2 * pair + a, stat[at, :], 0.0), axis=1, keepdims=True)
                scores = lax.dot_general(query, k[:, lanes], (((1,), (1,)), ((), ())), preferred_element_type=f32)
                attend = jnp.exp(jnp.where(same, scores, neg_fill) - total)
                attend_grad = lax.dot_general(grad, v[:, lanes], (((1,), (1,)), ((), ())), preferred_element_type=f32)
                mean = jnp.sum(attend * attend_grad, axis=1, keepdims=True)
                score_low = (attend * (attend_grad - mean)).astype(low_type)
                value_sum[...] += lax.dot_general(attend.astype(low_type), grad, (((0,), (0,)), ((), ())), preferred_element_type=f32)
                key_sum[...] += lax.dot_general(score_low, query, (((0,), (0,)), ((), ())), preferred_element_type=f32)
                parts.append(jnp.dot(score_low, k[:, lanes], preferred_element_type=f32))
            grads[0][at, lanes] = (jnp.where(lane < 64, parts[0], parts[1]) * DH ** (-0.5)).astype(low_type)
        if half == 1:
            grads[1][:, lanes] = key_sum[...].astype(low_type)
            grads[2][:, lanes] = value_sum[...].astype(low_type)

    def finish_matrix(m):
        fetch(m).wait()

        @pl.loop(0, terms[m].shape[0] // 256)
        def _(i):
            at = pl.ds(pl.multiple_of(i * 256, 256), 256)
            terms[m][at, :] = lax.dot_general(token_low[:, at], grads[m][...], (((0,), (0,)), ((), ())),
                                              preferred_element_type=f32).astype(low_type)

        begin_matrix(m)

        @pl.loop(0, 4)
        def _(j):
            to = pl.ds(pl.multiple_of(j * 256, 256), 256)
            grad_tokens[:, to] += lax.dot_general(grads[m][...], whole[to, :], (((1,), (1,)), ((), ())),
                                                  preferred_element_type=f32)

        if m < 2:
            fetch(m + 1).start()

    def fill_vectors():
        vec[...] = vec_in[...]
        for start, m in ((0, 0), (8, 2)):
            total = jnp.zeros((8, grads[m].shape[1]), f32)
            for i in range(token_count // 128):
                total += fold_rows(grads[m][i * 128 : i * 128 + 128, :].astype(f32))
            put_vector(vec, start, jnp.sum(total, axis=0, keepdims=True))
        for b in range(4):
            put_vector(vec, 24 + 8 * b, jnp.sum(hidden_sums[b], axis=0, keepdims=True))
        for r, start in ((0, 16), (1, 64), (2, 72)):
            put_vector(vec, start, jnp.sum(sums[r * 8 : r * 8 + 8, :], axis=0, keepdims=True))

    def mine(e, r, of_side):
        _, paired, _, part = entries[e]
        if paired:
            return acc[e].at[r, pl.ds(pl.multiple_of(of_side * part, 16), part), :]
        return acc[e].at[r]

    def columns(ref, e, at):
        width = terms[entries[e][0]].shape[1] // cols
        return ref.at[:, pl.ds(pl.multiple_of(at * width, width), width)]

    def send_x(e):
        sends.start(None, mine(e, other, side), x_land[e], x_out.at[e], x_in.at[e], x_dev)

    def core_stage(e):
        for copy in load(e):
            copy.wait()
        for r in range(rows):
            wait_arrival(c_land[e].at[r], c_in.at[e, r], c_dev)
        if entries[e][1]:
            for r in range(rows):
                add_into(mine(e, r, 1 - side), y_view(e, r))
                sends.start(None, mine(e, r, 1 - side), y_land[e].at[r], y_out.at[e, r], y_in.at[e, r], y_dev)
            for r in range(rows):
                add_into(mine(e, r, side), y_view(e, r, side))
        else:
            add_into(acc[e].at[other], c_land[e].at[other])
            send_x(e)
            add_into(acc[e].at[row], c_land[e].at[row])

    def y_view(e, r, of_side=None):
        part = entries[e][3]
        at = 1 - side if of_side is None else of_side
        return c_land[e].at[r, pl.ds(pl.multiple_of(at * part, 16), part), :]

    def y_stage(e):
        if not entries[e][1]:
            return
        for r in (other, row):
            wait_arrival(y_land[e].at[r], y_in.at[e, r], y_dev)
            add_into(mine(e, r, side), y_land[e].at[r])
            if r is other:
                send_x(e)

    def x_stage(e):
        wait_arrival(x_land[e], x_in.at[e], x_dev)
        add_into(mine(e, row, side), x_land[e])
        for step in range(1, cols):
            for way, ok, to in ((0, col + step < cols, jnp.minimum(col + step, cols - 1)),
                                (1, col >= step, jnp.maximum(col - step, 0))):
                sends.start(ok, columns(mine(e, row, side), e, to), z_land[e].at[col],
                            z_out.at[e, step, way], z_in.at[e, col], {"col": to})

    def out_rows(e, of_core, of_side):
        m, paired, base, part = entries[e]
        start = base + ((of_core * 2 + of_side) * part if paired else of_core * part)
        return full[m].at[pl.ds(pl.multiple_of(start, 16), part), :]

    def z_stage(e):
        total = columns(mine(e, row, side), e, col)
        for step in range(1, cols):
            for ok, at in ((col + step < cols, jnp.minimum(col + step, cols - 1)),
                           (col >= step, jnp.maximum(col - step, 0))):
                @pl.when(ok)
                def _():
                    wait_arrival(z_land[e].at[at], z_in.at[e, at], {"col": at})
                    add_into(total, z_land[e].at[at])
        if entries[e][1]:
            sends.start(None, total, out_rows(e, core, side), f_out.at[e], f_in.at[e], y_dev)
            sends.start(None, total, out_rows(e, core, side), g_out.at[e, 0], g_in.at[e, 0], c_dev)
            out_rows(e, core, side)[...] = total[...]
        else:
            sends.start(None, total, f_land[e], f_out.at[e], f_in.at[e], y_dev)

    def final_stage(e):
        m = entries[e][0]
        if entries[e][1]:
            piece = out_rows(e, core, 1 - side)
            wait_arrival(piece, f_in.at[e], y_dev)
            sends.start(None, piece, piece, g_out.at[e, 1], g_in.at[e, 1], c_dev)
        else:
            total = columns(mine(e, row, side), e, col)
            wait_arrival(f_land[e], f_in.at[e], y_dev)
            piece = out_rows(e, core, side)
            piece[...] = total[...] + f_land[e][...]
            sends.start(None, piece, piece, g_out.at[e, 0], g_in.at[e, 0], c_dev)

    def out_stage(e):
        m = entries[e][0]
        wait_arrival(out_rows(e, 1 - core, side), g_in.at[e, 0], c_dev)
        if entries[e][1]:
            wait_arrival(out_rows(e, 1 - core, 1 - side), g_in.at[e, 1], c_dev)

    v_rows = v_acc.shape[1]
    merge = lambda a, b: jnp.concatenate([a[: v_rows - 8] + b[: v_rows - 8], jnp.maximum(a[v_rows - 8 :], b[v_rows - 8 :])])
    v_devs = (c_dev, y_dev, x_dev)

    def vec_send(k):
        src = vec if k == 0 else v_acc.at[k - 1]
        sends.start(None, src, v_pair.at[k], vp_out.at[k], vp_in.at[k], v_devs[k])

    def vec_merge(k):
        wait_arrival(v_pair.at[k], vp_in.at[k], v_devs[k])
        before = vec[...] if k == 0 else v_acc_load(k - 1)
        v_acc.at[k][...] = merge(before, v_pair[k])

    def v_acc_load(k):
        return v_acc[k]

    def vec_cols():
        for step in range(1, cols):
            to = (col + step) % cols
            sends.start(None, v_acc.at[2], v_cols.at[col], vc_out.at[step], vc_in.at[col], {"col": to})
        v_cols[pl.ds(col, 1)] = v_acc[2][None]

    def vec_last():
        for step in range(1, cols):
            at = (col + step) % cols
            wait_arrival(v_cols.at[at], vc_in.at[at], {"col": at})
        total = v_cols[0]
        for k in range(1, cols):
            total = merge(total, v_cols[k])
        vec_out[...] = total

    steps = [lambda: vec_send(0), lambda: (vec_merge(0), vec_send(1)), lambda: (vec_merge(1), vec_send(2)),
             lambda: (vec_merge(2), vec_cols()), vec_last]
    stages = (core_stage, y_stage, x_stage, z_stage, final_stage, out_stage)
    work = [lambda b=b: hidden_gradient(b) for b in range(4)] + [inner_gradient]
    work += [lambda b=b: back_hidden(b) for b in range(4)] + [first_norm_back, output_gradient, context_gradient]
    work += [lambda pair=pair, half=half: attend_back(pair, half) for pair in range(H // 2) for half in range(2)]
    work += [lambda m=m: finish_matrix(m) for m in range(3)] + [fill_vectors]
    first_late = min(e for e in range(number) if entries[e][0] < 3)
    calls = [(e + lag, depth, e) for e in range(number)
             for depth, lag in enumerate(RL if entries[e][1] else ALONE) if lag is not None]
    for tick in range(1 + max(calls)[0]):
        for _, depth, e in sorted(call for call in calls if call[0] == tick):
            if depth == 0:
                while work and (entries[e][0] not in begun or e >= first_late):
                    work.pop(0)()
            stages[depth](e)
            if work:
                work.pop(0)()
        if 0 <= tick - first_late < len(steps):
            steps[tick - first_late]()
    sends.finish()


def backward_all(outer_term, wholes, found, seg):
    rows, cols = lax.axis_size("row"), lax.axis_size("col")
    q, k, v, stat, token_low, ctx, h1r, low_grad, gp, n1, gain, dz, vec = found
    shapes = [w.shape for w in wholes]
    count = len(shapes)
    heights = [s[0] // rows for s in shapes]
    widths = [s[1] for s in shapes]
    entries = reduce_entries(heights, (5, 4, 3, 0, 1, 2))
    number = len(entries)
    sizes = [(2 * part if paired else part, part, widths[m]) for m, paired, _, part in entries]
    vm, dma, f32 = pltpu.VMEM, pltpu.SemaphoreType.DMA, jnp.float32
    scratch = (
        [vm((rows, band, width), low_type) for band, _, width in sizes]
        + [vm((rows, band, width), low_type) for band, _, width in sizes]
        + [vm((rows, part, width) if entries[e][1] else (rows, 16, 128), low_type) for e, (_, part, width) in enumerate(sizes)]
        + [vm((part, width), low_type) for _, part, width in sizes]
        + [vm((cols, part, width // cols), low_type) for _, part, width in sizes]
        + [vm((part, width // cols), low_type) for _, part, width in sizes]
        + [vm((4, *wholes[0].shape), low_type), vm((4, *q.shape), low_type), vm((3, *q.shape), low_type), vm(q.shape, low_type),
           vm((q.shape[0], 128), f32), vm((q.shape[0], 128), f32), vm((4, 8, q.shape[1]), f32), vm((24, q.shape[1]), f32),
           vm(vec.shape, f32)]
        + [vm((3, *vec.shape), f32), vm((3, *vec.shape), f32), vm((cols, *vec.shape), f32), vm((q.shape[0], 128), jnp.int32)]
        + [dma((number, rows)), dma((number, rows)), dma((number, rows)), dma((number,)), dma((number, cols)),
           dma((number,)), dma((number, 2)), dma((3,)), dma((cols,)),
           dma((number, rows)), dma((number, rows)), dma((number,)), dma((number, cols, 2)),
           dma((number,)), dma((number, 2)), dma((3,)), dma((cols,)), dma((4,)), dma((4,)), dma((3,)), dma, dma((2,))]
    )
    blocks = [jax.ShapeDtypeStruct((heights[m], widths[m] // cols), low_type) for m in range(count)]
    anywhere, in_vmem = pl.BlockSpec(memory_space=pl.ANY), pl.BlockSpec(memory_space=pltpu.VMEM)
    found = pl.pallas_call(
        functools.partial(backward_kernel, rows, cols, entries),
        out_shape=(*blocks, jax.ShapeDtypeStruct(vec.shape, f32), jax.ShapeDtypeStruct(dz.shape, f32),
                   *(jax.ShapeDtypeStruct(w.shape, low_type) for w in wholes[3:5])),
        in_specs=[anywhere] * 16 + [in_vmem] * 5,
        out_specs=[in_vmem] * 8 + [anywhere] * 2,
        scratch_shapes=scratch,
        compiler_params=pltpu.CompilerParams(collective_id=1, has_side_effects=True, vmem_limit_bytes=65400 * 1024),
        name="backward_all",
    )(outer_term, *wholes, q, k, v, token_low, ctx, h1r, low_grad, gp, dz, stat, n1, gain, seg.reshape(1, -1), vec)
    return found[:6], found[6], found[7]


def finish_kernel(cols, lengths, spread, *refs):
    refs = list(refs)
    take = lambda n: [refs.pop(0) for _ in range(n)]
    far, (tau_num, tau_den) = take(9), take(2)
    block_outs, vector_outs, (peak_out, clipped_query, clipped_key) = take(6), take(len(lengths)), take(3)
    near, sem = take(9), refs[0]
    copies = [pltpu.make_async_copy(a, b, sem.at[i]) for i, (a, b) in enumerate(zip(far, near))]
    for copy in copies:
        copy.start()
    blocks, (vec, weight_query, weight_key) = near[:6], near[6:]
    col = lax.axis_index("col")
    at = lax.axis_index("row") * cols + col
    for copy, block, out in zip(copies, blocks, block_outs):
        copy.wait()
        step = min(block.shape[0], 65536 // block.shape[1])

        @pl.loop(0, block.shape[0] // step)
        def _(i):
            some = pl.ds(pl.multiple_of(i * step, step), step)
            out[some, :] = block[some, :].astype(jnp.float32)

    for copy in copies[6:]:
        copy.wait()
    start = 0
    for n, whole, out in zip(lengths, spread, vector_outs):
        if n >= 128:
            for j in range(n // 128):
                out[:, j * 128 : j * 128 + 128] = vec[pl.ds(start + at * (n // 128) + j, 1), :]
        else:
            per = 128 // n
            found = vec[pl.ds(start + at // per, 1), :]
            total = found[:, :n]
            for s in range(1, per):
                total = jnp.where(at % per == s, found[:, s * n : s * n + n], total)
            out[...] = total
        start += whole // 128
    peak = vec[start : start + 1, :]
    peak_out[...] = peak[:, :H]
    tau = tau_num[...].astype(jnp.float32) / tau_den[...].astype(jnp.float32)
    factor = jnp.sqrt(tau / jnp.maximum(peak, tau))
    width = weight_query.shape[1]
    head_of = (col * width + lax.broadcasted_iota(jnp.int32, (1, width), 1)) // DH
    by_column = jnp.zeros((1, width), jnp.float32)
    for h in range(H):
        by_column = jnp.where(head_of == h, factor[:, h : h + 1], by_column)
    for source, out in ((weight_query, clipped_query), (weight_key, clipped_key)):
        @pl.loop(0, source.shape[0] // 64)
        def _(i):
            some = pl.ds(pl.multiple_of(i * 64, 64), 64)
            out[some, :] = source[some, :] * by_column


def finish_all(blocks, vec, weight_query, weight_key, tau_num, tau_den, lengths, spread):
    shape, f32 = jax.ShapeDtypeStruct, jnp.float32
    in_vmem = pl.BlockSpec(memory_space=pltpu.VMEM)
    shapes = [b.shape for b in blocks] + [(1, n) for n in lengths] + [(1, H), weight_query.shape, weight_key.shape]
    found = pl.pallas_call(
        functools.partial(finish_kernel, lax.axis_size("col"), lengths, spread),
        out_shape=[shape(s, f32) for s in shapes],
        in_specs=[pl.BlockSpec(memory_space=pl.ANY)] * 9 + [in_vmem] * 2,
        out_specs=[in_vmem] * len(shapes),
        scratch_shapes=[pltpu.VMEM(a.shape, a.dtype) for a in (*blocks, vec, weight_query, weight_key)] + [pltpu.SemaphoreType.DMA((9,))],
        compiler_params=pltpu.CompilerParams(vmem_limit_bytes=65400 * 1024),
        name="finish",
    )(*blocks, vec, weight_query, weight_key, tau_num.reshape(1, 1), tau_den.reshape(1, 1))
    return found[:6], [v.reshape(-1) for v in found[6:-2]], found[-2:]


def on_device(tokens, segment_ids, cotangent, weight_query, weight_key, weight_value, weight_output, weight_inner,
              weight_outer, bias_query, bias_value, bias_output, bias_inner, bias_outer, gain_attn, shift_attn,
              gain_block, shift_block, tau_num, tau_den):
    rows, cols = lax.axis_size("row"), lax.axis_size("col")
    groups = rows * cols
    matrices = (weight_query, weight_key, weight_value, weight_output, weight_inner, weight_outer)
    vectors = (bias_query, bias_value, bias_output, bias_inner, bias_outer, gain_attn, shift_attn, gain_block, shift_block)
    lengths = [v.shape[0] for v in vectors]
    spread = [n * groups for n in lengths]
    wholes, outer_term, found = forward_all(matrices, vectors, lengths, tokens, cotangent, segment_ids)
    q, k, v, stat, token_low, ctx, h1r, low_grad, gp, n1, gain, output, dz, vec_terms = found
    low_blocks, vec_total, grad_tokens = backward_all(
        outer_term, wholes, (q, k, v, stat, token_low, ctx, h1r, low_grad, gp, n1, gain, dz, vec_terms), segment_ids)
    low_blocks, vec_total = sum_groups(low_blocks, vec_total)
    block_grads, owned, clipped = finish_all(
        low_blocks, vec_total, weight_query, weight_key, tau_num, tau_den, lengths, spread)
    return (output, grad_tokens, *block_grads, *owned, *clipped)


def sum_groups(blocks, vec):
    count = lax.axis_size("dp")
    if count <= 4:
        return blocks, vec
    blocks = [b.astype(jnp.float32) for b in blocks]
    totals, vec_sum = list(blocks), vec
    split = vec.shape[0] - 8
    for step in range(4, count, 4):
        shift = [(i, (i + step) % count) for i in range(count)]
        totals = [t + lax.ppermute(b, "dp", shift) for t, b in zip(totals, blocks)]
        moved = lax.ppermute(vec, "dp", shift)
        vec_sum = jnp.concatenate([vec_sum[:split] + moved[:split], jnp.maximum(vec_sum[split:], moved[split:])])
    return totals, vec_sum


def solution(mesh):
    tokens_spec, block_spec, vector_spec = P(("dp", "row", "col"), None), P("row", "col"), P(("row", "col"))
    in_specs = (tokens_spec, P(("dp", "row", "col")), tokens_spec, *(block_spec,) * 6, *(vector_spec,) * 9, P(), P())
    out_specs = (tokens_spec, tokens_spec, *(block_spec,) * 6, *(vector_spec,) * 9, P(), block_spec, block_spec)
    return jax.shard_map(on_device, mesh=mesh, in_specs=in_specs, out_specs=out_specs, check_vma=False)
```
